512 devices in a mesh: date: 16 (over x, y), col: 32 (over z, core).
Axes of the slice: x: 4, y: 4, z: 16, core: 2. Of those that a mesh axis runs over, the one named last changes fastest.
Arguments:
- slc_stack: bfloat16 [2, 192, 40, 20480], P(None, 'date', None, 'col'), may hold values from -60 to 60
- offsets: int32 [192, 2], replicated, may hold values from -4 to 4
- kernels: float32 [192, 2, 8], replicated, may hold values from -2.5 to 2.5
- partner: int32 [576], P('date'), may hold values from 1 to 191, as said below
- inverse: bfloat16 [191, 576], replicated, may hold values from -3.5 to 3.5
- rate_weights: float32 [191], replicated, may hold values from -0.4375 to 0.4375
- owners: int32 [32, 256, 1], P('col', 'date'), may hold values from 0 to 31; in each aligned block of 16 rows (0 to 15, 16 to 31, ..., all dimensions but the last counted through in order) at most 2 rows name the same one
- map_cell: int32 [32, 256], P('col', 'date'), may hold values from 0 to 127
Outputs:
- geocoded: float32 [32, 128, 192], P('col', 'date')
The draws below stay inside these ranges and needn't reach their ends.
Inputs may be any that keep to these rules, and one draw needn't show every extreme that they name: partner[k] differs from k // 3 by 1 to 6 dates; it is the later date where that lies in the stack, else the earlier one; the 3 partners of one date are distinct, and one of them is 1 date away. `owners`: within the rows of one device, no tile is named more than 2 times.
All inputs are finite; a program needn't handle non-finite values.
Results may differ from the reference program's by a relative error of at most 0.0075.
Values may be sent and summed in bfloat16 or wider, within the bound.
No kernel may reach another device: no remote copies, remote signals or barrier semaphores. Data moves between devices by JAX's collectives and lax.ppermute only.
A program may use at most 64 MiB of HBM per device.

```python
import math
import jax
import jax.numpy as jnp
import numpy as np
from jax import lax

PER_DATE = 3
SPAN = 6
ROWS = 40
ROW_BLOCK = 20
TAPS = 8
MAXOFF = 4
LOOK_AZ = 5
LOOK_RG = 20
DATES = 192
SERIES = 191
IFGS = 576
HALO = 8
NRB = 2
COLS = 20480
LROWS = 8
LC_DEV = 32
STRIPS = 32
PIX_STRIP = 256
PIX_DEV = 16
NPIX = 8192
MOST = 2
TILE_CELLS = 128


def draw_slc_stack(key, part):
    amp_key, base_key = jax.random.split(key)
    upper_log = math.log(10.0)
    amplitude = jnp.exp(jax.random.uniform(amp_key, (1, DATES, ROWS // LOOK_AZ, COLS // LOOK_RG), jnp.float32, 0.0, upper_log))
    amplitude = jnp.repeat(jnp.repeat(amplitude, LOOK_AZ, axis=2), LOOK_RG, axis=3)
    base_field = jnp.clip(jax.random.normal(base_key, (2, DATES, ROWS, COLS), jnp.float32), -6.0, 6.0)
    return (base_field * amplitude).astype(jnp.bfloat16)


def draw_partner(key, part):
    scores = jax.random.randint(key, (DATES, SPAN), 0, 1 << 20, dtype=jnp.int32) * SPAN + jnp.arange(SPAN, dtype=jnp.int32)[None, :]
    scores = jnp.where(jnp.arange(SPAN, dtype=jnp.int32)[None, :] == 0, -1, scores)
    deltas = jnp.argsort(scores, axis=1)[:, :PER_DATE].astype(jnp.int32) + 1
    date_index = jnp.arange(DATES, dtype=jnp.int32)[:, None]
    forward = date_index + deltas
    chosen = jnp.where(forward < DATES, forward, date_index - deltas)
    return chosen.reshape(DATES * PER_DATE).astype(jnp.int32)


def set_ends(values, rng, least, top_value):
    extent = values.shape
    index_at = [jax.random.randint(jax.random.fold_in(rng, axis), (), 0, extent[axis]) for axis in range(len(extent))]
    values = values.at[tuple(index_at)].set(least)
    longest = extent.index(max(extent))
    index_at[longest] = (index_at[longest] + 1) % extent[longest]
    return values.at[tuple(index_at)].set(top_value)


def routed_block(stream_key, own, number, rows, amount, top, bound, lean):
    ranking = jax.random.permutation(stream_key, amount)
    heavy_load, common = shares(amount, rows * top, bound, lean, True), shares(amount, rows * top, bound, lean, False)
    places = jnp.arange(amount)

    def named(sizes, offset_by):
        used = int((sizes > 0).sum())
        fixed = max(1, used // 4)
        shifted = fixed + (places - fixed + offset_by * (used - fixed)) % max(1, amount - fixed)
        return jnp.zeros((amount,), jnp.int32).at[ranking[jnp.where(places < fixed, places, shifted)]].set(jnp.asarray(sizes, jnp.int32))

    sizes = jnp.where(number % 4 == 0, named(heavy_load, number // 4), named(common, number - number // 4 - 1))
    mixed = jax.random.permutation(jax.random.fold_in(own, 3), amount)
    source_of, taker = mixed[0:amount // 2 * 2:2], mixed[1:amount // 2 * 2:2]
    room = jnp.minimum(sizes[source_of] - 1, bound - sizes[taker]) // 2
    room = jnp.where((source_of == ranking[0]) | (taker == ranking[0]) | (sizes[taker] == 0), 0, jnp.maximum(room, 0))
    shifted = jax.random.randint(jax.random.fold_in(own, 4), (amount // 2,), 0, 1 << 20) % (room + 1)
    sizes = sizes.at[source_of].add(-shifted).at[taker].add(shifted)
    labels = jnp.searchsorted(jnp.cumsum(sizes), jnp.arange(rows * top), side="right").astype(jnp.int32)
    listing = labels.reshape(top, rows).T
    listing = listing[jax.random.permutation(jax.random.fold_in(own, 1), rows)]
    offset_by = jax.random.randint(jax.random.fold_in(own, 2), (rows, 1), 0, top)
    return jnp.take_along_axis(listing, (jnp.arange(top)[None, :] + offset_by) % top, axis=1)


def shares(amount, total, most, lean, full):
    portions = [(1 << 20) // math.isqrt(standing ** lean) + 1 for standing in range(1, amount + 1)]
    largest = most if full else min(most, max(-(-total // amount), total * portions[0] // sum(portions)))
    least = 1 if total - largest >= amount - 1 else 0
    holding, surplus = [largest] + [least] * (amount - 1), total - largest - least * (amount - 1)
    while surplus > 0:
        movable = [i for i in range(1, amount) if holding[i] < largest] or [i for i in range(1, amount) if holding[i] < most]
        whole, left = sum([portions[i] for i in movable]), surplus
        for i in movable:
            more = min(most - holding[i], max(1, left * portions[i] // whole), surplus)
            holding[i] = holding[i] + more
            surplus = surplus - more
    return np.array(holding)


def bell_draw(rng, extent, scale, most, kind=jnp.bfloat16):
    values = scale * jax.random.normal(rng, extent, jnp.float32)
    return jnp.clip(values, min=-most, max=most).astype(kind)


def setup_inputs(seed: int = 0) -> dict:
    seeds = jax.random.split(jax.random.key(seed), 9)
    slc_stack = draw_slc_stack(jax.random.fold_in(seeds[8], 71), 0)
    offsets = set_ends(jax.random.randint(seeds[1], (DATES, NRB), 0 - MAXOFF, MAXOFF + 1), jax.random.fold_in(seeds[1], 1), 0 - MAXOFF, MAXOFF).astype(jnp.int32)
    kernels = bell_draw(seeds[2], (DATES, NRB, TAPS), 0.4, 2.5, jnp.float32)
    partner = draw_partner(jax.random.fold_in(seeds[8], 71), 0)
    inverse = bell_draw(seeds[4], (SERIES, IFGS), PER_DATE ** -0.5, 3.5)
    rate_weights = bell_draw(seeds[5], (SERIES,), SERIES ** -0.5, 0.4375, jnp.float32)
    owners_keys = jax.random.split(jax.random.fold_in(seeds[6], 1), STRIPS * PIX_STRIP // PIX_DEV)
    owners_turns = jax.random.permutation(jax.random.fold_in(seeds[6], 3), STRIPS * PIX_STRIP // PIX_DEV)
    owners = jax.vmap(lambda own, number: routed_block(jax.random.fold_in(seeds[6], 2), own, number, PIX_DEV, STRIPS, 1, MOST, 2))(owners_keys, owners_turns).reshape((STRIPS, PIX_STRIP, 1))
    map_cell = set_ends(jax.random.randint(seeds[7], (STRIPS, PIX_STRIP), 0, TILE_CELLS), jax.random.fold_in(seeds[7], 1), 0, TILE_CELLS - 1).astype(jnp.int32)
    return {"slc_stack": slc_stack, "offsets": offsets, "kernels": kernels, "partner": partner, "inverse": inverse, "rate_weights": rate_weights, "owners": owners, "map_cell": map_cell}


def look_mean(values_field):
    dims_shape = values_field.shape
    split_field = values_field.reshape(dims_shape[:-2] + (dims_shape[-2] // LOOK_AZ, LOOK_AZ, dims_shape[-1] // LOOK_RG, LOOK_RG))
    return lax.optimization_barrier(jnp.mean(split_field, axis=(-3, -1)))

def resample_date(block, shift_row, kernel_row, out_width):
    blocks = block.reshape(2, shift_row.shape[0], ROW_BLOCK, block.shape[-1])

    def one_block(block_piece, shift_value, kernel_taps):
        window = lax.dynamic_slice_in_dim(block_piece, HALO + shift_value - TAPS // 2, out_width + TAPS - 1, 2)
        accumulated = kernel_taps[0] * window[:, :, 0:out_width].astype(jnp.float32)
        for tap_index in range(1, TAPS):
            accumulated = accumulated + kernel_taps[tap_index] * window[:, :, tap_index:tap_index + out_width].astype(jnp.float32)
        return accumulated.astype(jnp.bfloat16)
    result = jax.vmap(one_block, in_axes=(1, 0, 0), out_axes=1)(blocks, shift_row, kernel_row)
    return result.reshape(2, block.shape[1], out_width)

def reference(slc_stack, offsets, kernels, partner, inverse, rate_weights, owners, map_cell):
    padded = jnp.pad(slc_stack, ((0, 0), (0, 0), (0, 0), (HALO, HALO)))
    by_date = jnp.moveaxis(padded, 1, 0)

    def one_date(inputs):
        block, shift_row, kernel_row = inputs
        resampled_date = resample_date(block, shift_row, kernel_row, COLS)
        real_part = resampled_date[0].astype(jnp.float32)
        imag_part = resampled_date[1].astype(jnp.float32)
        return (resampled_date, look_mean(real_part * real_part + imag_part * imag_part))
    resampled, power = lax.map(one_date, (by_date, offsets, kernels))

    def one_pair(inputs):
        pair_index, second_index = inputs
        first_index = pair_index // PER_DATE
        first_slc = resampled[first_index].astype(jnp.float32)
        second_slc = resampled[second_index].astype(jnp.float32)
        cross = look_mean(first_slc[1] * second_slc[0] - first_slc[0] * second_slc[1])
        return (cross / jnp.sqrt(power[first_index] * power[second_index] + 1e-06)).astype(jnp.bfloat16)
    phase_values = lax.map(one_pair, (jnp.arange(IFGS, dtype=jnp.int32), partner))
    pixel_phase = phase_values.reshape(IFGS, LROWS, STRIPS, LC_DEV).transpose(0, 2, 1, 3).reshape(IFGS, NPIX)
    series = jnp.dot(inverse, pixel_phase, preferred_element_type=jnp.float32)
    velocity = jnp.dot(rate_weights, series, precision=lax.Precision.HIGHEST)
    pixel_rows = jnp.concatenate([series.T, velocity[:, None]], axis=1).astype(jnp.bfloat16)
    target = owners.reshape(NPIX) * TILE_CELLS + map_cell.reshape(NPIX)
    tile_totals = jax.ops.segment_sum(pixel_rows.astype(jnp.float32), target, num_segments=STRIPS * TILE_CELLS)
    tile_counts = jax.ops.segment_sum(jnp.ones((NPIX,), jnp.float32), target, num_segments=STRIPS * TILE_CELLS)
    geocoded = tile_totals / jnp.maximum(tile_counts, 1.0)[:, None]
    return geocoded.reshape(STRIPS, TILE_CELLS, DATES)
```

```python
import functools

import jax
import jax.numpy as jnp
import numpy as np
from jax import lax
from jax.experimental import pallas as pl
from jax.experimental.pallas import tpu as pltpu
from jax.sharding import PartitionSpec as P

PER_DATE = 3
SPAN = 6
HALF = 3
ROW_BLOCK = 20
TAPS = 8
LOOK_AZ = 5
LOOK_RG = 20
LROWS = 8
LANES = 128
ROWS = 40
DATES = 192
K_ROWS = 64
EXTRA = 9
PAIR_ROWS = 48
F32 = jnp.float32
BF16 = jnp.bfloat16
VMEM_BYTES = 56 * 1024 * 1024

INNER = [(a, a + s) for a in range(6) for s in range(1, 7)]
INNER += [(a, b) for a in range(6, 11) for b in range(a + 1, 12)]
CROSS = [(a, b) for b in range(12, 15) for a in range(b - 6, 12)]
BEFORE = [(a, b) for b in range(15, 18) for a in range(b - 6, 12)]


def iota(shape, dim):
    return lax.broadcasted_iota(jnp.int32, shape, dim)


def lane_left(tiles, by, keep):
    lane = iota(tiles[0].shape, 1)
    turned = [pltpu.roll(t, LANES - by, 1) for t in tiles]
    out = [
        jnp.where(lane < LANES - by, turned[j], turned[j + 1])
        for j in range(len(tiles) - 1)
    ]
    if keep:
        out.append(turned[-1])
    return out


def resample(own, near, far, meta, shifts, taps, part, date, zs, slot):
    first, odd = meta[0], meta[2]
    count = own.shape[-1] // LANES
    at = jnp.clip(first + date, 0, DATES - 1)
    tile_a = near[part, date].astype(F32)
    tile_b = far[part, date].astype(F32)
    is_odd = odd == 1
    left = jnp.where(is_odd, tile_a, tile_b)
    right = jnp.where(is_odd, tile_b, tile_a)
    line = own[part, date].astype(F32)
    tiles = [left] + [line[:, LANES * j : LANES * (j + 1)] for j in range(count)] + [right]
    turn = [4 - shifts[b, at] for b in range(2)]
    lane = iota((24, LANES), 1)
    row = iota((8, LANES), 0)
    top = [pltpu.roll(t[:24], turn[0], 1) for t in tiles]
    low = [pltpu.roll(t[16:], turn[1], 1) for t in tiles]
    for j in range(count + 1):
        upper = jnp.where(lane < turn[0], top[j], top[j + 1])
        lower = jnp.where(lane < turn[1], low[j], low[j + 1])
        zs[slot, j, 0:16, :] = upper[:16]
        zs[slot, j, 16:24, :] = jnp.where(row < 4, upper[16:], lower[:8])
        zs[slot, j, 24:40, :] = lower[8:]
    weight = [
        jnp.where(row < 4, taps[t, at], taps[TAPS + t, at]) for t in range(TAPS)
    ]
    slabs = []
    for k in range(LOOK_AZ):
        z = [
            zs[slot, j, pl.ds(k, LROWS, stride=LOOK_AZ), :] for j in range(count + 1)
        ]
        z1 = lane_left(z, 1, True)
        a = [
            [weight[2 * t] * z[j] + weight[2 * t + 1] * z1[j] for j in range(count + 1)]
            for t in range(4)
        ]
        a1 = lane_left(a[1], 2, True)
        a3 = lane_left(a[3], 2, True)
        b0 = [a[0][j] + a1[j] for j in range(count + 1)]
        b1 = lane_left([a[2][j] + a3[j] for j in range(count + 1)], 4, False)
        slabs.append([(b0[j] + b1[j]).astype(BF16) for j in range(count)])
    return slabs


def column(row, rows, offset):
    wide = row.shape[1]
    at = iota((rows, wide), 1) == iota((rows, wide), 0) + offset
    return jnp.sum(jnp.where(at, row, 0.0), axis=1, keepdims=True)


def edge_kernel(meta, shifts, taps, own, near, far, partner, out0, out1, zs):
    odd_date = meta[1]
    local = column((partner[...] - meta[0]).astype(F32), 16, 36 - EXTRA)
    wide = out0.shape[1]
    for out, base in ((out0, 9 - 9 * odd_date), (out1, 9 * odd_date)):
        def one(i, _):
            for part in range(2):
                slabs = resample(own, near, far, meta, shifts, taps, part, base + i, zs, part)
                for k in range(LOOK_AZ):
                    for j, tile in enumerate(slabs[k]):
                        at = pl.multiple_of(i * 80 + part * 40 + k * 8, 8)
                        out[pl.ds(at, 8), LANES * j : LANES * (j + 1)] = tile
            return 0

        lax.fori_loop(0, HALF, one, 0)
        out[240:256, :] = jnp.broadcast_to(local, (16, wide)).astype(BF16)


def window_matrix(depth):
    col, lane = iota((depth, 256), 0), iota((depth, 256), 1)
    start = (lane % 32) * LOOK_RG
    return ((col >= start) & (col < start + LOOK_RG)).astype(BF16)


def window_sum(values, matrix):
    high = values.astype(BF16)
    low = (values - high.astype(F32)).astype(BF16)
    return jnp.dot(high, matrix, preferred_element_type=F32) + jnp.dot(
        low, matrix, preferred_element_type=F32
    )


def cross_sum(first, second):
    total = None
    for k in range(LOOK_AZ):
        re1, im1 = first(0, k), first(1, k)
        re2, im2 = second(0, k), second(1, k)
        term = im1 * re2 - re1 * im2
        total = term if total is None else total + term
    return total


def power_sum(date):
    total = None
    for k in range(LOOK_AZ):
        re, im = date(0, k), date(1, k)
        term = re * re + im * im
        total = term if total is None else total + term
    return total


def phase_of(cross, power_a, power_b):
    mask = iota((8, 256), 1) // 32 == iota((8, 256), 0)
    scale = 1.0 / (LOOK_AZ * LOOK_RG)
    value = (cross * scale) / jnp.sqrt((power_a * scale) * (power_b * scale) + 1e-06)
    return jnp.where(mask, value, 0.0)


def choose(names, have_a, have_b, reverse):
    a, b = names[0:1, :], names[1:2, :]
    take = ((have_a == a) & (have_b == b)).astype(F32)
    if reverse:
        take = take - ((have_a == b) & (have_b == a)).astype(F32)
    return take.astype(BF16)


def inner_kernel(
    meta, shifts, taps, own, near, far, partner, names, inverse, owners,
    phase_out, power_out, kept_out, weight_out, place_out,
    zs, ys, ps, ss, pm,
):
    width = own.shape[-1]
    count = width // LANES

    def one_date(d, _):
        for part in range(2):
            slabs = resample(own, near, far, meta, shifts, taps, part, d, zs, part)
            for k in range(LOOK_AZ):
                for j, tile in enumerate(slabs[k]):
                    ys[d, part, 8 * k : 8 * k + 8, LANES * j : LANES * (j + 1)] = tile.astype(F32)

        def date(part, k):
            return ys[d, part, 8 * k : 8 * k + 8, :]

        ps[pl.ds(pl.multiple_of(d * 8, 8), 8), :] = power_sum(date)
        return 0

    lax.fori_loop(0, 12, one_date, 0)
    for d in range(9):
        for part in range(2):
            at = d * 80 + part * 40
            kept_out[at : at + 40, :] = ys[d + 3, part].astype(BF16)

    def reader(d):
        return lambda part, k: ys[d, part, 8 * k : 8 * k + 8, :]

    def one_first(a, _):
        for s in range(SPAN):
            at = pl.multiple_of((a * SPAN + s) * 8, 8)
            ss[pl.ds(at, 8), :] = cross_sum(reader(a), reader(a + s + 1))
        return 0

    lax.fori_loop(0, 6, one_first, 0)
    for c in range(36, len(INNER)):
        a, b = INNER[c]
        ss[c * 8 : c * 8 + 8, :] = cross_sum(reader(a), reader(b))
    ss[len(INNER) * 8 :, :] = jnp.zeros_like(ss[len(INNER) * 8 :, :])
    matrix = window_matrix(width)
    power_out[...] = window_sum(ps[...], matrix)
    sums = window_sum(ss[...], matrix)
    for c, (a, b) in enumerate(INNER):
        rows = slice(8 * c, 8 * c + 8)
        pm[rows, :] = phase_of(
            sums[rows], power_out[8 * a : 8 * a + 8, :], power_out[8 * b : 8 * b + 8, :]
        )
    pm[len(INNER) * 8 :, :] = jnp.zeros_like(pm[len(INNER) * 8 :, :])
    local = column((partner[...] - meta[0]).astype(F32), PAIR_ROWS, 0)
    row = iota((PAIR_ROWS, 1), 0)
    have_a = jnp.where(row < 36, row // PER_DATE, -9).astype(F32)
    take = choose(names, have_a, local, True)
    phase_out[...] = jnp.dot(take, pm[...].astype(BF16), preferred_element_type=F32)

    rows = weight_out.shape[0]
    group, k = iota((rows, 1), 0) // K_ROWS, iota((rows, 1), 0) % K_ROWS
    target = jnp.where(k < 36, 36 * group + k, jnp.where(k < 45, 36 * group + k - 45, -1))
    gather = (iota((rows, inverse.shape[1]), 1) == target).astype(BF16)
    weight_out[...] = lax.dot_general(
        gather, inverse[...], (((1,), (1,)), ((), ())), preferred_element_type=F32
    ).astype(BF16)

    own_row = owners[...].astype(F32)
    n = own_row.shape[1]
    own_col = column(own_row, n, 0)
    earlier = (own_col == own_row) & (iota((n, n), 0) < iota((n, n), 1))
    rank = jnp.sum(earlier.astype(F32), axis=0, keepdims=True)
    dest = (own_row * 2 + rank).astype(jnp.int32)
    place_out[...] = (iota(place_out.shape, 0) == dest).astype(BF16)


def outer_kernel(
    meta, got0, got1, kept, power, phase, partner, names, out, rs, ps, ss, pm
):
    width = got0.shape[1]
    odd_date = meta[1]
    after, before = 3 * odd_date, 3 - 3 * odd_date
    for part in range(2):
        for i in range(HALF):
            at = i * 80 + part * 40
            rs[i, part] = got0[at : at + 40, :].astype(F32)
            rs[i + 3, part] = got1[at : at + 40, :].astype(F32)

    def there(d):
        return lambda part, k: rs[d, part, 8 * k : 8 * k + 8, :]

    def here(d):
        def read(part, k):
            at = (d - 3) * 80 + part * 40 + k * 8
            return kept[at : at + 8, :].astype(F32)
        return read

    for i in range(HALF):
        ps[8 * i : 8 * i + 8, :] = power_sum(there(after + i))
        ps[24 + 8 * i : 32 + 8 * i, :] = power_sum(there(before + i))
    for c, (a, b) in enumerate(CROSS):
        ss[8 * c : 8 * c + 8, :] = cross_sum(here(a), there(after + b - 12))
    for c, (a, b) in enumerate(BEFORE, len(CROSS)):
        ss[8 * c : 8 * c + 8, :] = cross_sum(there(before + a - 9), here(b - 12))
    matrix = window_matrix(width)
    powers = window_sum(ps[...], matrix)
    last = 8 * (len(CROSS) + len(BEFORE))
    ss[last:, :] = jnp.zeros_like(ss[last:, :])
    sums = window_sum(ss[...], matrix)
    for c, (a, b) in enumerate(CROSS + BEFORE):
        rows = slice(8 * c, 8 * c + 8)
        if c < len(CROSS):
            pa = power[8 * a : 8 * a + 8, :]
            pb = powers[8 * (b - 12) : 8 * (b - 12) + 8]
        else:
            pa = powers[24 + 8 * (a - 9) : 32 + 8 * (a - 9)]
            pb = power[8 * (b - 12) : 8 * (b - 12) + 8, :]
        pm[rows, :] = phase_of(sums[rows], pa, pb)
    pm[last:, :] = jnp.zeros_like(pm[last:, :])
    local = column((partner[...] - meta[0]).astype(F32), PAIR_ROWS, 0)
    row = iota((PAIR_ROWS, 1), 0)
    told = jnp.where(odd_date == 1, got0[240:256, 0:LANES], got1[240:256, 0:LANES]).astype(F32)
    told = jnp.max(told, axis=1, keepdims=True)
    spread = (iota((PAIR_ROWS, 16), 0) - 36 == iota((PAIR_ROWS, 16), 1)).astype(BF16)
    moved = jnp.dot(
        spread, jnp.broadcast_to(told, (16, LANES)).astype(BF16), preferred_element_type=F32
    )[:, 0:1]
    mine = jnp.where(row < 36, jnp.where(local < 15, local, -5.0), jnp.where(row < 45, moved, -5.0))
    mine = jnp.where((row >= 36) & (mine < 15), -5.0, mine)
    have_a = jnp.where(row < 36, row // PER_DATE, 9 + (row - 36) // PER_DATE).astype(F32)
    take = choose(names, have_a, mine, False)
    total = phase[...] + jnp.dot(take, pm[...].astype(BF16), preferred_element_type=F32)
    wide = jnp.concatenate([total, jnp.zeros((LANES - PAIR_ROWS, 256), F32)], axis=0)
    turned = jnp.concatenate([wide[:, 0:128].T, wide[:, 128:256].T], axis=0)
    out[...] = pltpu.roll(turned, K_ROWS * odd_date, 1).astype(BF16)


def series_kernel(got, weight, rates, place, cells, out):
    n = got.shape[1]
    pairs = [(got[2 * h].astype(F32) + got[2 * h + 1].astype(F32)).astype(BF16) for h in range(got.shape[0] // 2)]
    phases = jnp.concatenate(pairs, axis=1)
    series = jnp.dot(phases, weight[...], preferred_element_type=F32)
    velocity = jnp.sum(series * rates[...], axis=1, keepdims=True)
    cell = column(cells[...].astype(F32), n, 0) + 1.0
    lane = iota((n, 256), 1)
    rows = jnp.concatenate([series, jnp.zeros((n, 256 - series.shape[1]), F32)], axis=1)
    rows = jnp.where(lane == 191, velocity, rows)
    rows = jnp.where(lane == 192, 1.0, rows)
    rows = jnp.where(lane == 193, cell, rows)
    out[...] = jnp.dot(place[...], rows.astype(BF16), preferred_element_type=F32).astype(BF16)


def landing_kernel(got, out):
    rows = got[...]
    pick = (iota((8, 256), 1) == 193).astype(BF16)
    cells = lax.dot_general(pick, rows, (((1,), (1,)), ((), ())), preferred_element_type=F32)
    land = (cells[0:1, :] - 1.0 == iota((LANES, rows.shape[0]), 0).astype(F32)).astype(BF16)
    out[...] = jnp.dot(land, rows, preferred_element_type=F32).astype(BF16)


def final_kernel(got, out):
    total = got[0].astype(F32)
    for g in range(1, got.shape[0]):
        total = total + got[g].astype(F32)
    counts = jnp.sum(jnp.where(iota(total.shape, 1) == 192, total, 0.0), axis=1, keepdims=True)
    mean = total / jnp.maximum(counts, 1.0)
    out[...] = mean[:, 0:192]


SMEM = pl.BlockSpec(memory_space=pltpu.SMEM)
VMEM = pl.BlockSpec(memory_space=pltpu.VMEM)


def call(kernel, smem, vmem, outs, scratch=()):
    return pl.pallas_call(
        kernel,
        in_specs=[SMEM] * len(smem) + [VMEM] * len(vmem),
        out_specs=[VMEM] * len(outs),
        out_shape=[jax.ShapeDtypeStruct(s, t) for s, t in outs],
        scratch_shapes=list(scratch),
        compiler_params=pltpu.CompilerParams(vmem_limit_bytes=VMEM_BYTES),
    )(*smem, *vmem)


def swaps(count, start):
    return [p for i in range(start, count - 1, 2) for p in ((i, i + 1), (i + 1, i))]


def pair_names(pairs, rows):
    names = np.full((2, rows), -20.0, np.float32)
    for c, (a, b) in enumerate(pairs):
        names[0, 8 * c : 8 * c + 8] = a
        names[1, 8 * c : 8 * c + 8] = b
    return jnp.asarray(names)


def local(slc_stack, offsets, kernels, partner, inverse, rate_weights, owners, map_cell):
    date_count, width = slc_stack.shape[1], slc_stack.shape[3]
    groups, strips = lax.axis_size("date"), lax.axis_size("col")
    group, strip = lax.axis_index("date"), lax.axis_index("col")
    meta = jnp.stack([group * date_count, group % 2, strip % 2]).astype(jnp.int32)
    shifts = offsets.T
    taps = jnp.transpose(kernels, (1, 2, 0)).reshape(2 * TAPS, DATES)
    partner_row = partner.reshape(1, -1)

    head, tail = slc_stack[..., :LANES], slc_stack[..., width - LANES :]
    even = strip % 2 == 0
    near = lax.ppermute(jnp.where(even, tail, head), "col", swaps(strips, 0))
    far = lax.ppermute(jnp.where(even, head, tail), "col", swaps(strips, 1))
    scratch_z = pltpu.VMEM((2, width // LANES + 1, ROWS, LANES), F32)
    edge0, edge1 = call(
        edge_kernel,
        (meta, shifts, taps),
        (slc_stack, near, far, partner_row),
        [((256, width), BF16)] * 2,
        [scratch_z],
    )
    got0 = lax.ppermute(edge0, "date", swaps(groups, 0))
    got1 = lax.ppermute(edge1, "date", swaps(groups, 1))
    inner_rows = 8 * (len(INNER) + 1)
    outer_rows = 8 * (len(CROSS) + len(BEFORE) + 1)
    phase, power, kept, weight, place = call(
        inner_kernel,
        (meta, shifts, taps),
        (
            slc_stack, near, far, partner_row, pair_names(INNER, inner_rows), inverse,
            owners.reshape(1, -1),
        ),
        [
            ((PAIR_ROWS, 256), F32),
            ((96, 256), F32),
            ((720, width), BF16),
            ((groups * K_ROWS, inverse.shape[0]), BF16),
            ((2 * strips, 256 // groups), BF16),
        ],
        [
            scratch_z,
            pltpu.VMEM((12, 2, ROWS, width), F32),
            pltpu.VMEM((96, width), F32),
            pltpu.VMEM((inner_rows, width), F32),
            pltpu.VMEM((inner_rows, 256), F32),
        ],
    )
    (sent,) = call(
        outer_kernel,
        (meta,),
        (got0, got1, kept, power, phase, partner_row, pair_names(CROSS + BEFORE, outer_rows)),
        [((256, LANES), BF16)],
        [
            pltpu.VMEM((6, 2, ROWS, width), F32),
            pltpu.VMEM((48, width), F32),
            pltpu.VMEM((outer_rows, width), F32),
            pltpu.VMEM((outer_rows, 256), F32),
        ],
    )
    block = 256 // groups
    phases = lax.all_to_all(sent.reshape(groups, block, LANES), "date", 0, 0, tiled=True)
    (routed,) = call(
        series_kernel,
        (),
        (phases, weight, rate_weights.reshape(1, -1), place, map_cell),
        [((2 * strips, 256), BF16)],
    )
    landed = lax.all_to_all(routed.reshape(strips, 2, 256), "col", 0, 0, tiled=True)
    (totals,) = call(landing_kernel, (), (landed.reshape(2 * strips, 256),), [((LANES, 256), BF16)])
    parts = lax.all_to_all(
        totals.reshape(groups, LANES // groups, 256), "date", 0, 0, tiled=True
    )
    (mean,) = call(final_kernel, (), (parts,), [((LANES // groups, DATES), F32)])
    return mean.reshape(1, LANES // groups, DATES)


def solution(mesh):
    in_specs = (
        P(None, "date", None, "col"),
        P(),
        P(),
        P("date"),
        P(),
        P(),
        P("col", "date", None),
        P("col", "date"),
    )
    out_specs = P("col", "date", None)
    return jax.shard_map(local, mesh=mesh, in_specs=in_specs, out_specs=out_specs, check_vma=False)
```

```python
import functools

import jax
import jax.numpy as jnp
import numpy as np
from jax import lax
from jax.experimental import pallas as pl
from jax.experimental.pallas import tpu as pltpu
from jax.sharding import PartitionSpec as P

PER_DATE = 3
SPAN = 6
HALF = 3
ROW_BLOCK = 20
TAPS = 8
LOOK_AZ = 5
LOOK_RG = 20
LROWS = 8
LANES = 128
ROWS = 40
DATES = 192
EXTRA = 9
PAIR_ROWS = 48
F32 = jnp.float32
BF16 = jnp.bfloat16
VMEM_BYTES = 24 * 1024 * 1024

INNER = [(a, a + s) for a in range(6) for s in range(1, 7)]
INNER += [(a, b) for a in range(6, 11) for b in range(a + 1, 12)]
CROSS = [(a, b) for b in range(12, 15) for a in range(b - 6, 12)]
BEFORE = [(a, b) for b in range(15, 18) for a in range(b - 6, 12)]


def iota(shape, dim):
    return lax.broadcasted_iota(jnp.int32, shape, dim)


def lane_left(tiles, by, keep):
    lane = iota(tiles[0].shape, 1)
    turned = [pltpu.roll(t, LANES - by, 1) for t in tiles]
    out = [
        jnp.where(lane < LANES - by, turned[j], turned[j + 1])
        for j in range(len(tiles) - 1)
    ]
    if keep:
        out.append(turned[-1])
    return out


def resample(own, near, far, meta, shifts, taps, part, date, zs, slot):
    first, odd = meta[0], meta[2]
    count = own.shape[-1] // LANES
    at = jnp.clip(first + date, 0, DATES - 1)
    tile_a = near[part, date].astype(F32)
    tile_b = far[part, date].astype(F32)
    is_odd = odd == 1
    left = jnp.where(is_odd, tile_a, tile_b)
    right = jnp.where(is_odd, tile_b, tile_a)
    line = own[part, date].astype(F32)
    tiles = [left] + [line[:, LANES * j : LANES * (j + 1)] for j in range(count)] + [right]
    turn = [4 - shifts[b, at] for b in range(2)]
    lane = iota((24, LANES), 1)
    row = iota((8, LANES), 0)
    top = [pltpu.roll(t[:24], turn[0], 1) for t in tiles]
    low = [pltpu.roll(t[16:], turn[1], 1) for t in tiles]
    for j in range(count + 1):
        upper = jnp.where(lane < turn[0], top[j], top[j + 1])
        lower = jnp.where(lane < turn[1], low[j], low[j + 1])
        zs[slot, j, 0:16, :] = upper[:16]
        zs[slot, j, 16:24, :] = jnp.where(row < 4, upper[16:], lower[:8])
        zs[slot, j, 24:40, :] = lower[8:]
    weight = [
        jnp.where(row < 4, taps[t, at], taps[TAPS + t, at]) for t in range(TAPS)
    ]
    slabs = []
    for k in range(LOOK_AZ):
        z = [
            zs[slot, j, pl.ds(k, LROWS, stride=LOOK_AZ), :] for j in range(count + 1)
        ]
        z1 = lane_left(z, 1, True)
        a = [
            [weight[2 * t] * z[j] + weight[2 * t + 1] * z1[j] for j in range(count + 1)]
            for t in range(4)
        ]
        a1 = lane_left(a[1], 2, True)
        a3 = lane_left(a[3], 2, True)
        b0 = [a[0][j] + a1[j] for j in range(count + 1)]
        b1 = lane_left([a[2][j] + a3[j] for j in range(count + 1)], 4, False)
        slabs.append([(b0[j] + b1[j]).astype(BF16) for j in range(count)])
    return slabs


def column(row, rows, offset):
    wide = row.shape[1]
    at = iota((rows, wide), 1) == iota((rows, wide), 0) + offset
    return jnp.sum(jnp.where(at, row, 0.0), axis=1, keepdims=True)


def edge_kernel(meta, shifts, taps, own, near, far, partner, out0, out1, zs):
    odd_date = meta[1]
    local = column((partner[...] - meta[0]).astype(F32), 16, 36 - EXTRA)
    wide = out0.shape[1]
    for out, base in ((out0, 9 - 9 * odd_date), (out1, 9 * odd_date)):
        def one(i, _):
            for part in range(2):
                slabs = resample(own, near, far, meta, shifts, taps, part, base + i, zs, part)
                for k in range(LOOK_AZ):
                    for j, tile in enumerate(slabs[k]):
                        at = pl.multiple_of(i * 80 + part * 40 + k * 8, 8)
                        out[pl.ds(at, 8), LANES * j : LANES * (j + 1)] = tile
            return 0

        lax.fori_loop(0, HALF, one, 0, unroll=True)
        out[240:256, :] = jnp.broadcast_to(local, (16, wide)).astype(BF16)


def window_matrix(depth):
    col, lane = iota((depth, 256), 0), iota((depth, 256), 1)
    start = (lane % 32) * LOOK_RG
    return ((col >= start) & (col < start + LOOK_RG)).astype(BF16)


def window_sum(values, matrix):
    high = values.astype(BF16)
    low = (values - high.astype(F32)).astype(BF16)
    return jnp.dot(high, matrix, preferred_element_type=F32) + jnp.dot(
        low, matrix, preferred_element_type=F32
    )


def cross_sum(first, second):
    total = None
    for k in range(LOOK_AZ):
        re1, im1 = first(0, k), first(1, k)
        re2, im2 = second(0, k), second(1, k)
        term = im1 * re2 - re1 * im2
        total = term if total is None else total + term
    return total


def power_sum(date):
    total = None
    for k in range(LOOK_AZ):
        re, im = date(0, k), date(1, k)
        term = re * re + im * im
        total = term if total is None else total + term
    return total


def phase_of(cross, power_a, power_b):
    mask = iota((8, 256), 1) // 32 == iota((8, 256), 0)
    scale = 1.0 / (LOOK_AZ * LOOK_RG)
    value = (cross * scale) / jnp.sqrt((power_a * scale) * (power_b * scale) + 1e-06)
    return jnp.where(mask, value, 0.0)


def choose(names, have_a, have_b, reverse):
    a, b = names[0:1, :], names[1:2, :]
    take = ((have_a == a) & (have_b == b)).astype(F32)
    if reverse:
        take = take - ((have_a == b) & (have_b == a)).astype(F32)
    return take.astype(BF16)


def inner_kernel(
    meta, shifts, taps, own, near, far, partner, names, inverse, rates, owners, cells,
    phase_out, power_out, kept_out, weight_out, rates_out,
    zs, ys, ps, ss, pm,
):
    width = own.shape[-1]
    count = width // LANES

    def one_date(d, _):
        for part in range(2):
            slabs = resample(own, near, far, meta, shifts, taps, part, d, zs, part)
            for k in range(LOOK_AZ):
                for j, tile in enumerate(slabs[k]):
                    ys[d, part, 8 * k : 8 * k + 8, LANES * j : LANES * (j + 1)] = tile.astype(F32)

        def date(part, k):
            return ys[d, part, 8 * k : 8 * k + 8, :]

        ps[pl.ds(pl.multiple_of(d * 8, 8), 8), :] = power_sum(date)
        return 0

    lax.fori_loop(0, 12, one_date, 0, unroll=2)
    for d in range(9):
        for part in range(2):
            at = d * 80 + part * 40
            kept_out[at : at + 40, :] = ys[d + 3, part].astype(BF16)

    def reader(d):
        return lambda part, k: ys[d, part, 8 * k : 8 * k + 8, :]

    def one_first(a, _):
        for s in range(SPAN):
            at = pl.multiple_of((a * SPAN + s) * 8, 8)
            ss[pl.ds(at, 8), :] = cross_sum(reader(a), reader(a + s + 1))
        return 0

    lax.fori_loop(0, 6, one_first, 0)
    for c in range(36, len(INNER)):
        a, b = INNER[c]
        ss[c * 8 : c * 8 + 8, :] = cross_sum(reader(a), reader(b))
    ss[len(INNER) * 8 :, :] = jnp.zeros_like(ss[len(INNER) * 8 :, :])
    matrix = window_matrix(width)
    power_out[...] = window_sum(ps[...], matrix)
    sums = window_sum(ss[...], matrix)
    for c, (a, b) in enumerate(INNER):
        rows = slice(8 * c, 8 * c + 8)
        pm[rows, :] = phase_of(
            sums[rows], power_out[8 * a : 8 * a + 8, :], power_out[8 * b : 8 * b + 8, :]
        )
    pm[len(INNER) * 8 :, :] = jnp.zeros_like(pm[len(INNER) * 8 :, :])
    local = column((partner[...] - meta[0]).astype(F32), PAIR_ROWS, 0)
    row = iota((PAIR_ROWS, 1), 0)
    have_a = jnp.where(row < 36, row // PER_DATE, -9).astype(F32)
    take = choose(names, have_a, local, True)

    spots = iota((1, weight_out.shape[1]), 1)
    group, k = spots // PAIR_ROWS, spots % PAIR_ROWS
    target = jnp.where(k < 36, 36 * group + k, jnp.where(k < 45, 36 * group + k - 45, -1))
    gather = (iota((inverse.shape[1], weight_out.shape[1]), 0) == target).astype(BF16)
    weight_out[0:191, :] = jnp.dot(inverse[...], gather, preferred_element_type=F32).astype(BF16)
    weight_out[191:192, :] = jnp.zeros((1, weight_out.shape[1]), BF16)
    rates_out[...] = jnp.broadcast_to(column(rates[...], DATES, 0), rates_out.shape)

    n = owners.shape[1]
    spread = (iota((n, 256), 1) == iota((n, 256), 0) + n * meta[3]).astype(BF16)
    codes = jnp.concatenate([owners[...], cells[...]], axis=0).astype(F32).astype(BF16)
    placed = jnp.dot(codes, spread, preferred_element_type=F32)
    lines = iota((PAIR_ROWS, 256), 0)
    phases = jnp.dot(take, pm[...].astype(BF16), preferred_element_type=F32)
    phases = jnp.where(lines == 46, placed[0:1, :], phases)
    phase_out[...] = jnp.where(lines == 47, placed[1:2, :], phases)


def outer_kernel(
    meta, got0, got1, kept, power, phase, partner, names, out, rs, ps, ss, pm
):
    width = got0.shape[1]
    odd_date = meta[1]
    after, before = 3 * odd_date, 3 - 3 * odd_date
    for part in range(2):
        for i in range(HALF):
            at = i * 80 + part * 40
            rs[i, part] = got0[at : at + 40, :].astype(F32)
            rs[i + 3, part] = got1[at : at + 40, :].astype(F32)

    def there(d):
        return lambda part, k: rs[d, part, 8 * k : 8 * k + 8, :]

    def here(d):
        def read(part, k):
            at = (d - 3) * 80 + part * 40 + k * 8
            return kept[at : at + 8, :].astype(F32)
        return read

    for i in range(HALF):
        ps[8 * i : 8 * i + 8, :] = power_sum(there(after + i))
        ps[24 + 8 * i : 32 + 8 * i, :] = power_sum(there(before + i))
    for c, (a, b) in enumerate(CROSS):
        ss[8 * c : 8 * c + 8, :] = cross_sum(here(a), there(after + b - 12))
    for c, (a, b) in enumerate(BEFORE, len(CROSS)):
        ss[8 * c : 8 * c + 8, :] = cross_sum(there(before + a - 9), here(b - 12))
    matrix = window_matrix(width)
    powers = window_sum(ps[...], matrix)
    last = 8 * (len(CROSS) + len(BEFORE))
    ss[last:, :] = jnp.zeros_like(ss[last:, :])
    sums = window_sum(ss[...], matrix)
    for c, (a, b) in enumerate(CROSS + BEFORE):
        rows = slice(8 * c, 8 * c + 8)
        if c < len(CROSS):
            pa = power[8 * a : 8 * a + 8, :]
            pb = powers[8 * (b - 12) : 8 * (b - 12) + 8]
        else:
            pa = powers[24 + 8 * (a - 9) : 32 + 8 * (a - 9)]
            pb = power[8 * (b - 12) : 8 * (b - 12) + 8, :]
        pm[rows, :] = phase_of(sums[rows], pa, pb)
    pm[last:, :] = jnp.zeros_like(pm[last:, :])
    local = column((partner[...] - meta[0]).astype(F32), PAIR_ROWS, 0)
    row = iota((PAIR_ROWS, 1), 0)
    told = jnp.where(odd_date == 1, got0[240:256, 0:LANES], got1[240:256, 0:LANES]).astype(F32)
    told = jnp.max(told, axis=1, keepdims=True)
    spread = (iota((PAIR_ROWS, 16), 0) - 36 == iota((PAIR_ROWS, 16), 1)).astype(BF16)
    moved = jnp.dot(
        spread, jnp.broadcast_to(told, (16, LANES)).astype(BF16), preferred_element_type=F32
    )[:, 0:1]
    mine = jnp.where(row < 36, jnp.where(local < 15, local, -5.0), jnp.where(row < 45, moved, -5.0))
    mine = jnp.where((row >= 36) & (mine < 15), -5.0, mine)
    have_a = jnp.where(row < 36, row // PER_DATE, 9 + (row - 36) // PER_DATE).astype(F32)
    take = choose(names, have_a, mine, False)
    total = phase[...] + jnp.dot(take, pm[...].astype(BF16), preferred_element_type=F32)
    for g in range(out.shape[0]):
        out[g] = total.astype(BF16)


def series_kernel(meta, got, weight, rates, out):
    stack = jnp.concatenate([got[g] for g in range(got.shape[0])], axis=0)
    series = jnp.dot(weight[...], stack, preferred_element_type=F32)
    wide = series.shape[1]
    turned = [series[:, :LANES] * rates[...], series[:, LANES:] * rates[...]]
    velocity = jnp.sum(jnp.concatenate(turned, axis=1), axis=0, keepdims=True)
    series = jnp.where(iota(series.shape, 0) == 191, velocity, series)
    ones = jnp.where(iota((64, wide), 0) == 0, 1.0, 0.0)
    rows = jnp.concatenate([series, ones], axis=0).astype(BF16)
    codes = got[0, 40:48, :].astype(F32)
    for g in range(1, got.shape[0]):
        codes = codes + got[g, 40:48, :].astype(F32)
    owner, cell = codes[6:7, :], codes[7:8, :]
    base = (meta[3] * 8).astype(F32)
    mine = (cell >= base) & (cell < base + 8)
    target = jnp.where(mine, owner * 8 + cell - base, -1.0).astype(jnp.int32)
    select = (iota((out.shape[0], wide), 0) == target).astype(BF16)
    out[...] = lax.dot_general(
        select, rows, (((1,), (1,)), ((), ())), preferred_element_type=F32
    ).astype(BF16)


def final_kernel(got, out):
    total = got[0].astype(F32)
    for g in range(1, got.shape[0]):
        total = total + got[g].astype(F32)
    counts = jnp.sum(jnp.where(iota(total.shape, 1) == 192, total, 0.0), axis=1, keepdims=True)
    mean = total / jnp.maximum(counts, 1.0)
    out[...] = mean[:, 0:192]


SMEM = pl.BlockSpec(memory_space=pltpu.SMEM)
VMEM = pl.BlockSpec(memory_space=pltpu.VMEM)


def call(kernel, smem, vmem, outs, scratch=()):
    return pl.pallas_call(
        kernel,
        in_specs=[SMEM] * len(smem) + [VMEM] * len(vmem),
        out_specs=[VMEM] * len(outs),
        out_shape=[jax.ShapeDtypeStruct(s, t) for s, t in outs],
        scratch_shapes=list(scratch),
        compiler_params=pltpu.CompilerParams(vmem_limit_bytes=VMEM_BYTES),
    )(*smem, *vmem)


def swaps(count, start):
    return [p for i in range(start, count - 1, 2) for p in ((i, i + 1), (i + 1, i))]


def pair_names(pairs, rows):
    names = np.full((2, rows), -20.0, np.float32)
    for c, (a, b) in enumerate(pairs):
        names[0, 8 * c : 8 * c + 8] = a
        names[1, 8 * c : 8 * c + 8] = b
    return jnp.asarray(names)


def local(slc_stack, offsets, kernels, partner, inverse, rate_weights, owners, map_cell):
    date_count, width = slc_stack.shape[1], slc_stack.shape[3]
    groups, strips = lax.axis_size("date"), lax.axis_size("col")
    group, strip = lax.axis_index("date"), lax.axis_index("col")
    meta = jnp.stack([group * date_count, group % 2, strip % 2, group]).astype(jnp.int32)
    shifts = offsets.T
    taps = jnp.transpose(kernels, (1, 2, 0)).reshape(2 * TAPS, DATES)
    partner_row = partner.reshape(1, -1)

    head, tail = slc_stack[..., :LANES], slc_stack[..., width - LANES :]
    even = strip % 2 == 0
    near = lax.ppermute(jnp.where(even, tail, head), "col", swaps(strips, 0))
    far = lax.ppermute(jnp.where(even, head, tail), "col", swaps(strips, 1))
    scratch_z = pltpu.VMEM((2, width // LANES + 1, ROWS, LANES), F32)
    edge0, edge1 = call(
        edge_kernel,
        (meta, shifts, taps),
        (slc_stack, near, far, partner_row),
        [((256, width), BF16)] * 2,
        [scratch_z],
    )
    got0 = lax.ppermute(edge0, "date", swaps(groups, 0))
    got1 = lax.ppermute(edge1, "date", swaps(groups, 1))
    inner_rows = 8 * (len(INNER) + 1)
    outer_rows = 8 * (len(CROSS) + len(BEFORE) + 1)
    phase, power, kept, weight, rates = call(
        inner_kernel,
        (meta, shifts, taps),
        (
            slc_stack, near, far, partner_row, pair_names(INNER, inner_rows), inverse,
            rate_weights.reshape(1, -1), owners.reshape(1, -1), map_cell,
        ),
        [
            ((PAIR_ROWS, 256), F32),
            ((96, 256), F32),
            ((720, width), BF16),
            ((DATES, groups * PAIR_ROWS), BF16),
            ((DATES, LANES), F32),
        ],
        [
            scratch_z,
            pltpu.VMEM((12, 2, ROWS, width), F32),
            pltpu.VMEM((96, width), F32),
            pltpu.VMEM((inner_rows, width), F32),
            pltpu.VMEM((inner_rows, 256), F32),
        ],
    )
    (sent,) = call(
        outer_kernel,
        (meta,),
        (got0, got1, kept, power, phase, partner_row, pair_names(CROSS + BEFORE, outer_rows)),
        [((groups, PAIR_ROWS, 256), BF16)],
        [
            pltpu.VMEM((6, 2, ROWS, width), F32),
            pltpu.VMEM((48, width), F32),
            pltpu.VMEM((outer_rows, width), F32),
            pltpu.VMEM((outer_rows, 256), F32),
        ],
    )
    phases = lax.all_to_all(sent, "date", 0, 0, tiled=True)
    (routed,) = call(series_kernel, (meta,), (phases, weight, rates), [((8 * strips, 256), BF16)])
    parts = lax.all_to_all(routed.reshape(strips, 8, 256), "col", 0, 0, tiled=True)
    (mean,) = call(final_kernel, (), (parts,), [((8, DATES), F32)])
    return mean.reshape(1, 8, DATES)


def solution(mesh):
    in_specs = (
        P(None, "date", None, "col"),
        P(),
        P(),
        P("date"),
        P(),
        P(),
        P("col", "date", None),
        P("col", "date"),
    )
    out_specs = P("col", "date", None)
    return jax.shard_map(local, mesh=mesh, in_specs=in_specs, out_specs=out_specs, check_vma=False)
```

```python
import functools

import jax
import jax.numpy as jnp
import numpy as np
from jax import lax
from jax.experimental import pallas as pl
from jax.experimental.pallas import tpu as pltpu
from jax.sharding import PartitionSpec as P

PER_DATE = 3
SPAN = 6
HALF = 3
ROW_BLOCK = 20
TAPS = 8
LOOK_AZ = 5
LOOK_RG = 20
LROWS = 8
LANES = 128
ROWS = 40
DATES = 192
EXTRA = 9
PAIR_ROWS = 48
F32 = jnp.float32
BF16 = jnp.bfloat16
VMEM_BYTES = 24 * 1024 * 1024

INNER = [(a, a + s) for a in range(6) for s in range(1, 7)]
INNER += [(a, b) for a in range(6, 11) for b in range(a + 1, 12)]
CROSS = [(a, b) for b in range(12, 15) for a in range(b - 6, 12)]
BEFORE = [(a, b) for b in range(15, 18) for a in range(b - 6, 12)]


def iota(shape, dim):
    return lax.broadcasted_iota(jnp.int32, shape, dim)


def fact(table, n):
    return table[2 * TAPS + 3, n].astype(jnp.int32)


def partner_row(table, lines):
    return lines[2 * TAPS + 2 : 2 * TAPS + 3, 0:36] - table[2 * TAPS + 3, 0]


def lane_left(tiles, by, keep):
    lane = iota(tiles[0].shape, 1)
    turned = [pltpu.roll(t, LANES - by, 1) for t in tiles]
    out = [
        jnp.where(lane < LANES - by, turned[j], turned[j + 1])
        for j in range(len(tiles) - 1)
    ]
    if keep:
        out.append(turned[-1])
    return out


def resample(own, near, far, table, part, date, zs, slot):
    first, odd = fact(table, 0), fact(table, 2)
    count = own.shape[-1] // LANES
    at = jnp.clip(first + date, 0, DATES - 1)
    tile_a = near[part, date].astype(F32)
    tile_b = far[part, date].astype(F32)
    is_odd = odd == 1
    left = jnp.where(is_odd, tile_a, tile_b)
    right = jnp.where(is_odd, tile_b, tile_a)
    line = own[part, date].astype(F32)
    tiles = [left] + [line[:, LANES * j : LANES * (j + 1)] for j in range(count)] + [right]
    turn = [4 - table[2 * TAPS + b, at].astype(jnp.int32) for b in range(2)]
    lane = iota((24, LANES), 1)
    row = iota((8, LANES), 0)
    top = [pltpu.roll(t[:24], turn[0], 1) for t in tiles]
    low = [pltpu.roll(t[16:], turn[1], 1) for t in tiles]
    for j in range(count + 1):
        upper = jnp.where(lane < turn[0], top[j], top[j + 1])
        lower = jnp.where(lane < turn[1], low[j], low[j + 1])
        zs[slot, j, 0:16, :] = upper[:16]
        zs[slot, j, 16:24, :] = jnp.where(row < 4, upper[16:], lower[:8])
        zs[slot, j, 24:40, :] = lower[8:]
    weight = [
        jnp.where(row < 4, table[t, at], table[TAPS + t, at]) for t in range(TAPS)
    ]
    slabs = []
    for k in range(LOOK_AZ):
        z = [
            zs[slot, j, pl.ds(k, LROWS, stride=LOOK_AZ), :] for j in range(count + 1)
        ]
        z1 = lane_left(z, 1, True)
        a = [
            [weight[2 * t] * z[j] + weight[2 * t + 1] * z1[j] for j in range(count + 1)]
            for t in range(4)
        ]
        a1 = lane_left(a[1], 2, True)
        a3 = lane_left(a[3], 2, True)
        b0 = [a[0][j] + a1[j] for j in range(count + 1)]
        b1 = lane_left([a[2][j] + a3[j] for j in range(count + 1)], 4, False)
        slabs.append([(b0[j] + b1[j]).astype(BF16) for j in range(count)])
    return slabs


def column(row, rows, offset):
    wide = row.shape[1]
    at = iota((rows, wide), 1) == iota((rows, wide), 0) + offset
    return jnp.sum(jnp.where(at, row, 0.0), axis=1, keepdims=True)


def edge_kernel(table, own, near, far, lines, out0, out1, zs):
    odd_date = fact(table, 1)
    local = column(partner_row(table, lines), 16, 36 - EXTRA)
    wide = out0.shape[1]
    told = jnp.broadcast_to(local, (16, wide)).astype(BF16)
    out0[240:256, :] = told
    out1[240:256, :] = told

    def one(n, _):
        i, part = n // 2, n % 2
        for out, base in ((out0, 9 - 9 * odd_date), (out1, 9 * odd_date)):
            slabs = resample(
                own, near, far, table, part, base + i, zs, 0 if out is out0 else 1
            )
            for k in range(LOOK_AZ):
                for j, tile in enumerate(slabs[k]):
                    at = pl.multiple_of(n * 40 + k * 8, 8)
                    out[pl.ds(at, 8), LANES * j : LANES * (j + 1)] = tile
        return 0

    lax.fori_loop(0, 2 * HALF, one, 0)


def window_matrix(depth):
    col, lane = iota((depth, 256), 0), iota((depth, 256), 1)
    start = (lane % 32) * LOOK_RG
    return ((col >= start) & (col < start + LOOK_RG)).astype(BF16)


def window_sum(values, matrix):
    high = values.astype(BF16)
    low = (values - high.astype(F32)).astype(BF16)
    return jnp.dot(high, matrix, preferred_element_type=F32) + jnp.dot(
        low, matrix, preferred_element_type=F32
    )


def cross_sum(first, second):
    total = None
    for k in range(LOOK_AZ):
        re1, im1 = first(0, k), first(1, k)
        re2, im2 = second(0, k), second(1, k)
        term = im1 * re2 - re1 * im2
        total = term if total is None else total + term
    return total


def power_sum(date):
    total = None
    for k in range(LOOK_AZ):
        re, im = date(0, k), date(1, k)
        term = re * re + im * im
        total = term if total is None else total + term
    return total


def phase_of(cross, power_a, power_b):
    mask = iota((8, 256), 1) // 32 == iota((8, 256), 0)
    scale = 1.0 / (LOOK_AZ * LOOK_RG)
    value = (cross * scale) / jnp.sqrt((power_a * scale) * (power_b * scale) + 1e-06)
    return jnp.where(mask, value, 0.0)


def choose(names, have_a, have_b, reverse):
    a, b = names[0:1, :], names[1:2, :]
    take = ((have_a == a) & (have_b == b)).astype(F32)
    if reverse:
        take = take - ((have_a == b) & (have_b == a)).astype(F32)
    return take.astype(BF16)


def phases_of(pairs, first, sums, powers_a, powers_b, pm):
    def one(n, _):
        for u in range(4):
            c = 4 * n + u
            rows = pl.ds(pl.multiple_of(c * 8, 8), 8)
            row_a = pl.ds(pl.multiple_of(pairs[0, c] * 8, 8), 8)
            row_b = pl.ds(pl.multiple_of(pairs[1, c] * 8, 8), 8)
            pm[rows, :] = phase_of(sums[rows, :], powers_a[row_a, :], powers_b[row_b, :])
        return 0

    lax.fori_loop(0, first // 4, one, 0)


def inner_kernel(
    table, pairs, own, near, far, lines, names, inverse, rates, owners, cells,
    phase_out, power_out, kept_out, weight_out, rates_out,
    zs, ys, ps, ss, pm,
):
    width = own.shape[-1]
    count = width // LANES

    def one_date(d, _):
        for part in range(2):
            slabs = resample(own, near, far, table, part, d, zs, part)
            for k in range(LOOK_AZ):
                for j, tile in enumerate(slabs[k]):
                    ys[d, part, 8 * k : 8 * k + 8, LANES * j : LANES * (j + 1)] = tile.astype(F32)

        def date(part, k):
            return ys[d, part, 8 * k : 8 * k + 8, :]

        ps[pl.ds(pl.multiple_of(d * 8, 8), 8), :] = power_sum(date)
        return 0

    lax.fori_loop(0, 12, one_date, 0)

    def keep(n, _):
        at = pl.multiple_of(n * 80, 16)
        kept_out[pl.ds(at, 80), :] = jnp.concatenate([ys[n + 3, 0], ys[n + 3, 1]], axis=0).astype(BF16)
        return 0

    lax.fori_loop(0, 9, keep, 0)

    def reader(d):
        return lambda part, k: ys[d, part, 8 * k : 8 * k + 8, :]

    def one_pair(c, _):
        at = pl.multiple_of(c * 8, 8)
        ss[pl.ds(at, 8), :] = cross_sum(reader(pairs[0, c]), reader(pairs[1, c]))
        return 0

    total = ss.shape[0] // 8
    lax.fori_loop(0, total, one_pair, 0)
    matrix = window_matrix(width)
    power_out[...] = window_sum(ps[...], matrix)
    block = ss.shape[0] // 4

    def one_block(n, _):
        rows = pl.ds(pl.multiple_of(n * block, 8), block)
        pm[rows, :] = window_sum(ss[rows, :], matrix)
        return 0

    lax.fori_loop(0, 4, one_block, 0)
    phases_of(pairs, total, pm, power_out, power_out, pm)
    local = column(partner_row(table, lines), PAIR_ROWS, 0)
    row = iota((PAIR_ROWS, 1), 0)
    have_a = jnp.where(row < 36, row // PER_DATE, -9).astype(F32)
    take = choose(names, have_a, local, True)

    spots = iota((1, weight_out.shape[1]), 1)
    group, k = spots // PAIR_ROWS, spots % PAIR_ROWS
    target = jnp.where(k < 36, 36 * group + k, jnp.where(k < 45, 36 * group + k - 45, -1))
    gather = (iota((inverse.shape[1], weight_out.shape[1]), 0) == target).astype(BF16)
    weight_out[0:191, :] = jnp.dot(inverse[...], gather, preferred_element_type=F32).astype(BF16)
    weight_out[191:192, :] = jnp.zeros((1, weight_out.shape[1]), BF16)
    rates_out[...] = jnp.broadcast_to(column(rates[...], DATES, 0), rates_out.shape)

    n = owners.shape[1]
    spread = (iota((n, 256), 1) == iota((n, 256), 0) + n * fact(table, 3)).astype(BF16)
    codes = jnp.concatenate([owners[...], cells[...]], axis=0).astype(F32).astype(BF16)
    placed = jnp.dot(codes, spread, preferred_element_type=F32)
    lines = iota((PAIR_ROWS, 256), 0)
    phases = jnp.dot(take, pm[...].astype(BF16), preferred_element_type=F32)
    phases = jnp.where(lines == 46, placed[0:1, :], phases)
    phase_out[...] = jnp.where(lines == 47, placed[1:2, :], phases)


def outer_kernel(
    table, pairs, got0, got1, kept, power, phase, lines, names, out, rs, ps, ss, pm, pw
):
    width = got0.shape[1]
    odd_date = fact(table, 1)

    def fill(n, _):
        at = pl.multiple_of(n * 80, 16)
        both = kept[pl.ds(at, 80), :].astype(F32)
        rs[n, 0], rs[n, 1] = both[:40], both[40:]
        return 0

    lax.fori_loop(0, 9, fill, 0)

    def fill_far(n, _):
        at = pl.multiple_of(n * 80, 16)
        one, two = got0[pl.ds(at, 80), :].astype(F32), got1[pl.ds(at, 80), :].astype(F32)
        first = jnp.where(odd_date == 1, two, one)
        second = jnp.where(odd_date == 1, one, two)
        rs[n + 9, 0], rs[n + 9, 1] = first[:40], first[40:]
        rs[n + 12, 0], rs[n + 12, 1] = second[:40], second[40:]
        return 0

    lax.fori_loop(0, HALF, fill_far, 0)

    def reader(d):
        return lambda part, k: rs[d, part, 8 * k : 8 * k + 8, :]

    def one_power(n, _):
        ps[pl.ds(pl.multiple_of(n * 8, 8), 8), :] = power_sum(reader(n + 9))
        return 0

    lax.fori_loop(0, 2 * HALF, one_power, 0)

    def one_pair(c, _):
        at = pl.multiple_of(c * 8, 8)
        ss[pl.ds(at, 8), :] = cross_sum(reader(pairs[0, c]), reader(pairs[1, c]))
        return 0

    total = ss.shape[0] // 8
    lax.fori_loop(0, total, one_pair, 0)
    matrix = window_matrix(width)
    pw[0:72, :] = power[24:96, :]
    pw[72:120, :] = window_sum(ps[...], matrix)
    pm[...] = window_sum(ss[...], matrix)
    phases_of(pairs, total, pm, pw, pw, pm)
    local = column(partner_row(table, lines), PAIR_ROWS, 0)
    row = iota((PAIR_ROWS, 1), 0)
    told = jnp.where(odd_date == 1, got0[240:256, 0:LANES], got1[240:256, 0:LANES]).astype(F32)
    told = jnp.max(told, axis=1, keepdims=True)
    spread = (iota((PAIR_ROWS, 16), 0) - 36 == iota((PAIR_ROWS, 16), 1)).astype(BF16)
    moved = jnp.dot(
        spread, jnp.broadcast_to(told, (16, LANES)).astype(BF16), preferred_element_type=F32
    )[:, 0:1]
    mine = jnp.where(row < 36, jnp.where(local < 15, local, -5.0), jnp.where(row < 45, moved, -5.0))
    mine = jnp.where((row >= 36) & (mine < 15), -5.0, mine)
    have_a = jnp.where(row < 36, row // PER_DATE, 9 + (row - 36) // PER_DATE).astype(F32)
    take = choose(names, have_a, mine, False)
    total = phase[...] + jnp.dot(take, pm[...].astype(BF16), preferred_element_type=F32)
    for g in range(out.shape[0]):
        out[g] = total.astype(BF16)


def series_kernel(table, got, weight, rates, out):
    stack = jnp.concatenate([got[g] for g in range(got.shape[0])], axis=0)
    series = jnp.dot(weight[...], stack, preferred_element_type=F32)
    wide = series.shape[1]
    turned = [series[:, :LANES] * rates[...], series[:, LANES:] * rates[...]]
    velocity = jnp.sum(jnp.concatenate(turned, axis=1), axis=0, keepdims=True)
    series = jnp.where(iota(series.shape, 0) == 191, velocity, series)
    ones = jnp.where(iota((64, wide), 0) == 0, 1.0, 0.0)
    rows = jnp.concatenate([series, ones], axis=0).astype(BF16)
    codes = got[0, 40:48, :].astype(F32)
    for g in range(1, got.shape[0]):
        codes = codes + got[g, 40:48, :].astype(F32)
    owner, cell = codes[6:7, :], codes[7:8, :]
    base = table[2 * TAPS + 3, 3] * 8.0
    mine = (cell >= base) & (cell < base + 8)
    target = jnp.where(mine, owner * 8 + cell - base, -1.0).astype(jnp.int32)
    select = (iota((out.shape[0], wide), 0) == target).astype(BF16)
    out[...] = lax.dot_general(
        select, rows, (((1,), (1,)), ((), ())), preferred_element_type=F32
    ).astype(BF16)


def final_kernel(got, out):
    total = got[0].astype(F32)
    for g in range(1, got.shape[0]):
        total = total + got[g].astype(F32)
    counts = jnp.sum(jnp.where(iota(total.shape, 1) == 192, total, 0.0), axis=1, keepdims=True)
    mean = total / jnp.maximum(counts, 1.0)
    out[...] = mean[:, 0:192]


SMEM = pl.BlockSpec(memory_space=pltpu.SMEM)
VMEM = pl.BlockSpec(memory_space=pltpu.VMEM)


def call(kernel, smem, vmem, outs, scratch=()):
    return pl.pallas_call(
        kernel,
        in_specs=[SMEM] * len(smem) + [VMEM] * len(vmem),
        out_specs=[VMEM] * len(outs),
        out_shape=[jax.ShapeDtypeStruct(s, t) for s, t in outs],
        scratch_shapes=list(scratch),
        compiler_params=pltpu.CompilerParams(vmem_limit_bytes=VMEM_BYTES),
    )(*smem, *vmem)


def swaps(count, start):
    return [p for i in range(start, count - 1, 2) for p in ((i, i + 1), (i + 1, i))]


def pair_names(pairs, rows):
    names = np.full((2, rows), -20.0, np.float32)
    for c, (a, b) in enumerate(pairs):
        names[0, 8 * c : 8 * c + 8] = a
        names[1, 8 * c : 8 * c + 8] = b
    return jnp.asarray(names)


def pair_table(pairs, rows):
    table = np.zeros((2, rows // 8), np.int32)
    table[:, : len(pairs)] = np.array(pairs, np.int32).T
    return jnp.asarray(table)


def local(slc_stack, offsets, kernels, partner, inverse, rate_weights, owners, map_cell):
    date_count, width = slc_stack.shape[1], slc_stack.shape[3]
    groups, strips = lax.axis_size("date"), lax.axis_size("col")
    group, strip = lax.axis_index("date"), lax.axis_index("col")
    rows = [
        jnp.transpose(kernels, (1, 2, 0)).reshape(2 * TAPS, DATES),
        offsets.T.astype(F32),
        jnp.pad(partner.reshape(1, -1).astype(F32), ((0, 0), (0, DATES - partner.shape[0]))),
    ]
    facts = jnp.stack([group * date_count, group % 2, strip % 2, group]).astype(F32)
    rows.append(jnp.pad(facts.reshape(1, -1), ((0, 4), (0, DATES - 4))))
    table, at = jnp.zeros((24, DATES), F32), 0
    for part in rows:
        table = table + jnp.pad(part, ((at, 24 - at - part.shape[0]), (0, 0)))
        at += part.shape[0]

    own = lax.reduce_precision(slc_stack, 8, 7)
    head, tail = own[..., :LANES], own[..., width - LANES :]
    even = strip % 2 == 0
    tile0, tile1 = jnp.where(even, tail, head), jnp.where(even, head, tail)
    near = lax.ppermute(tile0, "col", swaps(strips, 0))
    far = lax.ppermute(tile1, "col", swaps(strips, 1))
    scratch_z = pltpu.VMEM((2, width // LANES + 1, ROWS, LANES), F32)
    edge0, edge1 = call(
        edge_kernel,
        (table,),
        (own, near, far, table),
        [((256, width), BF16)] * 2,
        [scratch_z],
    )
    got0 = lax.ppermute(edge0, "date", swaps(groups, 0))
    got1 = lax.ppermute(edge1, "date", swaps(groups, 1))
    inner_rows = 8 * (len(INNER) + 1)
    outer_rows = 8 * (len(CROSS) + len(BEFORE) + 3)
    outer_pairs = [(a - 3, b - 3) for a, b in CROSS] + [(a + 3, b - 15) for a, b in BEFORE]
    phase, power, kept, weight, rates = call(
        inner_kernel,
        (table, pair_table(INNER, inner_rows)),
        (
            own, near, far, table, pair_names(INNER, inner_rows), inverse,
            rate_weights.reshape(1, -1), owners.reshape(1, -1), map_cell,
        ),
        [
            ((PAIR_ROWS, 256), F32),
            ((96, 256), F32),
            ((720, width), BF16),
            ((DATES, groups * PAIR_ROWS), BF16),
            ((DATES, LANES), F32),
        ],
        [
            scratch_z,
            pltpu.VMEM((12, 2, ROWS, width), F32),
            pltpu.VMEM((96, width), F32),
            pltpu.VMEM((inner_rows, width), F32),
            pltpu.VMEM((inner_rows, 256), F32),
        ],
    )
    (sent,) = call(
        outer_kernel,
        (table, pair_table(outer_pairs, outer_rows)),
        (got0, got1, kept, power, phase, table, pair_names(CROSS + BEFORE, outer_rows)),
        [((groups, PAIR_ROWS, 256), BF16)],
        [
            pltpu.VMEM((15, 2, ROWS, width), F32),
            pltpu.VMEM((48, width), F32),
            pltpu.VMEM((outer_rows, width), F32),
            pltpu.VMEM((outer_rows, 256), F32),
            pltpu.VMEM((120, 256), F32),
        ],
    )
    phases = lax.all_to_all(sent, "date", 0, 0, tiled=True)
    (routed,) = call(series_kernel, (table,), (phases, weight, rates), [((8 * strips, 256), BF16)])
    parts = lax.all_to_all(routed.reshape(strips, 8, 256), "col", 0, 0, tiled=True)
    (mean,) = call(final_kernel, (), (parts,), [((8, DATES), F32)])
    return mean.reshape(1, 8, DATES)


def solution(mesh):
    in_specs = (
        P(None, "date", None, "col"),
        P(),
        P(),
        P("date"),
        P(),
        P(),
        P("col", "date", None),
        P("col", "date"),
    )
    out_specs = P("col", "date", None)
    return jax.shard_map(local, mesh=mesh, in_specs=in_specs, out_specs=out_specs, check_vma=False)
```

```python
import functools

import jax
import jax.numpy as jnp
import numpy as np
from jax import lax
from jax.experimental import pallas as pl
from jax.experimental.pallas import tpu as pltpu
from jax.sharding import PartitionSpec as P

PER_DATE = 3
SPAN = 6
HALF = 3
ROW_BLOCK = 20
TAPS = 8
HALO = 8
LOOK_AZ = 5
LOOK_RG = 20
LROWS = 8
LANES = 128
ROWS = 40
DATES = 192
EXTRA = 9
PAIR_ROWS = 48
F32 = jnp.float32
BF16 = jnp.bfloat16
VMEM_BYTES = 24 * 1024 * 1024

INNER = [(a, a + s) for a in range(6) for s in range(1, 7)]
INNER += [(a, b) for a in range(6, 11) for b in range(a + 1, 12)]
CROSS = [(a, b) for b in range(12, 15) for a in range(b - 6, 12)]
BEFORE = [(a, b) for b in range(15, 18) for a in range(b - 6, 12)]


def iota(shape, dim):
    return lax.broadcasted_iota(jnp.int32, shape, dim)


def fact(table, n):
    return table[2 * TAPS + 3, n].astype(jnp.int32)


def partner_row(table, lines):
    return lines[2 * TAPS + 2 : 2 * TAPS + 3, 0:36] - table[2 * TAPS + 3, 0]


def lane_left(tiles, by, keep):
    lane = iota(tiles[0].shape, 1)
    turned = [pltpu.roll(t, LANES - by, 1) for t in tiles]
    out = [
        jnp.where(lane < LANES - by, turned[j], turned[j + 1])
        for j in range(len(tiles) - 1)
    ]
    if keep:
        out.append(turned[-1])
    return out


def resample(own, near, far, table, part, date, zs, slot):
    first, odd = fact(table, 0), fact(table, 2)
    count = own.shape[-1] // LANES
    at = jnp.clip(first + date, 0, DATES - 1)
    tile_a, tile_b = near[part].astype(F32), far[part].astype(F32)
    is_odd = odd == 1
    left = pltpu.roll(jnp.where(is_odd, tile_a, tile_b), LANES - HALO - HALO * date, 1)
    right = pltpu.roll(
        jnp.where(is_odd, tile_b, tile_a), lax.rem(LANES - HALO * date, LANES), 1
    )
    line = own[part, date].astype(F32)
    tiles = [left] + [line[:, LANES * j : LANES * (j + 1)] for j in range(count)] + [right]
    turn = [4 - table[2 * TAPS + b, at].astype(jnp.int32) for b in range(2)]
    lane = iota((24, LANES), 1)
    row = iota((8, LANES), 0)
    top = [pltpu.roll(t[:24], turn[0], 1) for t in tiles]
    low = [pltpu.roll(t[16:], turn[1], 1) for t in tiles]
    for j in range(count + 1):
        upper = jnp.where(lane < turn[0], top[j], top[j + 1])
        lower = jnp.where(lane < turn[1], low[j], low[j + 1])
        zs[slot, j, 0:16, :] = upper[:16]
        zs[slot, j, 16:24, :] = jnp.where(row < 4, upper[16:], lower[:8])
        zs[slot, j, 24:40, :] = lower[8:]
    weight = [
        jnp.where(row < 4, table[t, at], table[TAPS + t, at]) for t in range(TAPS)
    ]
    slabs = []
    for k in range(LOOK_AZ):
        z = [
            zs[slot, j, pl.ds(k, LROWS, stride=LOOK_AZ), :] for j in range(count + 1)
        ]
        z1 = lane_left(z, 1, True)
        a = [
            [weight[2 * t] * z[j] + weight[2 * t + 1] * z1[j] for j in range(count + 1)]
            for t in range(4)
        ]
        a1 = lane_left(a[1], 2, True)
        a3 = lane_left(a[3], 2, True)
        b0 = [a[0][j] + a1[j] for j in range(count + 1)]
        b1 = lane_left([a[2][j] + a3[j] for j in range(count + 1)], 4, False)
        slabs.append([(b0[j] + b1[j]).astype(BF16) for j in range(count)])
    return slabs


def column(row, rows, offset):
    wide = row.shape[1]
    at = iota((rows, wide), 1) == iota((rows, wide), 0) + offset
    return jnp.sum(jnp.where(at, row, 0.0), axis=1, keepdims=True)


def pack_kernel(odd, own, out0, out1, acc):
    far = own.shape[3] - LANES
    even = odd[0] == 0
    acc[...] = jnp.zeros_like(acc)

    def one(d, _):
        for part in range(2):
            head = own[part, d, :, 0:LANES].astype(F32)
            tail = own[part, d, :, far : far + LANES].astype(F32)
            head = pltpu.roll(head, HALO * d, 1)
            tail = pltpu.roll(tail, HALO * d + HALO, 1)
            here = iota(head.shape, 1) // HALO == d
            for n, tile in enumerate((jnp.where(even, tail, head), jnp.where(even, head, tail))):
                acc[n, part] = jnp.where(here, tile, acc[n, part])
        return 0

    lax.fori_loop(0, own.shape[1], one, 0)
    out0[...] = acc[0].astype(BF16)
    out1[...] = acc[1].astype(BF16)


def edge_kernel(table, own, near, far, lines, out0, out1, zs):
    odd_date = fact(table, 1)
    local = column(partner_row(table, lines), 16, 36 - EXTRA)
    wide = out0.shape[1]
    told = jnp.broadcast_to(local, (16, wide)).astype(BF16)
    out0[240:256, :] = told
    out1[240:256, :] = told

    def one(n, _):
        i, part = n // 2, n % 2
        for out, base in ((out0, 9 - 9 * odd_date), (out1, 9 * odd_date)):
            slabs = resample(
                own, near, far, table, part, base + i, zs, 0 if out is out0 else 1
            )
            for k in range(LOOK_AZ):
                for j, tile in enumerate(slabs[k]):
                    at = pl.multiple_of(n * 40 + k * 8, 8)
                    out[pl.ds(at, 8), LANES * j : LANES * (j + 1)] = tile
        return 0

    lax.fori_loop(0, 2 * HALF, one, 0)


def window_matrix(depth):
    col, lane = iota((depth, 256), 0), iota((depth, 256), 1)
    start = (lane % 32) * LOOK_RG
    return ((col >= start) & (col < start + LOOK_RG)).astype(BF16)


def window_sum(values, matrix):
    high = values.astype(BF16)
    low = (values - high.astype(F32)).astype(BF16)
    return jnp.dot(high, matrix, preferred_element_type=F32) + jnp.dot(
        low, matrix, preferred_element_type=F32
    )


def cross_sum(first, second):
    total = None
    for k in range(LOOK_AZ):
        re1, im1 = first(0, k), first(1, k)
        re2, im2 = second(0, k), second(1, k)
        term = im1 * re2 - re1 * im2
        total = term if total is None else total + term
    return total


def power_sum(date):
    total = None
    for k in range(LOOK_AZ):
        re, im = date(0, k), date(1, k)
        term = re * re + im * im
        total = term if total is None else total + term
    return total


def phase_of(cross, power_a, power_b, mask):
    scale = 1.0 / (LOOK_AZ * LOOK_RG)
    product = (power_a * scale) * (power_b * scale) + 1e-06
    return jnp.where(mask, (cross * scale) * lax.rsqrt(product), 0.0)


def choose(names, have_a, have_b, reverse):
    a, b = names[0:1, :], names[1:2, :]
    take = ((have_a == a) & (have_b == b)).astype(F32)
    if reverse:
        take = take - ((have_a == b) & (have_b == a)).astype(F32)
    return take.astype(BF16)


def phases_of(pairs, count, pm, powers):
    mask = iota((8, 256), 1) // 32 == iota((8, 256), 0)

    def one(n, _):
        done = []
        for u in range(8):
            c = 8 * n + u
            rows = pl.ds(pl.multiple_of(c * 8, 8), 8)
            row_a = pl.ds(pl.multiple_of(pairs[0, c] * 8, 8), 8)
            row_b = pl.ds(pl.multiple_of(pairs[1, c] * 8, 8), 8)
            done.append(phase_of(pm[rows, :], powers[row_a, :], powers[row_b, :], mask))
        pm[pl.ds(pl.multiple_of(n * 64, 64), 64), :] = jnp.concatenate(done, axis=0)
        return 0

    lax.fori_loop(0, count // 8, one, 0)


def inner_kernel(
    table, pairs, own, near, far, lines, names, inverse, owners, cells,
    phase_out, power_out, ys, weight_out,
    zs, ps, ss, pm, gather,
):
    width = own.shape[-1]
    count = width // LANES

    def one_date(d, _):
        for part in range(2):
            slabs = resample(own, near, far, table, part, d, zs, part)
            for k in range(LOOK_AZ):
                for j, tile in enumerate(slabs[k]):
                    ys[d, part, 8 * k : 8 * k + 8, LANES * j : LANES * (j + 1)] = tile.astype(F32)

        def date(part, k):
            return ys[d, part, 8 * k : 8 * k + 8, :]

        ps[pl.ds(pl.multiple_of(d * 8, 8), 8), :] = power_sum(date)
        return 0

    lax.fori_loop(0, 12, one_date, 0)

    def reader(d):
        return lambda part, k: ys[d, part, 8 * k : 8 * k + 8, :]

    def one_pair(c, _):
        at = pl.multiple_of(c * 8, 8)
        ss[pl.ds(at, 8), :] = cross_sum(reader(pairs[0, c]), reader(pairs[1, c]))
        return 0

    total = ss.shape[0] // 8
    lax.fori_loop(0, total, one_pair, 0)
    matrix = window_matrix(width)
    power_out[...] = window_sum(ps[...], matrix)
    block = ss.shape[0] // 4

    def one_block(n, _):
        rows = pl.ds(pl.multiple_of(n * block, 8), block)
        pm[rows, :] = window_sum(ss[rows, :], matrix)
        return 0

    lax.fori_loop(0, 4, one_block, 0)
    phases_of(pairs, total, pm, power_out)
    local = column(partner_row(table, lines), PAIR_ROWS, 0)
    row = iota((PAIR_ROWS, 1), 0)
    have_a = jnp.where(row < 36, row // PER_DATE, -9).astype(F32)
    take = choose(names, have_a, local, True)

    spots = iota((1, weight_out.shape[1]), 1)
    group, k = spots // PAIR_ROWS, spots % PAIR_ROWS
    target = jnp.where(k < 36, 36 * group + k, jnp.where(k < 45, 36 * group + k - 45, -1))

    def one_rows(n, _):
        at = pl.multiple_of(n * 16, 16)
        gather[pl.ds(at, 16), :] = (iota((16, gather.shape[1]), 0) + at == target).astype(BF16)
        return 0

    lax.fori_loop(0, gather.shape[0] // 16, one_rows, 0)
    weight_out[0:191, :] = jnp.dot(
        inverse[...], gather[...], preferred_element_type=F32
    ).astype(BF16)
    weight_out[191:192, :] = jnp.zeros((1, weight_out.shape[1]), BF16)

    n = owners.shape[1]
    spread = (iota((n, 256), 1) == iota((n, 256), 0) + n * fact(table, 3)).astype(BF16)
    codes = jnp.concatenate([owners[...], cells[...]], axis=0).astype(F32).astype(BF16)
    placed = jnp.dot(codes, spread, preferred_element_type=F32)
    lines = iota((PAIR_ROWS, 256), 0)
    phases = jnp.dot(take, pm[...].astype(BF16), preferred_element_type=F32)
    phases = jnp.where(lines == 46, placed[0:1, :], phases)
    phase_out[...] = jnp.where(lines == 47, placed[1:2, :], phases)


def outer_kernel(
    table, pairs, got0, got1, ys, power, phase, lines, names, out, rs, ps, ss, pm, pw
):
    width = got0.shape[1]
    odd_date = fact(table, 1)

    def fill_far(n, _):
        at = pl.multiple_of(n * 80, 16)
        one, two = got0[pl.ds(at, 80), :].astype(F32), got1[pl.ds(at, 80), :].astype(F32)
        first = jnp.where(odd_date == 1, two, one)
        second = jnp.where(odd_date == 1, one, two)
        rs[n, 0], rs[n, 1] = first[:40], first[40:]
        rs[n + 3, 0], rs[n + 3, 1] = second[:40], second[40:]
        return 0

    lax.fori_loop(0, HALF, fill_far, 0)

    def here(d):
        return lambda part, k: ys[d, part, 8 * k : 8 * k + 8, :]

    def there(d):
        return lambda part, k: rs[d, part, 8 * k : 8 * k + 8, :]

    def one_power(n, _):
        ps[pl.ds(pl.multiple_of(n * 8, 8), 8), :] = power_sum(there(n))
        return 0

    lax.fori_loop(0, 2 * HALF, one_power, 0)

    def one_after(c, _):
        at = pl.multiple_of(c * 8, 8)
        ss[pl.ds(at, 8), :] = cross_sum(here(pairs[0, c]), there(pairs[1, c] - 12))
        return 0

    def one_before(c, _):
        at = pl.multiple_of(c * 8, 8)
        ss[pl.ds(at, 8), :] = cross_sum(there(pairs[0, c] - 12), here(pairs[1, c]))
        return 0

    total = ss.shape[0] // 8
    lax.fori_loop(0, len(CROSS), one_after, 0)
    lax.fori_loop(len(CROSS), len(CROSS) + len(BEFORE), one_before, 0)
    last = 8 * (len(CROSS) + len(BEFORE))
    ss[last:, :] = jnp.zeros_like(ss[last:, :])
    matrix = window_matrix(width)
    pw[0:96, :] = power[...]
    pw[96:144, :] = window_sum(ps[...], matrix)
    pm[...] = window_sum(ss[...], matrix)
    phases_of(pairs, total, pm, pw)
    local = column(partner_row(table, lines), PAIR_ROWS, 0)
    row = iota((PAIR_ROWS, 1), 0)
    told = jnp.where(odd_date == 1, got0[240:256, 0:LANES], got1[240:256, 0:LANES]).astype(F32)
    told = jnp.max(told, axis=1, keepdims=True)
    spread = (iota((PAIR_ROWS, 16), 0) - 36 == iota((PAIR_ROWS, 16), 1)).astype(BF16)
    moved = jnp.dot(
        spread, jnp.broadcast_to(told, (16, LANES)).astype(BF16), preferred_element_type=F32
    )[:, 0:1]
    mine = jnp.where(row < 36, jnp.where(local < 15, local, -5.0), jnp.where(row < 45, moved, -5.0))
    mine = jnp.where((row >= 36) & (mine < 15), -5.0, mine)
    have_a = jnp.where(row < 36, row // PER_DATE, 9 + (row - 36) // PER_DATE).astype(F32)
    take = choose(names, have_a, mine, False)
    total = phase[...] + jnp.dot(take, pm[...].astype(BF16), preferred_element_type=F32)
    for g in range(out.shape[0]):
        out[g] = total.astype(BF16)


def series_kernel(table, got, weight, out):
    stack = jnp.concatenate([got[g] for g in range(got.shape[0])], axis=0)
    series = jnp.dot(weight[...], stack, preferred_element_type=F32)
    wide = series.shape[1]
    rows = jnp.where(iota(series.shape, 0) == 191, 1.0, series)
    rows = jnp.concatenate([rows, jnp.zeros((64, wide), F32)], axis=0).astype(BF16)
    codes = got[0, 40:48, :].astype(F32)
    for g in range(1, got.shape[0]):
        codes = codes + got[g, 40:48, :].astype(F32)
    owner, cell = codes[6:7, :], codes[7:8, :]
    base = table[2 * TAPS + 3, 3] * 8.0
    mine = (cell >= base) & (cell < base + 8)
    target = jnp.where(mine, owner * 8 + cell - base, -1.0).astype(jnp.int32)
    select = (iota((out.shape[0], wide), 0) == target).astype(BF16)
    out[...] = lax.dot_general(
        select, rows, (((1,), (1,)), ((), ())), preferred_element_type=F32
    ).astype(BF16)


def final_kernel(got, rates, out):
    total = got[0].astype(F32)
    for g in range(1, got.shape[0]):
        total = total + got[g].astype(F32)
    total = total[:, 0:DATES]
    lane = iota(total.shape, 1)
    counts = jnp.sum(jnp.where(lane == DATES - 1, total, 0.0), axis=1, keepdims=True)
    velocity = jnp.sum(total * rates[...], axis=1, keepdims=True)
    total = jnp.where(lane == DATES - 1, velocity, total)
    out[...] = total / jnp.maximum(counts, 1.0)


SMEM = pl.BlockSpec(memory_space=pltpu.SMEM)
VMEM = pl.BlockSpec(memory_space=pltpu.VMEM)


def call(kernel, smem, vmem, outs, scratch=()):
    return pl.pallas_call(
        kernel,
        in_specs=[SMEM] * len(smem) + [VMEM] * len(vmem),
        out_specs=[VMEM] * len(outs),
        out_shape=[jax.ShapeDtypeStruct(s, t) for s, t in outs],
        scratch_shapes=list(scratch),
        compiler_params=pltpu.CompilerParams(vmem_limit_bytes=VMEM_BYTES),
    )(*smem, *vmem)


def swaps(count, start):
    return [p for i in range(start, count - 1, 2) for p in ((i, i + 1), (i + 1, i))]


def pair_names(pairs, rows):
    names = np.full((2, rows), -20.0, np.float32)
    for c, (a, b) in enumerate(pairs):
        names[0, 8 * c : 8 * c + 8] = a
        names[1, 8 * c : 8 * c + 8] = b
    return jnp.asarray(names)


def pair_table(pairs, rows):
    table = np.zeros((2, rows // 8), np.int32)
    table[:, : len(pairs)] = np.array(pairs, np.int32).T
    return jnp.asarray(table)


def local(slc_stack, offsets, kernels, partner, inverse, rate_weights, owners, map_cell):
    date_count, width = slc_stack.shape[1], slc_stack.shape[3]
    groups, strips = lax.axis_size("date"), lax.axis_size("col")
    group, strip = lax.axis_index("date"), lax.axis_index("col")
    rows = [
        jnp.transpose(kernels, (1, 2, 0)).reshape(2 * TAPS, DATES),
        offsets.T.astype(F32),
        jnp.pad(partner.reshape(1, -1).astype(F32), ((0, 0), (0, DATES - partner.shape[0]))),
    ]
    facts = jnp.stack([group * date_count, group % 2, strip % 2, group]).astype(F32)
    rows.append(jnp.pad(facts.reshape(1, -1), ((0, 4), (0, DATES - 4))))
    table, at = jnp.zeros((24, DATES), F32), 0
    for part in rows:
        table = table + jnp.pad(part, ((at, 24 - at - part.shape[0]), (0, 0)))
        at += part.shape[0]

    own = lax.reduce_precision(slc_stack, 8, 7)
    tile0, tile1 = call(
        pack_kernel,
        ((strip % 2).astype(jnp.int32).reshape(1),),
        (own,),
        [((2, ROWS, LANES), BF16)] * 2,
        [pltpu.VMEM((2, 2, ROWS, LANES), F32)],
    )
    near = lax.ppermute(tile0, "col", swaps(strips, 0))
    far = lax.ppermute(tile1, "col", swaps(strips, 1))
    scratch_z = pltpu.VMEM((2, width // LANES + 1, ROWS, LANES), F32)
    edge0, edge1 = call(
        edge_kernel,
        (table,),
        (own, near, far, table),
        [((256, width), BF16)] * 2,
        [scratch_z],
    )
    got0 = lax.ppermute(edge0, "date", swaps(groups, 0))
    got1 = lax.ppermute(edge1, "date", swaps(groups, 1))
    inner_rows = 8 * (len(INNER) + 5)
    outer_rows = 8 * (len(CROSS) + len(BEFORE) + 3)
    outer_pairs = CROSS + [(a + 6, b - 12) for a, b in BEFORE]
    phase, power, ys, weight = call(
        inner_kernel,
        (table, pair_table(INNER, inner_rows)),
        (
            own, near, far, table, pair_names(INNER, inner_rows), inverse,
            owners.reshape(1, -1), map_cell,
        ),
        [
            ((PAIR_ROWS, 256), F32),
            ((96, 256), F32),
            ((12, 2, ROWS, width), F32),
            ((DATES, groups * PAIR_ROWS), BF16),
        ],
        [
            scratch_z,
            pltpu.VMEM((96, width), F32),
            pltpu.VMEM((inner_rows, width), F32),
            pltpu.VMEM((inner_rows, 256), F32),
            pltpu.VMEM((inverse.shape[1], groups * PAIR_ROWS), BF16),
        ],
    )
    (sent,) = call(
        outer_kernel,
        (table, pair_table(outer_pairs, outer_rows)),
        (got0, got1, ys, power, phase, table, pair_names(CROSS + BEFORE, outer_rows)),
        [((groups, PAIR_ROWS, 256), BF16)],
        [
            pltpu.VMEM((6, 2, ROWS, width), F32),
            pltpu.VMEM((48, width), F32),
            pltpu.VMEM((outer_rows, width), F32),
            pltpu.VMEM((outer_rows, 256), F32),
            pltpu.VMEM((144, 256), F32),
        ],
    )
    phases = lax.all_to_all(sent, "date", 0, 0, tiled=True)
    (routed,) = call(series_kernel, (table,), (phases, weight), [((8 * strips, 256), BF16)])
    parts = lax.all_to_all(routed.reshape(strips, 8, 256), "col", 0, 0, tiled=True)
    rates = jnp.pad(rate_weights.reshape(1, -1), ((0, 0), (0, 1)))
    (mean,) = call(final_kernel, (), (parts, rates), [((8, DATES), F32)])
    return mean.reshape(1, 8, DATES)


def solution(mesh):
    in_specs = (
        P(None, "date", None, "col"),
        P(),
        P(),
        P("date"),
        P(),
        P(),
        P("col", "date", None),
        P("col", "date"),
    )
    out_specs = P("col", "date", None)
    return jax.shard_map(local, mesh=mesh, in_specs=in_specs, out_specs=out_specs, check_vma=False)
```

```python
import functools

import jax
import jax.numpy as jnp
import numpy as np
from jax import lax
from jax.experimental import pallas as pl
from jax.experimental.pallas import tpu as pltpu
from jax.sharding import PartitionSpec as P

PER_DATE = 3
SPAN = 6
HALF = 3
ROW_BLOCK = 20
TAPS = 8
HALO = 8
LOOK_AZ = 5
LOOK_RG = 20
LROWS = 8
LANES = 128
ROWS = 40
DATES = 192
EXTRA = 9
PAIR_ROWS = 48
F32 = jnp.float32
BF16 = jnp.bfloat16
VMEM_BYTES = 24 * 1024 * 1024

INNER = [(a, a + s) for a in range(6) for s in range(1, 7)]
INNER += [(a, b) for a in range(6, 11) for b in range(a + 1, 12)]
CROSS = [(a, b) for b in range(12, 15) for a in range(b - 6, 12)]
BEFORE = [(a, b) for b in range(15, 18) for a in range(b - 6, 12)]


def iota(shape, dim):
    return lax.broadcasted_iota(jnp.int32, shape, dim)


def fact(table, n):
    return table[2 * TAPS + 3, n].astype(jnp.int32)


def partner_row(table, lines):
    return lines[2 * TAPS + 2 : 2 * TAPS + 3, 0:36] - table[2 * TAPS + 3, 0]


def tap_weights(table, at, weights):
    lane, row = iota((16, LANES), 1), iota((16, LANES), 0)
    for b in range(2):
        start = LANES + 4 - table[2 * TAPS + b, at].astype(jnp.int32)
        line = jnp.zeros((8, LANES), F32)
        for t in range(TAPS):
            here = iota((8, LANES), 1) == lax.rem(start - t, LANES)
            line = jnp.where(here, table[TAPS * b + t, at], line)
        cols = slice(LANES * b, LANES * b + LANES)
        for m in range(0, LANES, 16):
            both = jnp.concatenate(
                [pltpu.roll(line, m + 8 * i, 1, stride=1, stride_axis=0) for i in range(2)], axis=0
            )
            apart = lane - row - m
            near = (apart < 64) & (apart > -64)
            for at_row, tile in ((m, jnp.where(near, both, 0.0)), (LANES + m, jnp.where(near, 0.0, both))):
                high = tile.astype(BF16)
                weights[at_row : at_row + 16, cols] = high
                weights[256 + at_row : 272 + at_row, cols] = (tile - high.astype(F32)).astype(BF16)


def resample(own, near, far, table, dates, lhs, weights, zs):
    is_odd = fact(table, 2) == 1
    count = own.shape[-1] // LANES
    lane = iota((ROWS, LANES), 1)
    for s, date in enumerate(dates):
        tap_weights(table, jnp.clip(fact(table, 0) + date, 0, DATES - 1), weights.at[s])
    for s, date in enumerate(dates):
        for part in range(2):
            tile_a, tile_b = near[part].astype(F32), far[part].astype(F32)
            left = pltpu.roll(jnp.where(is_odd, tile_a, tile_b), LANES - HALO - HALO * date, 1)
            right = pltpu.roll(
                jnp.where(is_odd, tile_b, tile_a), lax.rem(LANES - HALO * date, LANES), 1
            )
            line = own[part, date].astype(F32)
            tiles = [left] + [line[:, LANES * j : LANES * (j + 1)] for j in range(count)] + [right]
            for j in range(count):
                rows = slice(ROWS * (count * part + j), ROWS * (count * part + j + 1))
                lhs[s, rows, 0:LANES] = own[part, date, :, LANES * j : LANES * (j + 1)]
                lhs[s, rows, LANES : 2 * LANES] = jnp.where(
                    lane < 64, tiles[j + 2], tiles[j]
                ).astype(BF16)
    row = iota((8, LANES), 0)
    outs = []
    for s in range(len(dates)):
        taken = lhs[s]
        outs.append(
            jnp.dot(
                jnp.concatenate([taken, taken], axis=1), weights[s], preferred_element_type=F32
            )
        )
    for s, out in enumerate(outs):
        for part in range(2):
            for j in range(count):
                tile = out[ROWS * (count * part + j) : ROWS * (count * part + j + 1)]
                first, second = tile[:, :LANES], tile[:, LANES:]
                zs[s, part, j, 0:16, :] = first[:16]
                zs[s, part, j, 16:24, :] = jnp.where(row < 4, first[16:24], second[16:24])
                zs[s, part, j, 24:40, :] = second[24:]


def slabs(zs, s):
    for part in range(2):
        for k in range(LOOK_AZ):
            for j in range(zs.shape[2]):
                tile = zs[s, part, j, pl.ds(k, LROWS, stride=LOOK_AZ), :].astype(BF16)
                yield part, k, slice(LANES * j, LANES * (j + 1)), tile


def column(row, rows, offset):
    wide = row.shape[1]
    at = iota((rows, wide), 1) == iota((rows, wide), 0) + offset
    return jnp.sum(jnp.where(at, row, 0.0), axis=1, keepdims=True)


def pack_kernel(odd, own, out0, out1, acc):
    far = own.shape[3] - LANES
    even = odd[0] == 0
    acc[...] = jnp.zeros_like(acc)

    def one(d, _):
        for part in range(2):
            head = own[part, d, :, 0:LANES].astype(F32)
            tail = own[part, d, :, far : far + LANES].astype(F32)
            head = pltpu.roll(head, HALO * d, 1)
            tail = pltpu.roll(tail, HALO * d + HALO, 1)
            here = iota(head.shape, 1) // HALO == d
            for n, tile in enumerate((jnp.where(even, tail, head), jnp.where(even, head, tail))):
                acc[n, part] = jnp.where(here, tile, acc[n, part])
        return 0

    lax.fori_loop(0, own.shape[1], one, 0)
    out0[...] = acc[0].astype(BF16)
    out1[...] = acc[1].astype(BF16)


def edge_kernel(table, own, near, far, lines, out0, out1, lhs, weights, zs):
    odd_date = fact(table, 1)
    local = column(partner_row(table, lines), 16, 36 - EXTRA)
    wide = out0.shape[1]
    told = jnp.broadcast_to(local, (16, wide)).astype(BF16)
    out0[240:256, :] = told
    out1[240:256, :] = told

    def one(i, _):
        dates = (9 - 9 * odd_date + i, 9 * odd_date + i)
        resample(own, near, far, table, dates, lhs, weights, zs)
        for s, out in enumerate((out0, out1)):
            for part, k, cols, tile in slabs(zs, s):
                out[pl.ds(pl.multiple_of(i * 80 + part * 40 + k * 8, 8), 8), cols] = tile
        return 0

    lax.fori_loop(0, HALF, one, 0)


def window_sum(values, matrix):
    high = values.astype(BF16)
    low = (values - high.astype(F32)).astype(BF16)
    both = jnp.dot(
        jnp.concatenate([high, low], axis=0), matrix[...], preferred_element_type=F32
    )
    return both[: values.shape[0]] + both[values.shape[0] :]


def cross_sum(first, second):
    total = None
    for k in range(LOOK_AZ):
        re1, im1 = first(0, k), first(1, k)
        re2, im2 = second(0, k), second(1, k)
        term = im1 * re2 - re1 * im2
        total = term if total is None else total + term
    return total


def power_sum(date):
    total = None
    for k in range(LOOK_AZ):
        re, im = date(0, k), date(1, k)
        term = re * re + im * im
        total = term if total is None else total + term
    return total


def phase_of(cross, power_a, power_b, mask):
    scale = 1.0 / (LOOK_AZ * LOOK_RG)
    product = (power_a * scale) * (power_b * scale) + 1e-06
    return jnp.where(mask, (cross * scale) * lax.rsqrt(product), 0.0)


def choose(names, have_a, have_b, reverse):
    a, b = names[0:1, :], names[1:2, :]
    take = ((have_a == a) & (have_b == b)).astype(F32)
    if reverse:
        take = take - ((have_a == b) & (have_b == a)).astype(F32)
    return take.astype(BF16)


def phases_of(pairs, count, pm, powers):
    mask = iota((8, 256), 1) // 32 == iota((8, 256), 0)

    def one(n, _):
        done = []
        for u in range(8):
            c = 8 * n + u
            rows = pl.ds(pl.multiple_of(c * 8, 8), 8)
            row_a = pl.ds(pl.multiple_of(pairs[0, c] * 8, 8), 8)
            row_b = pl.ds(pl.multiple_of(pairs[1, c] * 8, 8), 8)
            done.append(phase_of(pm[rows, :], powers[row_a, :], powers[row_b, :], mask))
        pm[pl.ds(pl.multiple_of(n * 64, 64), 64), :] = jnp.concatenate(done, axis=0)
        return 0

    lax.fori_loop(0, count // 8, one, 0)


def spread_dates(even, odd, parity, dates, first, second):
    def one(n, _):
        at = pl.multiple_of(n * 80, 16)
        one, two = even[pl.ds(at, 80), :].astype(F32), odd[pl.ds(at, 80), :].astype(F32)
        low, high = jnp.where(parity == 1, two, one), jnp.where(parity == 1, one, two)
        dates[n + first, 0], dates[n + first, 1] = low[:40], low[40:]
        dates[n + second, 0], dates[n + second, 1] = high[:40], high[40:]
        return 0

    lax.fori_loop(0, HALF, one, 0)


def inner_kernel(
    table, pairs, own, near, far, edge0, edge1, lines, matrix, names, inverse, owners, cells,
    phase_out, power_out, ys, weight_out,
    lhs, weights, zs, ps, ss, pm, gather,
):
    width = own.shape[-1]

    def one_date(n, _):
        dates = (n + 3, n + 6)
        resample(own, near, far, table, dates, lhs, weights, zs)
        for s, d in enumerate(dates):
            for part, k, cols, tile in slabs(zs, s):
                ys[d, part, 8 * k : 8 * k + 8, cols] = tile.astype(F32)
        return 0

    lax.fori_loop(0, HALF, one_date, 0)
    spread_dates(edge1, edge0, fact(table, 1), ys, 0, 9)

    def one_power(d, _):
        ps[pl.ds(pl.multiple_of(d * 8, 8), 8), :] = power_sum(reader(d))
        return 0

    def reader(d):
        return lambda part, k: ys[d, part, 8 * k : 8 * k + 8, :]

    lax.fori_loop(0, 12, one_power, 0)

    def one_pair(c, _):
        at = pl.multiple_of(c * 8, 8)
        ss[pl.ds(at, 8), :] = cross_sum(reader(pairs[0, c]), reader(pairs[1, c]))
        return 0

    total = ss.shape[0] // 8
    lax.fori_loop(0, total, one_pair, 0)
    power_out[...] = window_sum(ps[...], matrix)
    block = ss.shape[0] // 2

    def one_block(n, _):
        rows = pl.ds(pl.multiple_of(n * block, 8), block)
        pm[rows, :] = window_sum(ss[rows, :], matrix)
        return 0

    lax.fori_loop(0, 2, one_block, 0)
    phases_of(pairs, total, pm, power_out)
    local = column(partner_row(table, lines), PAIR_ROWS, 0)
    row = iota((PAIR_ROWS, 1), 0)
    have_a = jnp.where(row < 36, row // PER_DATE, -9).astype(F32)
    take = choose(names, have_a, local, True)

    spots = iota((1, weight_out.shape[1]), 1)
    group, k = spots // PAIR_ROWS, spots % PAIR_ROWS
    target = jnp.where(k < 36, 36 * group + k, jnp.where(k < 45, 36 * group + k - 45, -1))

    def one_rows(n, _):
        at = pl.multiple_of(n * 16, 16)
        gather[pl.ds(at, 16), :] = (iota((16, gather.shape[1]), 0) + at == target).astype(BF16)
        return 0

    lax.fori_loop(0, gather.shape[0] // 16, one_rows, 0)
    weight_out[0:191, :] = jnp.dot(
        inverse[...], gather[...], preferred_element_type=F32
    ).astype(BF16)
    weight_out[191:192, :] = jnp.zeros((1, weight_out.shape[1]), BF16)

    n = owners.shape[1]
    spread = (iota((n, 256), 1) == iota((n, 256), 0) + n * fact(table, 3)).astype(BF16)
    codes = jnp.concatenate([owners[...], cells[...]], axis=0).astype(F32).astype(BF16)
    placed = jnp.dot(codes, spread, preferred_element_type=F32)
    lines = iota((PAIR_ROWS, 256), 0)
    phases = jnp.dot(take, pm[...].astype(BF16), preferred_element_type=F32)
    phases = jnp.where(lines == 46, placed[0:1, :], phases)
    phase_out[...] = jnp.where(lines == 47, placed[1:2, :], phases)


def outer_kernel(
    table, pairs, got0, got1, ys, power, phase, lines, matrix, names, out, rs, ps, ss, pm, pw
):
    width = got0.shape[1]
    odd_date = fact(table, 1)

    spread_dates(got0, got1, odd_date, rs, 0, 3)

    def here(d):
        return lambda part, k: ys[d, part, 8 * k : 8 * k + 8, :]

    def there(d):
        return lambda part, k: rs[d, part, 8 * k : 8 * k + 8, :]

    def one_power(n, _):
        ps[pl.ds(pl.multiple_of(n * 8, 8), 8), :] = power_sum(there(n))
        return 0

    lax.fori_loop(0, 2 * HALF, one_power, 0)

    def one_after(c, _):
        at = pl.multiple_of(c * 8, 8)
        ss[pl.ds(at, 8), :] = cross_sum(here(pairs[0, c]), there(pairs[1, c] - 12))
        return 0

    def one_before(c, _):
        at = pl.multiple_of(c * 8, 8)
        ss[pl.ds(at, 8), :] = cross_sum(there(pairs[0, c] - 12), here(pairs[1, c]))
        return 0

    total = ss.shape[0] // 8
    lax.fori_loop(0, len(CROSS), one_after, 0)
    lax.fori_loop(len(CROSS), len(CROSS) + len(BEFORE), one_before, 0)
    last = 8 * (len(CROSS) + len(BEFORE))
    ss[last:, :] = jnp.zeros_like(ss[last:, :])
    pw[0:96, :] = power[...]
    pw[96:144, :] = window_sum(ps[...], matrix)
    pm[...] = window_sum(ss[...], matrix)
    phases_of(pairs, total, pm, pw)
    local = column(partner_row(table, lines), PAIR_ROWS, 0)
    row = iota((PAIR_ROWS, 1), 0)
    told = jnp.where(odd_date == 1, got0[240:256, 0:LANES], got1[240:256, 0:LANES]).astype(F32)
    told = jnp.max(told, axis=1, keepdims=True)
    spread = (iota((PAIR_ROWS, 16), 0) - 36 == iota((PAIR_ROWS, 16), 1)).astype(BF16)
    moved = jnp.dot(
        spread, jnp.broadcast_to(told, (16, LANES)).astype(BF16), preferred_element_type=F32
    )[:, 0:1]
    mine = jnp.where(row < 36, jnp.where(local < 15, local, -5.0), jnp.where(row < 45, moved, -5.0))
    mine = jnp.where((row >= 36) & (mine < 15), -5.0, mine)
    have_a = jnp.where(row < 36, row // PER_DATE, 9 + (row - 36) // PER_DATE).astype(F32)
    take = choose(names, have_a, mine, False)
    total = phase[...] + jnp.dot(take, pm[...].astype(BF16), preferred_element_type=F32)
    for g in range(out.shape[0]):
        out[g] = total.astype(BF16)


def series_kernel(table, got, weight, out):
    stack = jnp.concatenate([got[g] for g in range(got.shape[0])], axis=0)
    series = jnp.dot(weight[...], stack, preferred_element_type=F32)
    wide = series.shape[1]
    rows = jnp.where(iota(series.shape, 0) == 191, 1.0, series)
    rows = jnp.concatenate([rows, jnp.zeros((64, wide), F32)], axis=0).astype(BF16)
    codes = got[0, 40:48, :].astype(F32)
    for g in range(1, got.shape[0]):
        codes = codes + got[g, 40:48, :].astype(F32)
    owner, cell = codes[6:7, :], codes[7:8, :]
    base = table[2 * TAPS + 3, 3] * 8.0
    mine = (cell >= base) & (cell < base + 8)
    target = jnp.where(mine, owner * 8 + cell - base, -1.0).astype(jnp.int32)
    select = (iota((out.shape[0], wide), 0) == target).astype(BF16)
    out[...] = lax.dot_general(
        select, rows, (((1,), (1,)), ((), ())), preferred_element_type=F32
    ).astype(BF16)


def final_kernel(got, rates, out):
    total = got[0].astype(F32)
    for g in range(1, got.shape[0]):
        total = total + got[g].astype(F32)
    total = total[:, 0:DATES]
    lane = iota(total.shape, 1)
    counts = jnp.sum(jnp.where(lane == DATES - 1, total, 0.0), axis=1, keepdims=True)
    velocity = jnp.sum(total * rates[...], axis=1, keepdims=True)
    total = jnp.where(lane == DATES - 1, velocity, total)
    out[...] = total / jnp.maximum(counts, 1.0)


SMEM = pl.BlockSpec(memory_space=pltpu.SMEM)
VMEM = pl.BlockSpec(memory_space=pltpu.VMEM)


def call(kernel, smem, vmem, outs, scratch=()):
    return pl.pallas_call(
        kernel,
        in_specs=[SMEM] * len(smem) + [VMEM] * len(vmem),
        out_specs=[VMEM] * len(outs),
        out_shape=[jax.ShapeDtypeStruct(s, t) for s, t in outs],
        scratch_shapes=list(scratch),
        compiler_params=pltpu.CompilerParams(vmem_limit_bytes=VMEM_BYTES),
    )(*smem, *vmem)


def swaps(count, start):
    return [p for i in range(start, count - 1, 2) for p in ((i, i + 1), (i + 1, i))]


def pair_names(pairs, rows):
    names = np.full((2, rows), -20.0, np.float32)
    for c, (a, b) in enumerate(pairs):
        names[0, 8 * c : 8 * c + 8] = a
        names[1, 8 * c : 8 * c + 8] = b
    return jnp.asarray(names)


def pair_table(pairs, rows):
    table = np.zeros((2, rows // 8), np.int32)
    table[:, : len(pairs)] = np.array(pairs, np.int32).T
    return jnp.asarray(table)


def local(slc_stack, offsets, kernels, partner, inverse, rate_weights, owners, map_cell):
    date_count, width = slc_stack.shape[1], slc_stack.shape[3]
    groups, strips = lax.axis_size("date"), lax.axis_size("col")
    group, strip = lax.axis_index("date"), lax.axis_index("col")
    rows = [
        jnp.transpose(kernels, (1, 2, 0)).reshape(2 * TAPS, DATES),
        offsets.T.astype(F32),
        jnp.pad(partner.reshape(1, -1).astype(F32), ((0, 0), (0, DATES - partner.shape[0]))),
    ]
    facts = jnp.stack([group * date_count, group % 2, strip % 2, group]).astype(F32)
    rows.append(jnp.pad(facts.reshape(1, -1), ((0, 4), (0, DATES - 4))))
    table, at = jnp.zeros((24, DATES), F32), 0
    for part in rows:
        table = table + jnp.pad(part, ((at, 24 - at - part.shape[0]), (0, 0)))
        at += part.shape[0]

    own = lax.reduce_precision(slc_stack, 8, 7)
    tile0, tile1 = call(
        pack_kernel,
        ((strip % 2).astype(jnp.int32).reshape(1),),
        (own,),
        [((2, ROWS, LANES), BF16)] * 2,
        [pltpu.VMEM((2, 2, ROWS, LANES), F32)],
    )
    near = lax.ppermute(tile0, "col", swaps(strips, 0))
    far = lax.ppermute(tile1, "col", swaps(strips, 1))
    scratch = [
        pltpu.VMEM((2, 2 * ROWS * width // LANES, 2 * LANES), BF16),
        pltpu.VMEM((2, 4 * LANES, 2 * LANES), BF16),
        pltpu.VMEM((2, 2, width // LANES, ROWS, LANES), F32),
    ]
    edge0, edge1 = call(
        edge_kernel,
        (table,),
        (own, near, far, table),
        [((256, width), BF16)] * 2,
        scratch,
    )
    got0 = lax.ppermute(edge0, "date", swaps(groups, 0))
    got1 = lax.ppermute(edge1, "date", swaps(groups, 1))
    window = np.arange(width)[:, None] // LOOK_RG == np.arange(256)[None, :] % (width // LOOK_RG)
    matrix = jnp.asarray(window.astype(np.float32)).astype(BF16)
    inner_rows = 8 * (len(INNER) + 5)
    outer_rows = 8 * (len(CROSS) + len(BEFORE) + 3)
    outer_pairs = CROSS + [(a + 6, b - 12) for a, b in BEFORE]
    phase, power, ys, weight = call(
        inner_kernel,
        (table, pair_table(INNER, inner_rows)),
        (
            own, near, far, edge0, edge1, table, matrix, pair_names(INNER, inner_rows), inverse,
            owners.reshape(1, -1), map_cell,
        ),
        [
            ((PAIR_ROWS, 256), F32),
            ((96, 256), F32),
            ((12, 2, ROWS, width), F32),
            ((DATES, groups * PAIR_ROWS), BF16),
        ],
        scratch
        + [
            pltpu.VMEM((96, width), F32),
            pltpu.VMEM((inner_rows, width), F32),
            pltpu.VMEM((inner_rows, 256), F32),
            pltpu.VMEM((inverse.shape[1], groups * PAIR_ROWS), BF16),
        ],
    )
    (sent,) = call(
        outer_kernel,
        (table, pair_table(outer_pairs, outer_rows)),
        (got0, got1, ys, power, phase, table, matrix, pair_names(CROSS + BEFORE, outer_rows)),
        [((groups, PAIR_ROWS, 256), BF16)],
        [
            pltpu.VMEM((6, 2, ROWS, width), F32),
            pltpu.VMEM((48, width), F32),
            pltpu.VMEM((outer_rows, width), F32),
            pltpu.VMEM((outer_rows, 256), F32),
            pltpu.VMEM((144, 256), F32),
        ],
    )
    phases = lax.all_to_all(sent, "date", 0, 0, tiled=True)
    (routed,) = call(series_kernel, (table,), (phases, weight), [((8 * strips, 256), BF16)])
    parts = lax.all_to_all(routed.reshape(strips, 8, 256), "col", 0, 0, tiled=True)
    rates = jnp.pad(rate_weights.reshape(1, -1), ((0, 0), (0, 1)))
    (mean,) = call(final_kernel, (), (parts, rates), [((8, DATES), F32)])
    return mean.reshape(1, 8, DATES)


def solution(mesh):
    in_specs = (
        P(None, "date", None, "col"),
        P(),
        P(),
        P("date"),
        P(),
        P(),
        P("col", "date", None),
        P("col", "date"),
    )
    out_specs = P("col", "date", None)
    return jax.shard_map(local, mesh=mesh, in_specs=in_specs, out_specs=out_specs, check_vma=False)
```

```python
import functools

import jax
import jax.numpy as jnp
import numpy as np
from jax import lax
from jax.experimental import pallas as pl
from jax.experimental.pallas import tpu as pltpu
from jax.sharding import PartitionSpec as P

PER_DATE = 3
SPAN = 6
HALF = 3
ROW_BLOCK = 20
TAPS = 8
HALO = 8
LOOK_AZ = 5
LOOK_RG = 20
LROWS = 8
LANES = 128
ROWS = 40
DATES = 192
EXTRA = 9
PAIR_ROWS = 48
F32 = jnp.float32
BF16 = jnp.bfloat16
VMEM_BYTES = 24 * 1024 * 1024

INNER = [(a, a + s) for a in range(6) for s in range(1, 7)]
INNER += [(a, b) for a in range(6, 11) for b in range(a + 1, 12)]
CROSS = [(a, b) for b in range(12, 15) for a in range(b - 6, 12)]
BEFORE = [(a, b) for b in range(15, 18) for a in range(b - 6, 12)]


def iota(shape, dim):
    return lax.broadcasted_iota(jnp.int32, shape, dim)


def fact(table, n):
    return table[2 * TAPS + 3, n].astype(jnp.int32)


def partner_row(table, lines):
    return lines[2 * TAPS + 2 : 2 * TAPS + 3, 0:36] - table[2 * TAPS + 3, 0]


def tap_weights(table, at, weights):
    lane, row = iota((16, LANES), 1), iota((16, LANES), 0)
    for b in range(2):
        start = LANES + 4 - table[2 * TAPS + b, at].astype(jnp.int32)
        line = jnp.zeros((8, LANES), F32)
        for t in range(TAPS):
            here = iota((8, LANES), 1) == lax.rem(start - t, LANES)
            line = jnp.where(here, table[TAPS * b + t, at], line)
        cols = slice(LANES * b, LANES * b + LANES)
        for m in range(0, LANES, 16):
            both = jnp.concatenate(
                [pltpu.roll(line, m + 8 * i, 1, stride=1, stride_axis=0) for i in range(2)], axis=0
            )
            apart = lane - row - m
            near = (apart < 64) & (apart > -64)
            for at_row, tile in ((m, jnp.where(near, both, 0.0)), (LANES + m, jnp.where(near, 0.0, both))):
                high = tile.astype(BF16)
                weights[at_row : at_row + 16, cols] = high
                weights[256 + at_row : 272 + at_row, cols] = (tile - high.astype(F32)).astype(BF16)


def resample(own, near, far, table, dates, lhs, weights, zs):
    is_odd = fact(table, 2) == 1
    count = own.shape[-1] // LANES
    lane = iota((ROWS, LANES), 1)
    for s, date in enumerate(dates):
        tap_weights(table, jnp.clip(fact(table, 0) + date, 0, DATES - 1), weights.at[s])
    for s, date in enumerate(dates):
        for part in range(2):
            tile_a, tile_b = near[part].astype(F32), far[part].astype(F32)
            left = pltpu.roll(jnp.where(is_odd, tile_a, tile_b), LANES - HALO - HALO * date, 1)
            right = pltpu.roll(
                jnp.where(is_odd, tile_b, tile_a), lax.rem(LANES - HALO * date, LANES), 1
            )
            line = own[part, date].astype(F32)
            tiles = [left] + [line[:, LANES * j : LANES * (j + 1)] for j in range(count)] + [right]
            for j in range(count):
                rows = slice(ROWS * (count * part + j), ROWS * (count * part + j + 1))
                lhs[s, rows, 0:LANES] = own[part, date, :, LANES * j : LANES * (j + 1)]
                lhs[s, rows, LANES : 2 * LANES] = jnp.where(
                    lane < 64, tiles[j + 2], tiles[j]
                ).astype(BF16)
    row = iota((8, LANES), 0)
    outs = []
    for s in range(len(dates)):
        taken = lhs[s]
        outs.append(
            jnp.dot(
                jnp.concatenate([taken, taken], axis=1), weights[s], preferred_element_type=F32
            )
        )
    for s, out in enumerate(outs):
        for part in range(2):
            for j in range(count):
                tile = out[ROWS * (count * part + j) : ROWS * (count * part + j + 1)]
                first, second = tile[:, :LANES], tile[:, LANES:]
                zs[s, part, j, 0:16, :] = first[:16]
                zs[s, part, j, 16:24, :] = jnp.where(row < 4, first[16:24], second[16:24])
                zs[s, part, j, 24:40, :] = second[24:]


def slabs(zs, s):
    for part in range(2):
        for k in range(LOOK_AZ):
            for j in range(zs.shape[2]):
                tile = zs[s, part, j, pl.ds(k, LROWS, stride=LOOK_AZ), :].astype(BF16)
                yield part, k, slice(LANES * j, LANES * (j + 1)), tile


def column(row, rows, offset):
    wide = row.shape[1]
    at = iota((rows, wide), 1) == iota((rows, wide), 0) + offset
    return jnp.sum(jnp.where(at, row, 0.0), axis=1, keepdims=True)


def pack_kernel(odd, own, out0, out1, ends, acc, sems):
    far = own.shape[3] - LANES
    even = odd[0] == 0
    copies = [
        pltpu.make_async_copy(own.at[:, :, :, at : at + LANES], ends.at[n], sems.at[n])
        for n, at in enumerate((0, far))
    ]
    for copy in copies:
        copy.start()
    acc[...] = jnp.zeros_like(acc)
    for copy in copies:
        copy.wait()

    def one(d, _):
        for part in range(2):
            head = pltpu.roll(ends[0, part, d].astype(F32), HALO * d, 1)
            tail = pltpu.roll(ends[1, part, d].astype(F32), HALO * d + HALO, 1)
            here = iota(head.shape, 1) // HALO == d
            for n, tile in enumerate((jnp.where(even, tail, head), jnp.where(even, head, tail))):
                acc[n, part] = jnp.where(here, tile, acc[n, part])
        return 0

    lax.fori_loop(0, own.shape[1], one, 0)
    out0[...] = acc[0].astype(BF16)
    out1[...] = acc[1].astype(BF16)


def edge_kernel(table, own, near, far, lines, out0, out1, lhs, weights, zs):
    odd_date = fact(table, 1)
    local = column(partner_row(table, lines), 16, 36 - EXTRA)
    wide = out0.shape[1]
    told = jnp.broadcast_to(local, (16, wide)).astype(BF16)
    out0[240:256, :] = told
    out1[240:256, :] = told

    def one(i, _):
        dates = (9 - 9 * odd_date + i, 9 * odd_date + i)
        resample(own, near, far, table, dates, lhs, weights, zs)
        for s, out in enumerate((out0, out1)):
            for part, k, cols, tile in slabs(zs, s):
                out[pl.ds(pl.multiple_of(i * 80 + part * 40 + k * 8, 8), 8), cols] = tile
        return 0

    lax.fori_loop(0, HALF, one, 0)


def window_sum(values, matrix):
    high = values.astype(BF16)
    low = (values - high.astype(F32)).astype(BF16)
    both = jnp.dot(
        jnp.concatenate([high, low], axis=0), matrix[...], preferred_element_type=F32
    )
    return both[: values.shape[0]] + both[values.shape[0] :]


def cross_sum(first, second):
    total = None
    for k in range(LOOK_AZ):
        re1, im1 = first(0, k), first(1, k)
        re2, im2 = second(0, k), second(1, k)
        term = im1 * re2 - re1 * im2
        total = term if total is None else total + term
    return total


def power_sum(date):
    total = None
    for k in range(LOOK_AZ):
        re, im = date(0, k), date(1, k)
        term = re * re + im * im
        total = term if total is None else total + term
    return total


def phase_of(cross, power_a, power_b, mask):
    scale = 1.0 / (LOOK_AZ * LOOK_RG)
    product = (power_a * scale) * (power_b * scale) + 1e-06
    return jnp.where(mask, (cross * scale) * lax.rsqrt(product), 0.0)


def choose(names, have_a, have_b, reverse):
    a, b = names[0:1, :], names[1:2, :]
    take = ((have_a == a) & (have_b == b)).astype(F32)
    if reverse:
        take = take - ((have_a == b) & (have_b == a)).astype(F32)
    return take.astype(BF16)


def phases_of(pairs, count, pm, powers):
    mask = iota((8, 256), 1) // 32 == iota((8, 256), 0)

    def one(n, _):
        done = []
        for u in range(8):
            c = 8 * n + u
            rows = pl.ds(pl.multiple_of(c * 8, 8), 8)
            row_a = pl.ds(pl.multiple_of(pairs[0, c] * 8, 8), 8)
            row_b = pl.ds(pl.multiple_of(pairs[1, c] * 8, 8), 8)
            done.append(phase_of(pm[rows, :], powers[row_a, :], powers[row_b, :], mask))
        pm[pl.ds(pl.multiple_of(n * 64, 64), 64), :] = jnp.concatenate(done, axis=0)
        return 0

    lax.fori_loop(0, count // 8, one, 0)


def spread_dates(even, odd, parity, dates, first, second):
    def one(n, _):
        at = pl.multiple_of(n * 80, 16)
        one, two = even[pl.ds(at, 80), :].astype(F32), odd[pl.ds(at, 80), :].astype(F32)
        low, high = jnp.where(parity == 1, two, one), jnp.where(parity == 1, one, two)
        dates[n + first, 0], dates[n + first, 1] = low[:40], low[40:]
        dates[n + second, 0], dates[n + second, 1] = high[:40], high[40:]
        return 0

    lax.fori_loop(0, HALF, one, 0)


def inner_kernel(
    table, pairs, own, near, far, edge0, edge1, lines, matrix, names, inverse, owners, cells,
    phase_out, power_out, ys, weight_out,
    lhs, weights, zs, ps, ss, pm, gather,
):
    width = own.shape[-1]

    def one_date(n, _):
        dates = (n + 3, n + 6)
        resample(own, near, far, table, dates, lhs, weights, zs)
        for s, d in enumerate(dates):
            for part, k, cols, tile in slabs(zs, s):
                ys[d, part, 8 * k : 8 * k + 8, cols] = tile.astype(F32)
        return 0

    lax.fori_loop(0, HALF, one_date, 0)
    spread_dates(edge1, edge0, fact(table, 1), ys, 0, 9)

    def one_power(d, _):
        ps[pl.ds(pl.multiple_of(d * 8, 8), 8), :] = power_sum(reader(d))
        return 0

    def reader(d):
        return lambda part, k: ys[d, part, 8 * k : 8 * k + 8, :]

    lax.fori_loop(0, 12, one_power, 0)

    def one_pair(c, _):
        at = pl.multiple_of(c * 8, 8)
        ss[pl.ds(at, 8), :] = cross_sum(reader(pairs[0, c]), reader(pairs[1, c]))
        return 0

    total = ss.shape[0] // 8
    lax.fori_loop(0, total, one_pair, 0)
    power_out[...] = window_sum(ps[...], matrix)
    block = ss.shape[0] // 2

    def one_block(n, _):
        rows = pl.ds(pl.multiple_of(n * block, 8), block)
        pm[rows, :] = window_sum(ss[rows, :], matrix)
        return 0

    lax.fori_loop(0, 2, one_block, 0)
    phases_of(pairs, total, pm, power_out)
    local = column(partner_row(table, lines), PAIR_ROWS, 0)
    row = iota((PAIR_ROWS, 1), 0)
    have_a = jnp.where(row < 36, row // PER_DATE, -9).astype(F32)
    take = choose(names, have_a, local, True)

    spots = iota((1, weight_out.shape[1]), 1)
    group, k = spots // PAIR_ROWS, spots % PAIR_ROWS
    target = jnp.where(k < 36, 36 * group + k, jnp.where(k < 45, 36 * group + k - 45, -1))

    def one_rows(n, _):
        at = pl.multiple_of(n * 16, 16)
        gather[pl.ds(at, 16), :] = (iota((16, gather.shape[1]), 0) + at == target).astype(BF16)
        return 0

    lax.fori_loop(0, gather.shape[0] // 16, one_rows, 0)
    weight_out[0:191, :] = jnp.dot(
        inverse[...], gather[...], preferred_element_type=F32
    ).astype(BF16)
    weight_out[191:192, :] = jnp.zeros((1, weight_out.shape[1]), BF16)

    n = owners.shape[1]
    spread = (iota((n, 256), 1) == iota((n, 256), 0) + n * fact(table, 3)).astype(BF16)
    codes = jnp.concatenate([owners[...], cells[...]], axis=0).astype(F32).astype(BF16)
    placed = jnp.dot(codes, spread, preferred_element_type=F32)
    lines = iota((PAIR_ROWS, 256), 0)
    phases = jnp.dot(take, pm[...].astype(BF16), preferred_element_type=F32)
    phases = jnp.where(lines == 46, placed[0:1, :], phases)
    phase_out[...] = jnp.where(lines == 47, placed[1:2, :], phases)


def outer_kernel(
    table, pairs, got0, got1, ys, power, phase, lines, matrix, names, out, rs, ps, ss, pm, pw
):
    width = got0.shape[1]
    odd_date = fact(table, 1)

    spread_dates(got0, got1, odd_date, rs, 0, 3)

    def here(d):
        return lambda part, k: ys[d, part, 8 * k : 8 * k + 8, :]

    def there(d):
        return lambda part, k: rs[d, part, 8 * k : 8 * k + 8, :]

    def one_power(n, _):
        ps[pl.ds(pl.multiple_of(n * 8, 8), 8), :] = power_sum(there(n))
        return 0

    lax.fori_loop(0, 2 * HALF, one_power, 0)

    def one_after(c, _):
        at = pl.multiple_of(c * 8, 8)
        ss[pl.ds(at, 8), :] = cross_sum(here(pairs[0, c]), there(pairs[1, c] - 12))
        return 0

    def one_before(c, _):
        at = pl.multiple_of(c * 8, 8)
        ss[pl.ds(at, 8), :] = cross_sum(there(pairs[0, c] - 12), here(pairs[1, c]))
        return 0

    total = ss.shape[0] // 8
    lax.fori_loop(0, len(CROSS), one_after, 0)
    lax.fori_loop(len(CROSS), len(CROSS) + len(BEFORE), one_before, 0)
    last = 8 * (len(CROSS) + len(BEFORE))
    ss[last:, :] = jnp.zeros_like(ss[last:, :])
    pw[0:96, :] = power[...]
    pw[96:144, :] = window_sum(ps[...], matrix)
    pm[...] = window_sum(ss[...], matrix)
    phases_of(pairs, total, pm, pw)
    local = column(partner_row(table, lines), PAIR_ROWS, 0)
    row = iota((PAIR_ROWS, 1), 0)
    told = jnp.where(odd_date == 1, got0[240:256, 0:LANES], got1[240:256, 0:LANES]).astype(F32)
    told = jnp.max(told, axis=1, keepdims=True)
    spread = (iota((PAIR_ROWS, 16), 0) - 36 == iota((PAIR_ROWS, 16), 1)).astype(BF16)
    moved = jnp.dot(
        spread, jnp.broadcast_to(told, (16, LANES)).astype(BF16), preferred_element_type=F32
    )[:, 0:1]
    mine = jnp.where(row < 36, jnp.where(local < 15, local, -5.0), jnp.where(row < 45, moved, -5.0))
    mine = jnp.where((row >= 36) & (mine < 15), -5.0, mine)
    have_a = jnp.where(row < 36, row // PER_DATE, 9 + (row - 36) // PER_DATE).astype(F32)
    take = choose(names, have_a, mine, False)
    total = phase[...] + jnp.dot(take, pm[...].astype(BF16), preferred_element_type=F32)
    for g in range(out.shape[0]):
        out[g] = total.astype(BF16)


def series_kernel(table, got, weight, out):
    stack = jnp.concatenate([got[g] for g in range(got.shape[0])], axis=0)
    series = jnp.dot(weight[...], stack, preferred_element_type=F32)
    wide = series.shape[1]
    rows = jnp.where(iota(series.shape, 0) == 191, 1.0, series)
    rows = jnp.concatenate([rows, jnp.zeros((64, wide), F32)], axis=0).astype(BF16)
    codes = got[0, 40:48, :].astype(F32)
    for g in range(1, got.shape[0]):
        codes = codes + got[g, 40:48, :].astype(F32)
    owner, cell = codes[6:7, :], codes[7:8, :]
    base = table[2 * TAPS + 3, 3] * 8.0
    mine = (cell >= base) & (cell < base + 8)
    target = jnp.where(mine, owner * 8 + cell - base, -1.0).astype(jnp.int32)
    select = (iota((out.shape[0], wide), 0) == target).astype(BF16)
    out[...] = lax.dot_general(
        select, rows, (((1,), (1,)), ((), ())), preferred_element_type=F32
    ).astype(BF16)


def final_kernel(got, lines, out):
    total = got[0].astype(F32)
    for g in range(1, got.shape[0]):
        total = total + got[g].astype(F32)
    total = total[:, 0:DATES]
    lane = iota(total.shape, 1)
    counts = jnp.sum(jnp.where(lane == DATES - 1, total, 0.0), axis=1, keepdims=True)
    velocity = jnp.sum(total * lines[2 * TAPS + 4 : 2 * TAPS + 5, :], axis=1, keepdims=True)
    total = jnp.where(lane == DATES - 1, velocity, total)
    out[...] = total / jnp.maximum(counts, 1.0)


SMEM = pl.BlockSpec(memory_space=pltpu.SMEM)
VMEM = pl.BlockSpec(memory_space=pltpu.VMEM)


def call(kernel, smem, vmem, outs, scratch=()):
    return pl.pallas_call(
        kernel,
        in_specs=[SMEM] * len(smem) + [VMEM] * len(vmem),
        out_specs=[VMEM] * len(outs),
        out_shape=[jax.ShapeDtypeStruct(s, t) for s, t in outs],
        scratch_shapes=list(scratch),
        compiler_params=pltpu.CompilerParams(vmem_limit_bytes=VMEM_BYTES),
    )(*smem, *vmem)


def swaps(count, start):
    return [p for i in range(start, count - 1, 2) for p in ((i, i + 1), (i + 1, i))]


def pair_names(pairs, rows):
    names = np.full((2, rows), -20.0, np.float32)
    for c, (a, b) in enumerate(pairs):
        names[0, 8 * c : 8 * c + 8] = a
        names[1, 8 * c : 8 * c + 8] = b
    return jnp.asarray(names)


def pair_table(pairs, rows):
    table = np.zeros((2, rows // 8), np.int32)
    table[:, : len(pairs)] = np.array(pairs, np.int32).T
    return jnp.asarray(table)


def local(slc_stack, offsets, kernels, partner, inverse, rate_weights, owners, map_cell):
    date_count, width = slc_stack.shape[1], slc_stack.shape[3]
    groups, strips = lax.axis_size("date"), lax.axis_size("col")
    group, strip = lax.axis_index("date"), lax.axis_index("col")
    rows = [
        jnp.transpose(kernels, (1, 2, 0)).reshape(2 * TAPS, DATES),
        offsets.T.astype(F32),
        jnp.pad(partner.reshape(1, -1).astype(F32), ((0, 0), (0, DATES - partner.shape[0]))),
    ]
    facts = jnp.stack([group * date_count, group % 2, strip % 2, group]).astype(F32)
    rows.append(jnp.pad(facts.reshape(1, -1), ((0, 0), (0, DATES - 4))))
    rows.append(jnp.pad(rate_weights.reshape(1, -1), ((0, 0), (0, DATES - rate_weights.shape[0]))))
    table, at = jnp.zeros((24, DATES), F32), 0
    for part in rows:
        table = table + jnp.pad(part, ((at, 24 - at - part.shape[0]), (0, 0)))
        at += part.shape[0]

    tile = jax.ShapeDtypeStruct((2, ROWS, LANES), BF16)
    tile0, tile1 = pl.pallas_call(
        pack_kernel,
        in_specs=[SMEM, pl.BlockSpec(memory_space=pl.ANY)],
        out_specs=[VMEM] * 2,
        out_shape=[tile] * 2,
        scratch_shapes=[
            pltpu.VMEM((2,) + slc_stack.shape[:3] + (LANES,), BF16),
            pltpu.VMEM((2, 2, ROWS, LANES), F32),
            pltpu.SemaphoreType.DMA((2,)),
        ],
        compiler_params=pltpu.CompilerParams(vmem_limit_bytes=53 * 1024 * 1024),
    )((strip % 2).astype(jnp.int32).reshape(1), slc_stack)
    own = lax.reduce_precision(slc_stack, 8, 7)
    near = lax.ppermute(tile0, "col", swaps(strips, 0))
    far = lax.ppermute(tile1, "col", swaps(strips, 1))
    scratch = [
        pltpu.VMEM((2, 2 * ROWS * width // LANES, 2 * LANES), BF16),
        pltpu.VMEM((2, 4 * LANES, 2 * LANES), BF16),
        pltpu.VMEM((2, 2, width // LANES, ROWS, LANES), F32),
    ]
    edge0, edge1 = call(
        edge_kernel,
        (table,),
        (own, near, far, table),
        [((256, width), BF16)] * 2,
        scratch,
    )
    got0 = lax.ppermute(edge0, "date", swaps(groups, 0))
    got1 = lax.ppermute(edge1, "date", swaps(groups, 1))
    window = np.arange(width)[:, None] // LOOK_RG == np.arange(256)[None, :] % (width // LOOK_RG)
    matrix = jnp.asarray(window.astype(np.float32)).astype(BF16)
    inner_rows = 8 * (len(INNER) + 5)
    outer_rows = 8 * (len(CROSS) + len(BEFORE) + 3)
    outer_pairs = CROSS + [(a + 6, b - 12) for a, b in BEFORE]
    phase, power, ys, weight = call(
        inner_kernel,
        (table, pair_table(INNER, inner_rows)),
        (
            own, near, far, edge0, edge1, table, matrix, pair_names(INNER, inner_rows), inverse,
            owners.reshape(1, -1), map_cell,
        ),
        [
            ((PAIR_ROWS, 256), F32),
            ((96, 256), F32),
            ((12, 2, ROWS, width), F32),
            ((DATES, groups * PAIR_ROWS), BF16),
        ],
        scratch
        + [
            pltpu.VMEM((96, width), F32),
            pltpu.VMEM((inner_rows, width), F32),
            pltpu.VMEM((inner_rows, 256), F32),
            pltpu.VMEM((inverse.shape[1], groups * PAIR_ROWS), BF16),
        ],
    )
    (sent,) = call(
        outer_kernel,
        (table, pair_table(outer_pairs, outer_rows)),
        (got0, got1, ys, power, phase, table, matrix, pair_names(CROSS + BEFORE, outer_rows)),
        [((groups, PAIR_ROWS, 256), BF16)],
        [
            pltpu.VMEM((6, 2, ROWS, width), F32),
            pltpu.VMEM((48, width), F32),
            pltpu.VMEM((outer_rows, width), F32),
            pltpu.VMEM((outer_rows, 256), F32),
            pltpu.VMEM((144, 256), F32),
        ],
    )
    phases = lax.all_to_all(sent, "date", 0, 0, tiled=True)
    (routed,) = call(series_kernel, (table,), (phases, weight), [((8 * strips, 256), BF16)])
    parts = lax.all_to_all(routed.reshape(strips, 8, 256), "col", 0, 0, tiled=True)
    (mean,) = call(final_kernel, (), (parts, table), [((8, DATES), F32)])
    return mean.reshape(1, 8, DATES)


def solution(mesh):
    in_specs = (
        P(None, "date", None, "col"),
        P(),
        P(),
        P("date"),
        P(),
        P(),
        P("col", "date", None),
        P("col", "date"),
    )
    out_specs = P("col", "date", None)
    return jax.shard_map(local, mesh=mesh, in_specs=in_specs, out_specs=out_specs, check_vma=False)
```

```python
import functools

import jax
import jax.numpy as jnp
import numpy as np
from jax import lax
from jax.experimental import pallas as pl
from jax.experimental.pallas import tpu as pltpu
from jax.sharding import PartitionSpec as P

PER_DATE = 3
SPAN = 6
HALF = 3
ROW_BLOCK = 20
TAPS = 8
HALO = 8
LOOK_AZ = 5
LOOK_RG = 20
LROWS = 8
LANES = 128
ROWS = 40
DATES = 192
EXTRA = 9
FACTS = 20
PAIR_ROWS = 48
F32 = jnp.float32
BF16 = jnp.bfloat16
VMEM_BYTES = 24 * 1024 * 1024

INNER = [(a, a + s) for a in range(6) for s in range(1, 7)]
INNER += [(a, b) for a in range(6, 11) for b in range(a + 1, 12)]
CROSS = [(a, b) for b in range(12, 15) for a in range(b - 6, 12)]
BEFORE = [(a, b) for b in range(15, 18) for a in range(b - 6, 12)]


def iota(shape, dim):
    return lax.broadcasted_iota(jnp.int32, shape, dim)


def fact(table, n):
    return (table[0, n] if table.shape[0] == 1 else table[FACTS + n, 0]).astype(jnp.int32)


def partner_row(table, lines):
    return lines[18:19, 0:36] - fact(table, 0).astype(F32)


def tap_weights(table, at, weights):
    lane, row = iota((16, LANES), 1), iota((16, LANES), 0)
    for b in range(2):
        start = LANES + 4 - table[2 * TAPS + b, at].astype(jnp.int32)
        line = jnp.zeros((8, LANES), F32)
        for t in range(TAPS):
            here = iota((8, LANES), 1) == lax.rem(start - t, LANES)
            line = jnp.where(here, table[TAPS * b + t, at], line)
        cols = slice(LANES * b, LANES * b + LANES)
        for m in range(0, LANES, 16):
            both = jnp.concatenate(
                [pltpu.roll(line, m + 8 * i, 1, stride=1, stride_axis=0) for i in range(2)], axis=0
            )
            apart = lane - row - m
            near = (apart < 64) & (apart > -64)
            for at_row, tile in ((m, jnp.where(near, both, 0.0)), (LANES + m, jnp.where(near, 0.0, both))):
                high = tile.astype(BF16)
                weights[at_row : at_row + 16, cols] = high
                weights[256 + at_row : 272 + at_row, cols] = (tile - high.astype(F32)).astype(BF16)


def resample(own, near, far, table, dates, lhs, weights, zs):
    is_odd = fact(table, 2) == 1
    count = own.shape[-1] // LANES
    lane = iota((ROWS, LANES), 1)
    for s, date in enumerate(dates):
        tap_weights(table, date, weights.at[s])
    for s, date in enumerate(dates):
        for part in range(2):
            tile_a, tile_b = near[part].astype(F32), far[part].astype(F32)
            left = pltpu.roll(jnp.where(is_odd, tile_a, tile_b), LANES - HALO - HALO * date, 1)
            right = pltpu.roll(
                jnp.where(is_odd, tile_b, tile_a), lax.rem(LANES - HALO * date, LANES), 1
            )
            line = own[part, date].astype(F32)
            tiles = [left] + [line[:, LANES * j : LANES * (j + 1)] for j in range(count)] + [right]
            for j in range(count):
                rows = slice(ROWS * (count * part + j), ROWS * (count * part + j + 1))
                lhs[s, rows, 0:LANES] = own[part, date, :, LANES * j : LANES * (j + 1)]
                lhs[s, rows, LANES : 2 * LANES] = jnp.where(
                    lane < 64, tiles[j + 2], tiles[j]
                ).astype(BF16)
    row = iota((8, LANES), 0)
    outs = []
    for s in range(len(dates)):
        taken = lhs[s]
        outs.append(
            jnp.dot(
                jnp.concatenate([taken, taken], axis=1), weights[s], preferred_element_type=F32
            )
        )
    for s, out in enumerate(outs):
        for part in range(2):
            for j in range(count):
                tile = out[ROWS * (count * part + j) : ROWS * (count * part + j + 1)]
                first, second = tile[:, :LANES], tile[:, LANES:]
                zs[s, part, j, 0:16, :] = first[:16]
                zs[s, part, j, 16:24, :] = jnp.where(row < 4, first[16:24], second[16:24])
                zs[s, part, j, 24:40, :] = second[24:]


def slabs(zs, s):
    for part in range(2):
        for k in range(LOOK_AZ):
            for j in range(zs.shape[2]):
                tile = zs[s, part, j, pl.ds(k, LROWS, stride=LOOK_AZ), :].astype(BF16)
                yield part, k, slice(LANES * j, LANES * (j + 1)), tile


def column(row, rows, offset):
    wide = row.shape[1]
    at = iota((rows, wide), 1) == iota((rows, wide), 0) + offset
    return jnp.sum(jnp.where(at, row, 0.0), axis=1, keepdims=True)


def pack_kernel(odd, own, out0, out1, ends, acc, sems):
    far = own.shape[3] - LANES
    even = odd[0] == 0
    copies = [
        pltpu.make_async_copy(own.at[:, :, :, at : at + LANES], ends.at[n], sems.at[n])
        for n, at in enumerate((0, far))
    ]
    for copy in copies:
        copy.start()
    acc[...] = jnp.zeros_like(acc)
    for copy in copies:
        copy.wait()

    def one(d, _):
        for part in range(2):
            head = pltpu.roll(ends[0, part, d].astype(F32), HALO * d, 1)
            tail = pltpu.roll(ends[1, part, d].astype(F32), HALO * d + HALO, 1)
            here = iota(head.shape, 1) // HALO == d
            for n, tile in enumerate((jnp.where(even, tail, head), jnp.where(even, head, tail))):
                acc[n, part] = jnp.where(here, tile, acc[n, part])
        return 0

    lax.fori_loop(0, own.shape[1], one, 0)
    out0[...] = acc[0].astype(BF16)
    out1[...] = acc[1].astype(BF16)


def edge_kernel(table, own, near, far, lines, out0, out1, lhs, weights, zs):
    odd_date = fact(table, 1)
    local = column(partner_row(table, lines), 16, 36 - EXTRA)
    wide = out0.shape[1]
    told = jnp.broadcast_to(local, (16, wide)).astype(BF16)
    out0[240:256, :] = told
    out1[240:256, :] = told

    def one(i, _):
        dates = (9 - 9 * odd_date + i, 9 * odd_date + i)
        resample(own, near, far, table, dates, lhs, weights, zs)
        for s, out in enumerate((out0, out1)):
            for part, k, cols, tile in slabs(zs, s):
                out[pl.ds(pl.multiple_of(i * 80 + part * 40 + k * 8, 8), 8), cols] = tile
        return 0

    lax.fori_loop(0, HALF, one, 0)


def window_sum(values, matrix):
    high = values.astype(BF16)
    low = (values - high.astype(F32)).astype(BF16)
    both = jnp.dot(
        jnp.concatenate([high, low], axis=0), matrix[...], preferred_element_type=F32
    )
    return both[: values.shape[0]] + both[values.shape[0] :]


def cross_sum(first, second):
    total = None
    for k in range(LOOK_AZ):
        re1, im1 = first(0, k), first(1, k)
        re2, im2 = second(0, k), second(1, k)
        term = im1 * re2 - re1 * im2
        total = term if total is None else total + term
    return total


def power_sum(date):
    total = None
    for k in range(LOOK_AZ):
        re, im = date(0, k), date(1, k)
        term = re * re + im * im
        total = term if total is None else total + term
    return total


def phase_of(cross, power_a, power_b, mask):
    scale = 1.0 / (LOOK_AZ * LOOK_RG)
    product = (power_a * scale) * (power_b * scale) + 1e-06
    return jnp.where(mask, (cross * scale) * lax.rsqrt(product), 0.0)


def choose(names, have_a, have_b, reverse):
    a, b = names[0:1, :], names[1:2, :]
    take = ((have_a == a) & (have_b == b)).astype(F32)
    if reverse:
        take = take - ((have_a == b) & (have_b == a)).astype(F32)
    return take.astype(BF16)


def phases_of(pairs, count, pm, powers):
    mask = iota((8, 256), 1) // 32 == iota((8, 256), 0)

    def one(n, _):
        done = []
        for u in range(8):
            c = 8 * n + u
            rows = pl.ds(pl.multiple_of(c * 8, 8), 8)
            row_a = pl.ds(pl.multiple_of(pairs[0, c] * 8, 8), 8)
            row_b = pl.ds(pl.multiple_of(pairs[1, c] * 8, 8), 8)
            done.append(phase_of(pm[rows, :], powers[row_a, :], powers[row_b, :], mask))
        pm[pl.ds(pl.multiple_of(n * 64, 64), 64), :] = jnp.concatenate(done, axis=0)
        return 0

    lax.fori_loop(0, count // 8, one, 0)


def spread_dates(even, odd, parity, dates, first, second):
    def one(n, _):
        at = pl.multiple_of(n * 80, 16)
        one, two = even[pl.ds(at, 80), :].astype(F32), odd[pl.ds(at, 80), :].astype(F32)
        low, high = jnp.where(parity == 1, two, one), jnp.where(parity == 1, one, two)
        dates[n + first, 0], dates[n + first, 1] = low[:40], low[40:]
        dates[n + second, 0], dates[n + second, 1] = high[:40], high[40:]
        return 0

    lax.fori_loop(0, HALF, one, 0)


def inner_kernel(
    table, pairs, own, near, far, edge0, edge1, lines, matrix, names, owners, cells,
    phase_out, power_out, ys,
    lhs, weights, zs, ps, ss, pm,
):
    width = own.shape[-1]

    def one_date(n, _):
        dates = (n + 3, n + 6)
        resample(own, near, far, table, dates, lhs, weights, zs)
        for s, d in enumerate(dates):
            for part, k, cols, tile in slabs(zs, s):
                ys[d, part, 8 * k : 8 * k + 8, cols] = tile.astype(F32)
        return 0

    lax.fori_loop(0, HALF, one_date, 0)
    spread_dates(edge1, edge0, fact(table, 1), ys, 0, 9)

    def one_power(d, _):
        ps[pl.ds(pl.multiple_of(d * 8, 8), 8), :] = power_sum(reader(d))
        return 0

    def reader(d):
        return lambda part, k: ys[d, part, 8 * k : 8 * k + 8, :]

    lax.fori_loop(0, 12, one_power, 0)

    def one_pair(c, _):
        at = pl.multiple_of(c * 8, 8)
        ss[pl.ds(at, 8), :] = cross_sum(reader(pairs[0, c]), reader(pairs[1, c]))
        return 0

    total = ss.shape[0] // 8
    lax.fori_loop(0, total, one_pair, 0)
    power_out[...] = window_sum(ps[...], matrix)
    block = ss.shape[0] // 2

    def one_block(n, _):
        rows = pl.ds(pl.multiple_of(n * block, 8), block)
        pm[rows, :] = window_sum(ss[rows, :], matrix)
        return 0

    lax.fori_loop(0, 2, one_block, 0)
    phases_of(pairs, total, pm, power_out)
    local = column(partner_row(table, lines), PAIR_ROWS, 0)
    row = iota((PAIR_ROWS, 1), 0)
    have_a = jnp.where(row < 36, row // PER_DATE, -9).astype(F32)
    take = choose(names, have_a, local, True)

    n = owners.shape[1]
    spread = (iota((n, 256), 1) == iota((n, 256), 0) + n * fact(table, 3)).astype(BF16)
    codes = jnp.concatenate([owners[...], cells[...]], axis=0).astype(F32).astype(BF16)
    placed = jnp.dot(codes, spread, preferred_element_type=F32)
    lines = iota((PAIR_ROWS, 256), 0)
    phases = jnp.dot(take, pm[...].astype(BF16), preferred_element_type=F32)
    phases = jnp.where(lines == 46, placed[0:1, :], phases)
    phase_out[...] = jnp.where(lines == 47, placed[1:2, :], phases)


def weights_kernel(inverse, weight_out, gather):
    spots = iota((1, weight_out.shape[1]), 1)
    group, k = spots // PAIR_ROWS, spots % PAIR_ROWS
    target = jnp.where(k < 36, 36 * group + k, jnp.where(k < 45, 36 * group + k - 45, -1))

    def one_rows(n, _):
        at = pl.multiple_of(n * 16, 16)
        gather[pl.ds(at, 16), :] = (iota((16, gather.shape[1]), 0) + at == target).astype(BF16)
        return 0

    lax.fori_loop(0, gather.shape[0] // 16, one_rows, 0)
    weight_out[0:191, :] = jnp.dot(
        inverse[...], gather[...], preferred_element_type=F32
    ).astype(BF16)
    weight_out[191:192, :] = jnp.zeros((1, weight_out.shape[1]), BF16)


def outer_kernel(
    table, pairs, got0, got1, ys, power, phase, lines, matrix, names, out, rs, ps, ss, pm, pw
):
    width = got0.shape[1]
    odd_date = fact(table, 1)

    spread_dates(got0, got1, odd_date, rs, 0, 3)

    def here(d):
        return lambda part, k: ys[d, part, 8 * k : 8 * k + 8, :]

    def there(d):
        return lambda part, k: rs[d, part, 8 * k : 8 * k + 8, :]

    def one_power(n, _):
        ps[pl.ds(pl.multiple_of(n * 8, 8), 8), :] = power_sum(there(n))
        return 0

    lax.fori_loop(0, 2 * HALF, one_power, 0)

    def one_after(c, _):
        at = pl.multiple_of(c * 8, 8)
        ss[pl.ds(at, 8), :] = cross_sum(here(pairs[0, c]), there(pairs[1, c] - 12))
        return 0

    def one_before(c, _):
        at = pl.multiple_of(c * 8, 8)
        ss[pl.ds(at, 8), :] = cross_sum(there(pairs[0, c] - 12), here(pairs[1, c]))
        return 0

    total = ss.shape[0] // 8
    lax.fori_loop(0, len(CROSS), one_after, 0)
    lax.fori_loop(len(CROSS), len(CROSS) + len(BEFORE), one_before, 0)
    last = 8 * (len(CROSS) + len(BEFORE))
    ss[last:, :] = jnp.zeros_like(ss[last:, :])
    pw[0:96, :] = power[...]
    sums = window_sum(jnp.concatenate([ss[...], ps[...]], axis=0), matrix)
    pm[...] = sums[: ss.shape[0]]
    pw[96:144, :] = sums[ss.shape[0] :]
    phases_of(pairs, total, pm, pw)
    local = column(partner_row(table, lines), PAIR_ROWS, 0)
    row = iota((PAIR_ROWS, 1), 0)
    told = jnp.where(odd_date == 1, got0[240:256, 0:LANES], got1[240:256, 0:LANES]).astype(F32)
    told = jnp.max(told, axis=1, keepdims=True)
    spread = (iota((PAIR_ROWS, 16), 0) - 36 == iota((PAIR_ROWS, 16), 1)).astype(BF16)
    moved = jnp.dot(
        spread, jnp.broadcast_to(told, (16, LANES)).astype(BF16), preferred_element_type=F32
    )[:, 0:1]
    mine = jnp.where(row < 36, jnp.where(local < 15, local, -5.0), jnp.where(row < 45, moved, -5.0))
    mine = jnp.where((row >= 36) & (mine < 15), -5.0, mine)
    have_a = jnp.where(row < 36, row // PER_DATE, 9 + (row - 36) // PER_DATE).astype(F32)
    take = choose(names, have_a, mine, False)
    total = phase[...] + jnp.dot(take, pm[...].astype(BF16), preferred_element_type=F32)
    for g in range(out.shape[0]):
        out[g] = total.astype(BF16)


def series_kernel(table, got, weight, out):
    stack = jnp.concatenate([got[g] for g in range(got.shape[0])], axis=0)
    series = jnp.dot(weight[...], stack, preferred_element_type=F32)
    wide = series.shape[1]
    rows = jnp.where(iota(series.shape, 0) == 191, 1.0, series)
    rows = jnp.concatenate([rows, jnp.zeros((64, wide), F32)], axis=0).astype(BF16)
    codes = got[0, 40:48, :].astype(F32)
    for g in range(1, got.shape[0]):
        codes = codes + got[g, 40:48, :].astype(F32)
    owner, cell = codes[6:7, :], codes[7:8, :]
    base = fact(table, 3).astype(F32) * 8.0
    mine = (cell >= base) & (cell < base + 8)
    target = jnp.where(mine, owner * 8 + cell - base, -1.0).astype(jnp.int32)
    select = (iota((out.shape[0], wide), 0) == target).astype(BF16)
    out[...] = lax.dot_general(
        select, rows, (((1,), (1,)), ((), ())), preferred_element_type=F32
    ).astype(BF16)


def final_kernel(got, lines, out):
    total = got[0].astype(F32)
    for g in range(1, got.shape[0]):
        total = total + got[g].astype(F32)
    total = total[:, 0:DATES]
    lane = iota(total.shape, 1)
    counts = jnp.sum(jnp.where(lane == DATES - 1, total, 0.0), axis=1, keepdims=True)
    velocity = jnp.sum(total * lines[19:20, :], axis=1, keepdims=True)
    total = jnp.where(lane == DATES - 1, velocity, total)
    out[...] = total / jnp.maximum(counts, 1.0)


SMEM = pl.BlockSpec(memory_space=pltpu.SMEM)
VMEM = pl.BlockSpec(memory_space=pltpu.VMEM)


def call(kernel, smem, vmem, outs, scratch=()):
    return pl.pallas_call(
        kernel,
        in_specs=[SMEM] * len(smem) + [VMEM] * len(vmem),
        out_specs=[VMEM] * len(outs),
        out_shape=[jax.ShapeDtypeStruct(s, t) for s, t in outs],
        scratch_shapes=list(scratch),
        compiler_params=pltpu.CompilerParams(vmem_limit_bytes=VMEM_BYTES),
    )(*smem, *vmem)


def swaps(count, start):
    return [p for i in range(start, count - 1, 2) for p in ((i, i + 1), (i + 1, i))]


def pair_names(pairs, rows):
    names = np.full((2, rows), -20.0, np.float32)
    for c, (a, b) in enumerate(pairs):
        names[0, 8 * c : 8 * c + 8] = a
        names[1, 8 * c : 8 * c + 8] = b
    return jnp.asarray(names)


def pair_table(pairs, rows):
    table = np.zeros((2, rows // 8), np.int32)
    table[:, : len(pairs)] = np.array(pairs, np.int32).T
    return jnp.asarray(table)


def local(slc_stack, offsets, kernels, partner, inverse, rate_weights, owners, map_cell):
    date_count, width = slc_stack.shape[1], slc_stack.shape[3]
    groups, strips = lax.axis_size("date"), lax.axis_size("col")
    group, strip = lax.axis_index("date"), lax.axis_index("col")
    rows = [
        jnp.transpose(kernels, (1, 2, 0)).reshape(2 * TAPS, DATES),
        offsets.T.astype(F32),
        jnp.pad(partner.reshape(1, -1).astype(F32), ((0, 0), (0, DATES - partner.shape[0]))),
    ]
    rows.append(jnp.pad(rate_weights.reshape(1, -1), ((0, 0), (0, DATES - rate_weights.shape[0]))))
    facts = jnp.stack([group * date_count, group % 2, strip % 2, group]).astype(F32)
    rows.append(jnp.broadcast_to(facts[:, None], (4, DATES)))
    facts = facts.reshape(1, -1)
    table, at = jnp.zeros((24, DATES), F32), 0
    for part in rows:
        table = table + jnp.pad(part, ((at, 24 - at - part.shape[0]), (0, 0)))
        at += part.shape[0]
    mine = lax.dynamic_slice(table, (0, group * date_count), (table.shape[0], date_count))

    tile = jax.ShapeDtypeStruct((2, ROWS, LANES), BF16)
    tile0, tile1 = pl.pallas_call(
        pack_kernel,
        in_specs=[SMEM, pl.BlockSpec(memory_space=pl.ANY)],
        out_specs=[VMEM] * 2,
        out_shape=[tile] * 2,
        scratch_shapes=[
            pltpu.VMEM((2,) + slc_stack.shape[:3] + (LANES,), BF16),
            pltpu.VMEM((2, 2, ROWS, LANES), F32),
            pltpu.SemaphoreType.DMA((2,)),
        ],
        compiler_params=pltpu.CompilerParams(vmem_limit_bytes=53 * 1024 * 1024),
    )((strip % 2).astype(jnp.int32).reshape(1), slc_stack)
    own = lax.reduce_precision(slc_stack, 8, 7)
    near = lax.ppermute(tile0, "col", swaps(strips, 0))
    far = lax.ppermute(tile1, "col", swaps(strips, 1))
    (weight,) = call(
        weights_kernel,
        (),
        (inverse,),
        [((DATES, groups * PAIR_ROWS), BF16)],
        [pltpu.VMEM((inverse.shape[1], groups * PAIR_ROWS), BF16)],
    )
    far, weight = lax.optimization_barrier((far, weight))
    scratch = [
        pltpu.VMEM((2, 2 * ROWS * width // LANES, 2 * LANES), BF16),
        pltpu.VMEM((2, 4 * LANES, 2 * LANES), BF16),
        pltpu.VMEM((2, 2, width // LANES, ROWS, LANES), F32),
    ]
    edge0, edge1 = call(
        edge_kernel,
        (mine,),
        (own, near, far, table),
        [((256, width), BF16)] * 2,
        scratch,
    )
    got0 = lax.ppermute(edge0, "date", swaps(groups, 0))
    got1 = lax.ppermute(edge1, "date", swaps(groups, 1))
    window = np.arange(width)[:, None] // LOOK_RG == np.arange(256)[None, :] % (width // LOOK_RG)
    matrix = jnp.asarray(window.astype(np.float32)).astype(BF16)
    inner_rows = 8 * (len(INNER) + 5)
    outer_rows = 8 * (len(CROSS) + len(BEFORE) + 3)
    outer_pairs = CROSS + [(a + 6, b - 12) for a, b in BEFORE]
    phase, power, ys = call(
        inner_kernel,
        (mine, pair_table(INNER, inner_rows)),
        (
            own, near, far, edge0, edge1, table, matrix, pair_names(INNER, inner_rows),
            owners.reshape(1, -1), map_cell,
        ),
        [
            ((PAIR_ROWS, 256), F32),
            ((96, 256), F32),
            ((12, 2, ROWS, width), F32),
        ],
        scratch
        + [
            pltpu.VMEM((96, width), F32),
            pltpu.VMEM((inner_rows, width), F32),
            pltpu.VMEM((inner_rows, 256), F32),
        ],
    )
    (sent,) = call(
        outer_kernel,
        (facts, pair_table(outer_pairs, outer_rows)),
        (got0, got1, ys, power, phase, table, matrix, pair_names(CROSS + BEFORE, outer_rows)),
        [((groups, PAIR_ROWS, 256), BF16)],
        [
            pltpu.VMEM((6, 2, ROWS, width), F32),
            pltpu.VMEM((48, width), F32),
            pltpu.VMEM((outer_rows, width), F32),
            pltpu.VMEM((outer_rows, 256), F32),
            pltpu.VMEM((144, 256), F32),
        ],
    )
    phases = lax.all_to_all(sent, "date", 0, 0, tiled=True)
    (routed,) = call(series_kernel, (facts,), (phases, weight), [((8 * strips, 256), BF16)])
    parts = lax.all_to_all(routed.reshape(strips, 8, 256), "col", 0, 0, tiled=True)
    (mean,) = call(final_kernel, (), (parts, table), [((8, DATES), F32)])
    return mean.reshape(1, 8, DATES)


def solution(mesh):
    in_specs = (
        P(None, "date", None, "col"),
        P(),
        P(),
        P("date"),
        P(),
        P(),
        P("col", "date", None),
        P("col", "date"),
    )
    out_specs = P("col", "date", None)
    return jax.shard_map(local, mesh=mesh, in_specs=in_specs, out_specs=out_specs, check_vma=False)
```

```python
import functools

import jax
import jax.numpy as jnp
import numpy as np
from jax import lax
from jax.experimental import pallas as pl
from jax.experimental.pallas import tpu as pltpu
from jax.sharding import PartitionSpec as P

PER_DATE = 3
SPAN = 6
HALF = 3
ROW_BLOCK = 20
TAPS = 8
HALO = 8
LOOK_AZ = 5
LOOK_RG = 20
LROWS = 8
LANES = 128
ROWS = 40
DATES = 192
EXTRA = 9
FACTS = 20
PAIR_ROWS = 48
F32 = jnp.float32
BF16 = jnp.bfloat16
VMEM_BYTES = 24 * 1024 * 1024

INNER = [(a, a + s) for a in range(6) for s in range(1, 7)]
INNER += [(a, b) for a in range(6, 11) for b in range(a + 1, 12)]
CROSS = [(a, b) for b in range(12, 15) for a in range(b - 6, 12)]
BEFORE = [(a, b) for b in range(15, 18) for a in range(b - 6, 12)]


def iota(shape, dim):
    return lax.broadcasted_iota(jnp.int32, shape, dim)


def fact(table, n):
    return (table[0, n] if table.shape[0] == 1 else table[FACTS + n, 0]).astype(jnp.int32)


def partner_row(table, lines):
    return lines[18:19, 0:36] - fact(table, 0).astype(F32)


def tap_weights(table, at, weights):
    lane, row = iota((16, LANES), 1), iota((16, LANES), 0)
    for b in range(2):
        start = LANES + 4 - table[2 * TAPS + b, at].astype(jnp.int32)
        line = jnp.zeros((8, LANES), F32)
        for t in range(TAPS):
            here = iota((8, LANES), 1) == lax.rem(start - t, LANES)
            line = jnp.where(here, table[TAPS * b + t, at], line)
        cols = slice(LANES * b, LANES * b + LANES)
        for m in range(0, LANES, 16):
            both = jnp.concatenate(
                [pltpu.roll(line, m + 8 * i, 1, stride=1, stride_axis=0) for i in range(2)], axis=0
            )
            apart = lane - row - m
            near = (apart < 64) & (apart > -64)
            for at_row, tile in ((m, jnp.where(near, both, 0.0)), (LANES + m, jnp.where(near, 0.0, both))):
                high = tile.astype(BF16)
                weights[at_row : at_row + 16, cols] = high
                weights[256 + at_row : 272 + at_row, cols] = (tile - high.astype(F32)).astype(BF16)


def resample(own, near, far, table, dates, lhs, weights, zs):
    is_odd = fact(table, 2) == 1
    count = own.shape[-1] // LANES
    lane = iota((ROWS, LANES), 1)
    for s, date in enumerate(dates):
        tap_weights(table, date, weights.at[s])
    for s, date in enumerate(dates):
        for part in range(2):
            tile_a, tile_b = near[part].astype(F32), far[part].astype(F32)
            left = pltpu.roll(jnp.where(is_odd, tile_a, tile_b), LANES - HALO - HALO * date, 1)
            right = pltpu.roll(
                jnp.where(is_odd, tile_b, tile_a), lax.rem(LANES - HALO * date, LANES), 1
            )
            line = own[part, date].astype(F32)
            tiles = [left] + [line[:, LANES * j : LANES * (j + 1)] for j in range(count)] + [right]
            for j in range(count):
                rows = slice(ROWS * (count * part + j), ROWS * (count * part + j + 1))
                lhs[s, rows, 0:LANES] = own[part, date, :, LANES * j : LANES * (j + 1)]
                lhs[s, rows, LANES : 2 * LANES] = jnp.where(
                    lane < 64, tiles[j + 2], tiles[j]
                ).astype(BF16)
    row = iota((8, LANES), 0)
    outs = []
    for s in range(len(dates)):
        taken = lhs[s]
        outs.append(
            jnp.dot(
                jnp.concatenate([taken, taken], axis=1), weights[s], preferred_element_type=F32
            )
        )
    for s, out in enumerate(outs):
        for part in range(2):
            for j in range(count):
                tile = out[ROWS * (count * part + j) : ROWS * (count * part + j + 1)]
                first, second = tile[:, :LANES], tile[:, LANES:]
                zs[s, part, j, 0:16, :] = first[:16]
                zs[s, part, j, 16:24, :] = jnp.where(row < 4, first[16:24], second[16:24])
                zs[s, part, j, 24:40, :] = second[24:]


def slabs(zs, s):
    for part in range(2):
        for k in range(LOOK_AZ):
            for j in range(zs.shape[2]):
                tile = zs[s, part, j, pl.ds(k, LROWS, stride=LOOK_AZ), :].astype(BF16)
                yield part, k, slice(LANES * j, LANES * (j + 1)), tile


def column(row, rows, offset):
    wide = row.shape[1]
    at = iota((rows, wide), 1) == iota((rows, wide), 0) + offset
    return jnp.sum(jnp.where(at, row, 0.0), axis=1, keepdims=True)


def pack_kernel(odd, own, out0, out1, ends, acc, sems):
    far = own.shape[3] - LANES
    even = odd[0] == 0
    copies = [
        pltpu.make_async_copy(own.at[:, :, :, at : at + LANES], ends.at[n], sems.at[n])
        for n, at in enumerate((0, far))
    ]
    for copy in copies:
        copy.start()
    acc[...] = jnp.zeros_like(acc)
    for copy in copies:
        copy.wait()

    def one(d, _):
        for part in range(2):
            head = pltpu.roll(ends[0, part, d].astype(F32), HALO * d, 1)
            tail = pltpu.roll(ends[1, part, d].astype(F32), HALO * d + HALO, 1)
            here = iota(head.shape, 1) // HALO == d
            for n, tile in enumerate((jnp.where(even, tail, head), jnp.where(even, head, tail))):
                acc[n, part] = jnp.where(here, tile, acc[n, part])
        return 0

    lax.fori_loop(0, own.shape[1], one, 0)
    out0[...] = acc[0].astype(BF16)
    out1[...] = acc[1].astype(BF16)


def edge_kernel(table, own, near, far, lines, head, tail, lhs, weights, zs):
    local = column(partner_row(table, lines), 16, 36 - EXTRA)
    for out in (head, tail):
        out[240:256, :] = jnp.broadcast_to(local, (16, out.shape[1])).astype(BF16)

    def one(i, _):
        dates = (i, i + 9)
        resample(own, near, far, table, dates, lhs, weights, zs)
        for s, out in enumerate((head, tail)):
            for part, k, cols, tile in slabs(zs, s):
                out[pl.ds(pl.multiple_of(i * 80 + part * 40 + k * 8, 8), 8), cols] = tile
        return 0

    lax.fori_loop(0, HALF, one, 0)


def window_sum(values, matrix):
    high = values.astype(BF16)
    low = (values - high.astype(F32)).astype(BF16)
    both = jnp.dot(
        jnp.concatenate([high, low], axis=0), matrix[...], preferred_element_type=F32
    )
    return both[: values.shape[0]] + both[values.shape[0] :]


def cross_sum(first, second):
    total = None
    for k in range(LOOK_AZ):
        re1, im1 = first(0, k), first(1, k)
        re2, im2 = second(0, k), second(1, k)
        term = im1 * re2 - re1 * im2
        total = term if total is None else total + term
    return total


def power_sum(date):
    total = None
    for k in range(LOOK_AZ):
        re, im = date(0, k), date(1, k)
        term = re * re + im * im
        total = term if total is None else total + term
    return total


def phase_of(cross, power_a, power_b, mask):
    scale = 1.0 / (LOOK_AZ * LOOK_RG)
    product = (power_a * scale) * (power_b * scale) + 1e-06
    return jnp.where(mask, (cross * scale) * lax.rsqrt(product), 0.0)


def choose(names, have_a, have_b, reverse):
    a, b = names[0:1, :], names[1:2, :]
    take = ((have_a == a) & (have_b == b)).astype(F32)
    if reverse:
        take = take - ((have_a == b) & (have_b == a)).astype(F32)
    return take.astype(BF16)


def phases_of(pairs, count, pm, powers):
    mask = iota((8, 256), 1) // 32 == iota((8, 256), 0)

    def one(n, _):
        done = []
        for u in range(8):
            c = 8 * n + u
            rows = pl.ds(pl.multiple_of(c * 8, 8), 8)
            row_a = pl.ds(pl.multiple_of(pairs[0, c] * 8, 8), 8)
            row_b = pl.ds(pl.multiple_of(pairs[1, c] * 8, 8), 8)
            done.append(phase_of(pm[rows, :], powers[row_a, :], powers[row_b, :], mask))
        pm[pl.ds(pl.multiple_of(n * 64, 64), 64), :] = jnp.concatenate(done, axis=0)
        return 0

    lax.fori_loop(0, count // 8, one, 0)


def unpack_dates(packed, dates, start):
    def one(n, _):
        both = packed[pl.ds(pl.multiple_of(n * 80, 16), 80), :].astype(F32)
        dates[n + start, 0], dates[n + start, 1] = both[:40], both[40:]
        return 0

    lax.fori_loop(0, HALF, one, 0)


def inner_kernel(
    table, pairs, own, near, far, edge0, edge1, lines, matrix, names, owners, cells,
    phase_out, power_out, ys,
    lhs, weights, zs, ps, ss, pm,
):
    width = own.shape[-1]

    def one_date(n, _):
        dates = (n + 3, n + 6)
        resample(own, near, far, table, dates, lhs, weights, zs)
        for s, d in enumerate(dates):
            for part, k, cols, tile in slabs(zs, s):
                ys[d, part, 8 * k : 8 * k + 8, cols] = tile.astype(F32)
        return 0

    lax.fori_loop(0, HALF, one_date, 0)
    unpack_dates(edge0, ys, 0)
    unpack_dates(edge1, ys, 9)

    def one_power(d, _):
        ps[pl.ds(pl.multiple_of(d * 8, 8), 8), :] = power_sum(reader(d))
        return 0

    def reader(d):
        return lambda part, k: ys[d, part, 8 * k : 8 * k + 8, :]

    lax.fori_loop(0, 12, one_power, 0)

    def one_pair(c, _):
        at = pl.multiple_of(c * 8, 8)
        ss[pl.ds(at, 8), :] = cross_sum(reader(pairs[0, c]), reader(pairs[1, c]))
        return 0

    total = ss.shape[0] // 8
    lax.fori_loop(0, total, one_pair, 0)
    power_out[...] = window_sum(ps[...], matrix)
    block = ss.shape[0] // 2

    def one_block(n, _):
        rows = pl.ds(pl.multiple_of(n * block, 8), block)
        pm[rows, :] = window_sum(ss[rows, :], matrix)
        return 0

    lax.fori_loop(0, 2, one_block, 0)
    phases_of(pairs, total, pm, power_out)
    local = column(partner_row(table, lines), PAIR_ROWS, 0)
    row = iota((PAIR_ROWS, 1), 0)
    have_a = jnp.where(row < 36, row // PER_DATE, -9).astype(F32)
    take = choose(names, have_a, local, True)

    n = owners.shape[1]
    spread = (iota((n, 256), 1) == iota((n, 256), 0) + n * fact(table, 3)).astype(BF16)
    codes = jnp.concatenate([owners[...], cells[...]], axis=0).astype(F32).astype(BF16)
    placed = jnp.dot(codes, spread, preferred_element_type=F32)
    lines = iota((PAIR_ROWS, 256), 0)
    phases = jnp.dot(take, pm[...].astype(BF16), preferred_element_type=F32)
    phases = jnp.where(lines == 46, placed[0:1, :], phases)
    phase_out[...] = jnp.where(lines == 47, placed[1:2, :], phases)


def weights_kernel(inverse, weight_out, gather):
    spots = iota((1, weight_out.shape[1]), 1)
    group, k = spots // PAIR_ROWS, spots % PAIR_ROWS
    target = jnp.where(k < 36, 36 * group + k, jnp.where(k < 45, 36 * group + k - 45, -1))

    def one_rows(n, _):
        at = pl.multiple_of(n * 16, 16)
        gather[pl.ds(at, 16), :] = (iota((16, gather.shape[1]), 0) + at == target).astype(BF16)
        return 0

    lax.fori_loop(0, gather.shape[0] // 16, one_rows, 0)
    weight_out[0:191, :] = jnp.dot(
        inverse[...], gather[...], preferred_element_type=F32
    ).astype(BF16)
    weight_out[191:192, :] = jnp.zeros((1, weight_out.shape[1]), BF16)


def boundary_phases(pairs, count, later, got, ys, power, matrix, rs, ss, pm, pw):
    unpack_dates(got, rs, 0)

    def here(d):
        return lambda part, k: ys[d, part, 8 * k : 8 * k + 8, :]

    def there(d):
        return lambda part, k: rs[d - 12, part, 8 * k : 8 * k + 8, :]

    first, second = (here, there) if later else (there, here)

    def one_pair(c, _):
        at = pl.multiple_of(c * 8, 8)
        ss[pl.ds(at, 8), :] = cross_sum(first(pairs[0, c]), second(pairs[1, c]))
        return 0

    lax.fori_loop(0, count, one_pair, 0)
    rows = pm.shape[0]

    def one_power(n, _):
        ss[pl.ds(pl.multiple_of(rows + n * 8, 8), 8), :] = power_sum(there(n + 12))
        return 0

    lax.fori_loop(0, HALF, one_power, 0)
    ss[count * 8 : rows, :] = jnp.zeros_like(ss[count * 8 : rows, :])
    pw[0:96, :] = power[...]
    sums = window_sum(ss[...], matrix)
    pm[...] = sums[:rows]
    pw[96:120, :] = sums[rows:]
    phases_of(pairs, rows // 8, pm, pw)


def after_kernel(
    facts, pairs, got, ys, power, phase, lines, matrix, names, out, rs, ss, pm, pw
):
    boundary_phases(pairs, len(CROSS), True, got, ys, power, matrix, rs, ss, pm, pw)
    local = column(partner_row(facts, lines), PAIR_ROWS, 0)
    row = iota((PAIR_ROWS, 1), 0)
    have_a = jnp.where(row < 36, row // PER_DATE, -9).astype(F32)
    take = choose(names, have_a, local, False)
    out[...] = phase[...] + jnp.dot(take, pm[...].astype(BF16), preferred_element_type=F32)


def before_kernel(pairs, got, ys, power, phase, matrix, names, out, rs, ss, pm, pw):
    boundary_phases(pairs, len(BEFORE), False, got, ys, power, matrix, rs, ss, pm, pw)
    told = jnp.max(got[240:256, 0:LANES].astype(F32), axis=1, keepdims=True)
    spread = (iota((PAIR_ROWS, 16), 0) - 36 == iota((PAIR_ROWS, 16), 1)).astype(BF16)
    moved = jnp.dot(
        spread, jnp.broadcast_to(told, (16, LANES)).astype(BF16), preferred_element_type=F32
    )[:, 0:1]
    row = iota((PAIR_ROWS, 1), 0)
    theirs = (row >= 36) & (row < 36 + EXTRA)
    have_a = jnp.where(theirs, 9 + (row - 36) // PER_DATE, -9).astype(F32)
    take = choose(names, have_a, jnp.where(theirs, moved, -5.0), False)
    total = phase[...] + jnp.dot(take, pm[...].astype(BF16), preferred_element_type=F32)
    for g in range(out.shape[0]):
        out[g] = total.astype(BF16)


def series_kernel(table, got, weight, out):
    stack = jnp.concatenate([got[g] for g in range(got.shape[0])], axis=0)
    series = jnp.dot(weight[...], stack, preferred_element_type=F32)
    wide = series.shape[1]
    rows = jnp.where(iota(series.shape, 0) == 191, 1.0, series)
    rows = jnp.concatenate([rows, jnp.zeros((64, wide), F32)], axis=0).astype(BF16)
    codes = got[0, 40:48, :].astype(F32)
    for g in range(1, got.shape[0]):
        codes = codes + got[g, 40:48, :].astype(F32)
    owner, cell = codes[6:7, :], codes[7:8, :]
    base = fact(table, 3).astype(F32) * 8.0
    mine = (cell >= base) & (cell < base + 8)
    target = jnp.where(mine, owner * 8 + cell - base, -1.0).astype(jnp.int32)
    select = (iota((out.shape[0], wide), 0) == target).astype(BF16)
    out[...] = lax.dot_general(
        select, rows, (((1,), (1,)), ((), ())), preferred_element_type=F32
    ).astype(BF16)


def final_kernel(got, lines, out):
    total = got[0].astype(F32)
    for g in range(1, got.shape[0]):
        total = total + got[g].astype(F32)
    total = total[:, 0:DATES]
    lane = iota(total.shape, 1)
    counts = jnp.sum(jnp.where(lane == DATES - 1, total, 0.0), axis=1, keepdims=True)
    velocity = jnp.sum(total * lines[19:20, :], axis=1, keepdims=True)
    total = jnp.where(lane == DATES - 1, velocity, total)
    out[...] = total / jnp.maximum(counts, 1.0)


SMEM = pl.BlockSpec(memory_space=pltpu.SMEM)
VMEM = pl.BlockSpec(memory_space=pltpu.VMEM)


def call(kernel, smem, vmem, outs, scratch=()):
    return pl.pallas_call(
        kernel,
        in_specs=[SMEM] * len(smem) + [VMEM] * len(vmem),
        out_specs=[VMEM] * len(outs),
        out_shape=[jax.ShapeDtypeStruct(s, t) for s, t in outs],
        scratch_shapes=list(scratch),
        compiler_params=pltpu.CompilerParams(vmem_limit_bytes=VMEM_BYTES),
    )(*smem, *vmem)


def swaps(count, start):
    return [p for i in range(start, count - 1, 2) for p in ((i, i + 1), (i + 1, i))]


def pair_names(pairs, rows):
    names = np.full((2, rows), -20.0, np.float32)
    for c, (a, b) in enumerate(pairs):
        names[0, 8 * c : 8 * c + 8] = a
        names[1, 8 * c : 8 * c + 8] = b
    return jnp.asarray(names)


def pair_table(pairs, rows):
    table = np.zeros((2, rows // 8), np.int32)
    table[:, : len(pairs)] = np.array(pairs, np.int32).T
    return jnp.asarray(table)


def local(slc_stack, offsets, kernels, partner, inverse, rate_weights, owners, map_cell):
    date_count, width = slc_stack.shape[1], slc_stack.shape[3]
    groups, strips = lax.axis_size("date"), lax.axis_size("col")
    group, strip = lax.axis_index("date"), lax.axis_index("col")
    rows = [
        jnp.transpose(kernels, (1, 2, 0)).reshape(2 * TAPS, DATES),
        offsets.T.astype(F32),
        jnp.pad(partner.reshape(1, -1).astype(F32), ((0, 0), (0, DATES - partner.shape[0]))),
    ]
    rows.append(jnp.pad(rate_weights.reshape(1, -1), ((0, 0), (0, DATES - rate_weights.shape[0]))))
    facts = jnp.stack([group * date_count, group % 2, strip % 2, group]).astype(F32)
    rows.append(jnp.broadcast_to(facts[:, None], (4, DATES)))
    facts = facts.reshape(1, -1)
    table, at = jnp.zeros((24, DATES), F32), 0
    for part in rows:
        table = table + jnp.pad(part, ((at, 24 - at - part.shape[0]), (0, 0)))
        at += part.shape[0]
    mine = lax.dynamic_slice(table, (0, group * date_count), (table.shape[0], date_count))

    tile = jax.ShapeDtypeStruct((2, ROWS, LANES), BF16)
    tile0, tile1 = pl.pallas_call(
        pack_kernel,
        in_specs=[SMEM, pl.BlockSpec(memory_space=pl.ANY)],
        out_specs=[VMEM] * 2,
        out_shape=[tile] * 2,
        scratch_shapes=[
            pltpu.VMEM((2,) + slc_stack.shape[:3] + (LANES,), BF16),
            pltpu.VMEM((2, 2, ROWS, LANES), F32),
            pltpu.SemaphoreType.DMA((2,)),
        ],
        compiler_params=pltpu.CompilerParams(vmem_limit_bytes=53 * 1024 * 1024),
    )((strip % 2).astype(jnp.int32).reshape(1), slc_stack)
    own = lax.reduce_precision(slc_stack, 8, 7)
    near = lax.ppermute(tile0, "col", swaps(strips, 0))
    far = lax.ppermute(tile1, "col", swaps(strips, 1))
    (weight,) = call(
        weights_kernel,
        (),
        (inverse,),
        [((DATES, groups * PAIR_ROWS), BF16)],
        [pltpu.VMEM((inverse.shape[1], groups * PAIR_ROWS), BF16)],
    )
    far, weight = lax.optimization_barrier((far, weight))
    scratch = [
        pltpu.VMEM((2, 2 * ROWS * width // LANES, 2 * LANES), BF16),
        pltpu.VMEM((2, 4 * LANES, 2 * LANES), BF16),
        pltpu.VMEM((2, 2, width // LANES, ROWS, LANES), F32),
    ]
    edge0, edge1 = call(
        edge_kernel,
        (mine,),
        (own, near, far, table),
        [((256, width), BF16)] * 2,
        scratch,
    )
    later = lax.ppermute(edge0, "date", [(i + 1, i) for i in range(groups - 1)])
    earlier = lax.ppermute(edge1, "date", [(i, i + 1) for i in range(groups - 1)])
    window = np.arange(width)[:, None] // LOOK_RG == np.arange(256)[None, :] % (width // LOOK_RG)
    matrix = jnp.asarray(window.astype(np.float32)).astype(BF16)
    inner_rows = 8 * (len(INNER) + 5)
    phase, power, ys = call(
        inner_kernel,
        (mine, pair_table(INNER, inner_rows)),
        (
            own, near, far, edge0, edge1, table, matrix, pair_names(INNER, inner_rows),
            owners.reshape(1, -1), map_cell,
        ),
        [
            ((PAIR_ROWS, 256), F32),
            ((96, 256), F32),
            ((12, 2, ROWS, width), F32),
        ],
        scratch
        + [
            pltpu.VMEM((96, width), F32),
            pltpu.VMEM((inner_rows, width), F32),
            pltpu.VMEM((inner_rows, 256), F32),
        ],
    )
    def boundary(kernel, smem, vmem, pairs, table_pairs, out):
        rows = 8 * (-(-len(pairs) // 8) * 8)
        (result,) = call(
            kernel,
            smem + (pair_table(table_pairs, rows),),
            vmem + (pair_names(pairs, rows),),
            [out],
            [
                pltpu.VMEM((HALF, 2, ROWS, width), F32),
                pltpu.VMEM((rows + 8 * HALF, width), F32),
                pltpu.VMEM((rows, 256), F32),
                pltpu.VMEM((96 + 8 * HALF, 256), F32),
            ],
        )
        return result

    phase = boundary(
        after_kernel,
        (facts,),
        (later, ys, power, phase, table, matrix),
        CROSS,
        CROSS,
        ((PAIR_ROWS, 256), F32),
    )
    sent = boundary(
        before_kernel,
        (),
        (earlier, ys, power, phase, matrix),
        BEFORE,
        [(a + 3, b - 12) for a, b in BEFORE],
        ((groups, PAIR_ROWS, 256), BF16),
    )
    phases = lax.all_to_all(sent, "date", 0, 0, tiled=True)
    (routed,) = call(series_kernel, (facts,), (phases, weight), [((8 * strips, 256), BF16)])
    parts = lax.all_to_all(routed.reshape(strips, 8, 256), "col", 0, 0, tiled=True)
    (mean,) = call(final_kernel, (), (parts, table), [((8, DATES), F32)])
    return mean.reshape(1, 8, DATES)


def solution(mesh):
    in_specs = (
        P(None, "date", None, "col"),
        P(),
        P(),
        P("date"),
        P(),
        P(),
        P("col", "date", None),
        P("col", "date"),
    )
    out_specs = P("col", "date", None)
    return jax.shard_map(local, mesh=mesh, in_specs=in_specs, out_specs=out_specs, check_vma=False)
```

```python
import functools

import jax
import jax.numpy as jnp
import numpy as np
from jax import lax
from jax.experimental import pallas as pl
from jax.experimental.pallas import tpu as pltpu
from jax.sharding import PartitionSpec as P

PER_DATE = 3
SPAN = 6
HALF = 3
ROW_BLOCK = 20
TAPS = 8
HALO = 8
LOOK_AZ = 5
LOOK_RG = 20
LROWS = 8
LANES = 128
ROWS = 40
DATES = 192
EXTRA = 9
FACTS = 20
PAIR_ROWS = 48
F32 = jnp.float32
BF16 = jnp.bfloat16
VMEM_BYTES = 24 * 1024 * 1024

INNER = [(a, a + s) for a in range(6) for s in range(1, 7)]
INNER += [(a, b) for a in range(6, 11) for b in range(a + 1, 12)]
CROSS = [(a, b) for b in range(12, 15) for a in range(b - 6, 12)]
BEFORE = [(a, b) for b in range(15, 18) for a in range(b - 6, 12)]


def iota(shape, dim):
    return lax.broadcasted_iota(jnp.int32, shape, dim)


def fact(table, n):
    return (table[0, n] if table.shape[0] == 1 else table[FACTS + n, 0]).astype(jnp.int32)


def partner_row(table, lines):
    return lines[18:19, 0:36] - fact(table, 0).astype(F32)


def tap_weights(table, at, weights):
    lane, row = iota((16, LANES), 1), iota((16, LANES), 0)
    for b in range(2):
        start = LANES + 4 - table[2 * TAPS + b, at].astype(jnp.int32)
        line = jnp.zeros((8, LANES), F32)
        for t in range(TAPS):
            here = iota((8, LANES), 1) == lax.rem(start - t, LANES)
            line = jnp.where(here, table[TAPS * b + t, at], line)
        cols = slice(LANES * b, LANES * b + LANES)
        for m in range(0, LANES, 16):
            both = jnp.concatenate(
                [pltpu.roll(line, m + 8 * i, 1, stride=1, stride_axis=0) for i in range(2)], axis=0
            )
            apart = lane - row - m
            near = (apart < 64) & (apart > -64)
            for at_row, tile in ((m, jnp.where(near, both, 0.0)), (LANES + m, jnp.where(near, 0.0, both))):
                high = tile.astype(BF16)
                weights[at_row : at_row + 16, cols] = high
                weights[256 + at_row : 272 + at_row, cols] = (tile - high.astype(F32)).astype(BF16)


def resample(own, near, far, table, dates, lhs, weights, zs):
    is_odd = fact(table, 2) == 1
    count = own.shape[-1] // LANES
    lane = iota((ROWS, LANES), 1)
    for s, date in enumerate(dates):
        tap_weights(table, date, weights.at[s])
    for s, date in enumerate(dates):
        for part in range(2):
            tile_a, tile_b = near[part].astype(F32), far[part, 0:ROWS].astype(F32)
            left = pltpu.roll(jnp.where(is_odd, tile_a, tile_b), LANES - HALO - HALO * date, 1)
            right = pltpu.roll(
                jnp.where(is_odd, tile_b, tile_a), lax.rem(LANES - HALO * date, LANES), 1
            )
            line = own[part, date].astype(F32)
            tiles = [left] + [line[:, LANES * j : LANES * (j + 1)] for j in range(count)] + [right]
            for j in range(count):
                rows = slice(ROWS * (count * part + j), ROWS * (count * part + j + 1))
                lhs[s, rows, 0:LANES] = own[part, date, :, LANES * j : LANES * (j + 1)]
                lhs[s, rows, LANES : 2 * LANES] = jnp.where(
                    lane < 64, tiles[j + 2], tiles[j]
                ).astype(BF16)
    row = iota((8, LANES), 0)
    outs = []
    for s in range(len(dates)):
        taken = lhs[s]
        outs.append(
            jnp.dot(
                jnp.concatenate([taken, taken], axis=1), weights[s], preferred_element_type=F32
            )
        )
    for s, out in enumerate(outs):
        for part in range(2):
            for j in range(count):
                tile = out[ROWS * (count * part + j) : ROWS * (count * part + j + 1)]
                first, second = tile[:, :LANES], tile[:, LANES:]
                zs[s, part, j, 0:16, :] = first[:16]
                zs[s, part, j, 16:24, :] = jnp.where(row < 4, first[16:24], second[16:24])
                zs[s, part, j, 24:40, :] = second[24:]


def slabs(zs, s):
    for part in range(2):
        for k in range(LOOK_AZ):
            for j in range(zs.shape[2]):
                tile = zs[s, part, j, pl.ds(k, LROWS, stride=LOOK_AZ), :].astype(BF16)
                yield part, k, slice(LANES * j, LANES * (j + 1)), tile


def column(row, rows, offset):
    wide = row.shape[1]
    at = iota((rows, wide), 1) == iota((rows, wide), 0) + offset
    return jnp.sum(jnp.where(at, row, 0.0), axis=1, keepdims=True)


def pack_kernel(odd, own, out0, out1, ends, sems):
    far = own.shape[3] - LANES
    even = odd[0] == 0
    copies = [
        pltpu.make_async_copy(own.at[:, :, :, at : at + LANES], ends.at[n], sems.at[n])
        for n, at in enumerate((0, far))
    ]
    for copy in copies:
        copy.start()
    lane = iota((ROWS, LANES), 1) // HALO
    for copy in copies:
        copy.wait()

    def one(d, totals):
        here = lane == d
        rolled = [
            pltpu.roll(ends[n, part, d].astype(F32), HALO * d + HALO * n, 1)
            for part in range(2)
            for n in range(2)
        ]
        return tuple(jnp.where(here, r, t) for r, t in zip(rolled, totals))

    zero = jnp.zeros((ROWS, LANES), F32)
    totals = lax.fori_loop(0, own.shape[1], one, (zero,) * 4, unroll=4)
    for part in range(2):
        head, tail = totals[2 * part], totals[2 * part + 1]
        out0[part] = jnp.where(even, tail, head).astype(BF16)
        out1[part, 0:ROWS] = jnp.where(even, head, tail).astype(BF16)
        out1[part, ROWS:] = jnp.zeros((8, LANES), BF16)


def edge_kernel(table, own, near, far, lines, head, tail, lhs, weights, zs):
    local = column(partner_row(table, lines), 16, 36 - EXTRA)
    for out in (head, tail):
        out[240:256, :] = jnp.broadcast_to(local, (16, out.shape[1])).astype(BF16)

    def one(i, _):
        dates = (i, i + 9)
        resample(own, near, far, table, dates, lhs, weights, zs)
        for s, out in enumerate((head, tail)):
            for part, k, cols, tile in slabs(zs, s):
                out[pl.ds(pl.multiple_of(i * 80 + part * 40 + k * 8, 8), 8), cols] = tile
        return 0

    lax.fori_loop(0, HALF, one, 0)


def window_sum(values, matrix):
    high = values.astype(BF16)
    low = (values - high.astype(F32)).astype(BF16)
    both = jnp.dot(
        jnp.concatenate([high, low], axis=0), matrix[...], preferred_element_type=F32
    )
    return both[: values.shape[0]] + both[values.shape[0] :]


def cross_sum(first, second):
    total = None
    for k in range(LOOK_AZ):
        re1, im1 = first(0, k), first(1, k)
        re2, im2 = second(0, k), second(1, k)
        term = im1 * re2 - re1 * im2
        total = term if total is None else total + term
    return total


def power_sum(date):
    total = None
    for k in range(LOOK_AZ):
        re, im = date(0, k), date(1, k)
        term = re * re + im * im
        total = term if total is None else total + term
    return total


def phase_of(cross, power_a, power_b, mask):
    scale = 1.0 / (LOOK_AZ * LOOK_RG)
    product = (power_a * scale) * (power_b * scale) + 1e-06
    return jnp.where(mask, (cross * scale) * lax.rsqrt(product), 0.0)


def choose(names, have_a, have_b, reverse):
    a, b = names[0:1, :], names[1:2, :]
    take = ((have_a == a) & (have_b == b)).astype(F32)
    if reverse:
        take = take - ((have_a == b) & (have_b == a)).astype(F32)
    return take.astype(BF16)


def phases_of(pairs, count, pm, powers):
    mask = iota((8, 256), 1) // 32 == iota((8, 256), 0)

    def one(n, _):
        done = []
        for u in range(8):
            c = 8 * n + u
            rows = pl.ds(pl.multiple_of(c * 8, 8), 8)
            row_a = pl.ds(pl.multiple_of(pairs[0, c] * 8, 8), 8)
            row_b = pl.ds(pl.multiple_of(pairs[1, c] * 8, 8), 8)
            done.append(phase_of(pm[rows, :], powers[row_a, :], powers[row_b, :], mask))
        pm[pl.ds(pl.multiple_of(n * 64, 64), 64), :] = jnp.concatenate(done, axis=0)
        return 0

    lax.fori_loop(0, count // 8, one, 0)


def unpack_dates(packed, dates, start):
    def one(n, _):
        both = packed[pl.ds(pl.multiple_of(n * 80, 16), 80), :].astype(F32)
        dates[n + start, 0], dates[n + start, 1] = both[:40], both[40:]
        return 0

    lax.fori_loop(0, HALF, one, 0)


def inner_kernel(
    table, pairs, own, near, far, edge0, edge1, lines, matrix, names, owners, cells,
    phase_out, power_out, ys,
    lhs, weights, zs, ps, ss, pm,
):
    width = own.shape[-1]

    def one_date(n, _):
        dates = (n + 3, n + 6)
        resample(own, near, far, table, dates, lhs, weights, zs)
        for s, d in enumerate(dates):
            for part, k, cols, tile in slabs(zs, s):
                ys[d, part, 8 * k : 8 * k + 8, cols] = tile.astype(F32)
        return 0

    lax.fori_loop(0, HALF, one_date, 0)
    unpack_dates(edge0, ys, 0)
    unpack_dates(edge1, ys, 9)

    def one_power(d, _):
        ps[pl.ds(pl.multiple_of(d * 8, 8), 8), :] = power_sum(reader(d))
        return 0

    def reader(d):
        return lambda part, k: ys[d, part, 8 * k : 8 * k + 8, :]

    lax.fori_loop(0, 12, one_power, 0)

    def one_pair(c, _):
        at = pl.multiple_of(c * 8, 8)
        ss[pl.ds(at, 8), :] = cross_sum(reader(pairs[0, c]), reader(pairs[1, c]))
        return 0

    total = ss.shape[0] // 8
    lax.fori_loop(0, total, one_pair, 0)
    power_out[...] = window_sum(ps[...], matrix)
    block = ss.shape[0] // 2

    def one_block(n, _):
        rows = pl.ds(pl.multiple_of(n * block, 8), block)
        pm[rows, :] = window_sum(ss[rows, :], matrix)
        return 0

    lax.fori_loop(0, 2, one_block, 0)
    phases_of(pairs, total, pm, power_out)
    local = column(partner_row(table, lines), PAIR_ROWS, 0)
    row = iota((PAIR_ROWS, 1), 0)
    have_a = jnp.where(row < 36, row // PER_DATE, -9).astype(F32)
    take = choose(names, have_a, local, True)

    n = owners.shape[1]
    spread = (iota((n, 256), 1) == iota((n, 256), 0) + n * fact(table, 3)).astype(BF16)
    codes = jnp.concatenate([owners[...], cells[...]], axis=0).astype(F32).astype(BF16)
    placed = jnp.dot(codes, spread, preferred_element_type=F32)
    lines = iota((PAIR_ROWS, 256), 0)
    phases = jnp.dot(take, pm[...].astype(BF16), preferred_element_type=F32)
    phases = jnp.where(lines == 46, placed[0:1, :], phases)
    phase_out[...] = jnp.where(lines == 47, placed[1:2, :], phases)


def weights_kernel(inverse, weight_out, gather):
    spots = iota((1, weight_out.shape[1]), 1)
    group, k = spots // PAIR_ROWS, spots % PAIR_ROWS
    target = jnp.where(k < 36, 36 * group + k, jnp.where(k < 45, 36 * group + k - 45, -1))

    def one_rows(n, _):
        at = pl.multiple_of(n * 16, 16)
        gather[pl.ds(at, 16), :] = (iota((16, gather.shape[1]), 0) + at == target).astype(BF16)
        return 0

    lax.fori_loop(0, gather.shape[0] // 16, one_rows, 0)
    weight_out[0:191, :] = jnp.dot(
        inverse[...], gather[...], preferred_element_type=F32
    ).astype(BF16)
    weight_out[191:192, :] = jnp.zeros((1, weight_out.shape[1]), BF16)


def boundary_phases(pairs, count, later, got, ys, power, matrix, rs, ss, pm, pw):
    unpack_dates(got, rs, 0)

    def here(d):
        return lambda part, k: ys[d, part, 8 * k : 8 * k + 8, :]

    def there(d):
        return lambda part, k: rs[d - 12, part, 8 * k : 8 * k + 8, :]

    first, second = (here, there) if later else (there, here)

    def one_pair(c, _):
        at = pl.multiple_of(c * 8, 8)
        ss[pl.ds(at, 8), :] = cross_sum(first(pairs[0, c]), second(pairs[1, c]))
        return 0

    lax.fori_loop(0, count, one_pair, 0)
    rows = pm.shape[0]

    def one_power(n, _):
        ss[pl.ds(pl.multiple_of(rows + n * 8, 8), 8), :] = power_sum(there(n + 12))
        return 0

    lax.fori_loop(0, HALF, one_power, 0)
    ss[count * 8 : rows, :] = jnp.zeros_like(ss[count * 8 : rows, :])
    pw[0:96, :] = power[...]
    sums = window_sum(ss[...], matrix)
    pm[...] = sums[:rows]
    pw[96:120, :] = sums[rows:]
    phases_of(pairs, rows // 8, pm, pw)


def after_kernel(
    facts, pairs, got, ys, power, phase, lines, matrix, names, out, rs, ss, pm, pw
):
    boundary_phases(pairs, len(CROSS), True, got, ys, power, matrix, rs, ss, pm, pw)
    local = column(partner_row(facts, lines), PAIR_ROWS, 0)
    row = iota((PAIR_ROWS, 1), 0)
    have_a = jnp.where(row < 36, row // PER_DATE, -9).astype(F32)
    take = choose(names, have_a, local, False)
    out[...] = phase[...] + jnp.dot(take, pm[...].astype(BF16), preferred_element_type=F32)


def before_kernel(pairs, got, ys, power, phase, matrix, names, out, rs, ss, pm, pw):
    boundary_phases(pairs, len(BEFORE), False, got, ys, power, matrix, rs, ss, pm, pw)
    told = jnp.max(got[240:256, 0:LANES].astype(F32), axis=1, keepdims=True)
    spread = (iota((PAIR_ROWS, 16), 0) - 36 == iota((PAIR_ROWS, 16), 1)).astype(BF16)
    moved = jnp.dot(
        spread, jnp.broadcast_to(told, (16, LANES)).astype(BF16), preferred_element_type=F32
    )[:, 0:1]
    row = iota((PAIR_ROWS, 1), 0)
    theirs = (row >= 36) & (row < 36 + EXTRA)
    have_a = jnp.where(theirs, 9 + (row - 36) // PER_DATE, -9).astype(F32)
    take = choose(names, have_a, jnp.where(theirs, moved, -5.0), False)
    total = phase[...] + jnp.dot(take, pm[...].astype(BF16), preferred_element_type=F32)
    for g in range(out.shape[0]):
        out[g] = total.astype(BF16)


def series_kernel(table, got, weight, out):
    stack = jnp.concatenate([got[g] for g in range(got.shape[0])], axis=0)
    series = jnp.dot(weight[...], stack, preferred_element_type=F32)
    wide = series.shape[1]
    rows = jnp.where(iota(series.shape, 0) == 191, 1.0, series)
    rows = jnp.concatenate([rows, jnp.zeros((64, wide), F32)], axis=0).astype(BF16)
    codes = got[0, 40:48, :].astype(F32)
    for g in range(1, got.shape[0]):
        codes = codes + got[g, 40:48, :].astype(F32)
    owner, cell = codes[6:7, :], codes[7:8, :]
    base = fact(table, 3).astype(F32) * 8.0
    mine = (cell >= base) & (cell < base + 8)
    target = jnp.where(mine, owner * 8 + cell - base, -1.0).astype(jnp.int32)
    select = (iota((out.shape[0], wide), 0) == target).astype(BF16)
    out[...] = lax.dot_general(
        select, rows, (((1,), (1,)), ((), ())), preferred_element_type=F32
    ).astype(BF16)


def final_kernel(got, lines, out):
    total = got[0].astype(F32)
    for g in range(1, got.shape[0]):
        total = total + got[g].astype(F32)
    total = total[:, 0:DATES]
    lane = iota(total.shape, 1)
    counts = jnp.sum(jnp.where(lane == DATES - 1, total, 0.0), axis=1, keepdims=True)
    velocity = jnp.sum(total * lines[19:20, :], axis=1, keepdims=True)
    total = jnp.where(lane == DATES - 1, velocity, total)
    out[...] = total / jnp.maximum(counts, 1.0)


SMEM = pl.BlockSpec(memory_space=pltpu.SMEM)
VMEM = pl.BlockSpec(memory_space=pltpu.VMEM)


def call(kernel, smem, vmem, outs, scratch=()):
    return pl.pallas_call(
        kernel,
        in_specs=[SMEM] * len(smem) + [VMEM] * len(vmem),
        out_specs=[VMEM] * len(outs),
        out_shape=[jax.ShapeDtypeStruct(s, t) for s, t in outs],
        scratch_shapes=list(scratch),
        compiler_params=pltpu.CompilerParams(vmem_limit_bytes=VMEM_BYTES),
    )(*smem, *vmem)


def swaps(count, start):
    return [p for i in range(start, count - 1, 2) for p in ((i, i + 1), (i + 1, i))]


def pair_names(pairs, rows):
    names = np.full((2, rows), -20.0, np.float32)
    for c, (a, b) in enumerate(pairs):
        names[0, 8 * c : 8 * c + 8] = a
        names[1, 8 * c : 8 * c + 8] = b
    return jnp.asarray(names)


def pair_table(pairs, rows):
    table = np.zeros((2, rows // 8), np.int32)
    table[:, : len(pairs)] = np.array(pairs, np.int32).T
    return jnp.asarray(table)


def local(slc_stack, offsets, kernels, partner, inverse, rate_weights, owners, map_cell):
    date_count, width = slc_stack.shape[1], slc_stack.shape[3]
    groups, strips = lax.axis_size("date"), lax.axis_size("col")
    group, strip = lax.axis_index("date"), lax.axis_index("col")
    rows = [
        jnp.transpose(kernels, (1, 2, 0)).reshape(2 * TAPS, DATES),
        offsets.T.astype(F32),
        jnp.pad(partner.reshape(1, -1).astype(F32), ((0, 0), (0, DATES - partner.shape[0]))),
    ]
    rows.append(jnp.pad(rate_weights.reshape(1, -1), ((0, 0), (0, DATES - rate_weights.shape[0]))))
    facts = jnp.stack([group * date_count, group % 2, strip % 2, group]).astype(F32)
    rows.append(jnp.broadcast_to(facts[:, None], (4, DATES)))
    facts = facts.reshape(1, -1)
    table, at = jnp.zeros((24, DATES), F32), 0
    for part in rows:
        table = table + jnp.pad(part, ((at, 24 - at - part.shape[0]), (0, 0)))
        at += part.shape[0]
    mine = lax.dynamic_slice(table, (0, group * date_count), (table.shape[0], date_count))

    tile = jax.ShapeDtypeStruct((2, ROWS, LANES), BF16)
    tile0, tile1 = pl.pallas_call(
        pack_kernel,
        in_specs=[SMEM, pl.BlockSpec(memory_space=pl.ANY)],
        out_specs=[VMEM] * 2,
        out_shape=[tile, jax.ShapeDtypeStruct((2, ROWS + 8, LANES), BF16)],
        scratch_shapes=[
            pltpu.VMEM((2,) + slc_stack.shape[:3] + (LANES,), BF16),
            pltpu.SemaphoreType.DMA((2,)),
        ],
        compiler_params=pltpu.CompilerParams(vmem_limit_bytes=53 * 1024 * 1024),
    )((strip % 2).astype(jnp.int32).reshape(1), slc_stack)
    own = lax.reduce_precision(slc_stack, 8, 7)
    near = lax.ppermute(tile0, "col", swaps(strips, 0))
    far = lax.ppermute(tile1, "col", swaps(strips, 1))
    (weight,) = call(
        weights_kernel,
        (),
        (inverse,),
        [((DATES, groups * PAIR_ROWS), BF16)],
        [pltpu.VMEM((inverse.shape[1], groups * PAIR_ROWS), BF16)],
    )
    scratch = [
        pltpu.VMEM((2, 2 * ROWS * width // LANES, 2 * LANES), BF16),
        pltpu.VMEM((2, 4 * LANES, 2 * LANES), BF16),
        pltpu.VMEM((2, 2, width // LANES, ROWS, LANES), F32),
    ]
    edge0, edge1 = call(
        edge_kernel,
        (mine,),
        (own, near, far, table),
        [((256, width), BF16)] * 2,
        scratch,
    )
    later = lax.ppermute(edge0, "date", [(i + 1, i) for i in range(groups - 1)])
    earlier = lax.ppermute(edge1, "date", [(i, i + 1) for i in range(groups - 1)])
    window = np.arange(width)[:, None] // LOOK_RG == np.arange(256)[None, :] % (width // LOOK_RG)
    matrix = jnp.asarray(window.astype(np.float32)).astype(BF16)
    inner_rows = 8 * (len(INNER) + 5)
    phase, power, ys = call(
        inner_kernel,
        (mine, pair_table(INNER, inner_rows)),
        (
            own, near, far, edge0, edge1, table, matrix, pair_names(INNER, inner_rows),
            owners.reshape(1, -1), map_cell,
        ),
        [
            ((PAIR_ROWS, 256), F32),
            ((96, 256), F32),
            ((12, 2, ROWS, width), F32),
        ],
        scratch
        + [
            pltpu.VMEM((96, width), F32),
            pltpu.VMEM((inner_rows, width), F32),
            pltpu.VMEM((inner_rows, 256), F32),
        ],
    )
    def boundary(kernel, smem, vmem, pairs, table_pairs, out):
        rows = 8 * (-(-len(pairs) // 8) * 8)
        (result,) = call(
            kernel,
            smem + (pair_table(table_pairs, rows),),
            vmem + (pair_names(pairs, rows),),
            [out],
            [
                pltpu.VMEM((HALF, 2, ROWS, width), F32),
                pltpu.VMEM((rows + 8 * HALF, width), F32),
                pltpu.VMEM((rows, 256), F32),
                pltpu.VMEM((96 + 8 * HALF, 256), F32),
            ],
        )
        return result

    later, weight = lax.optimization_barrier((later, weight))
    phase = boundary(
        after_kernel,
        (facts,),
        (later, ys, power, phase, table, matrix),
        CROSS,
        CROSS,
        ((PAIR_ROWS, 256), F32),
    )
    sent = boundary(
        before_kernel,
        (),
        (earlier, ys, power, phase, matrix),
        BEFORE,
        [(a + 3, b - 12) for a, b in BEFORE],
        ((groups, PAIR_ROWS, 256), BF16),
    )
    phases = lax.all_to_all(sent, "date", 0, 0, tiled=True)
    (routed,) = call(series_kernel, (facts,), (phases, weight), [((8 * strips, 256), BF16)])
    parts = lax.all_to_all(routed.reshape(strips, 8, 256), "col", 0, 0, tiled=True)
    (mean,) = call(final_kernel, (), (parts, table), [((8, DATES), F32)])
    return mean.reshape(1, 8, DATES)


def solution(mesh):
    in_specs = (
        P(None, "date", None, "col"),
        P(),
        P(),
        P("date"),
        P(),
        P(),
        P("col", "date", None),
        P("col", "date"),
    )
    out_specs = P("col", "date", None)
    return jax.shard_map(local, mesh=mesh, in_specs=in_specs, out_specs=out_specs, check_vma=False)
```

```python
import functools

import jax
import jax.numpy as jnp
import numpy as np
from jax import lax
from jax.experimental import pallas as pl
from jax.experimental.pallas import tpu as pltpu
from jax.sharding import PartitionSpec as P

PER_DATE = 3
SPAN = 6
HALF = 3
ROW_BLOCK = 20
TAPS = 8
HALO = 8
LOOK_AZ = 5
LOOK_RG = 20
LROWS = 8
LANES = 128
ROWS = 40
DATES = 192
EXTRA = 9
FACTS = 20
PAIR_ROWS = 48
F32 = jnp.float32
BF16 = jnp.bfloat16
VMEM_BYTES = 24 * 1024 * 1024

INNER = [(a, a + s) for a in range(6) for s in range(1, 7)]
INNER += [(a, b) for a in range(6, 11) for b in range(a + 1, 12)]
CROSS = [(a, b) for b in range(12, 15) for a in range(b - 6, 12)]
BEFORE = [(a, b) for b in range(15, 18) for a in range(b - 6, 12)]


def iota(shape, dim):
    return lax.broadcasted_iota(jnp.int32, shape, dim)


def fact(table, n):
    return (table[0, n] if table.shape[0] == 1 else table[FACTS + n, 0]).astype(jnp.int32)


def partner_row(table, lines):
    return lines[18:19, 0:36] - fact(table, 0).astype(F32)


def tap_weights(table, at, weights):
    lane, row = iota((16, LANES), 1), iota((16, LANES), 0)
    for b in range(2):
        start = LANES + 4 - table[2 * TAPS + b, at].astype(jnp.int32)
        line = jnp.zeros((8, LANES), F32)
        for t in range(TAPS):
            here = iota((8, LANES), 1) == lax.rem(start - t, LANES)
            line = jnp.where(here, table[TAPS * b + t, at], line)
        cols = slice(LANES * b, LANES * b + LANES)
        for m in range(0, LANES, 16):
            both = jnp.concatenate(
                [pltpu.roll(line, m + 8 * i, 1, stride=1, stride_axis=0) for i in range(2)], axis=0
            )
            apart = lane - row - m
            near = (apart < 64) & (apart > -64)
            for at_row, tile in ((m, jnp.where(near, both, 0.0)), (LANES + m, jnp.where(near, 0.0, both))):
                high = tile.astype(BF16)
                weights[at_row : at_row + 16, cols] = high
                weights[256 + at_row : 272 + at_row, cols] = (tile - high.astype(F32)).astype(BF16)


def resample(own, near, far, table, dates, lhs, weights, zs):
    is_odd = fact(table, 2) == 1
    count = own.shape[-1] // LANES
    lane = iota((ROWS, LANES), 1)
    for s, date in enumerate(dates):
        tap_weights(table, date, weights.at[s])
    for s, date in enumerate(dates):
        for part in range(2):
            tile_a, tile_b = near[part].astype(F32), far[part, 0:ROWS].astype(F32)
            left = pltpu.roll(jnp.where(is_odd, tile_a, tile_b), LANES - HALO - HALO * date, 1)
            right = pltpu.roll(
                jnp.where(is_odd, tile_b, tile_a), lax.rem(LANES - HALO * date, LANES), 1
            )
            line = own[part, date].astype(F32)
            tiles = [left] + [line[:, LANES * j : LANES * (j + 1)] for j in range(count)] + [right]
            for j in range(count):
                rows = slice(ROWS * (count * part + j), ROWS * (count * part + j + 1))
                lhs[s, rows, 0:LANES] = own[part, date, :, LANES * j : LANES * (j + 1)]
                lhs[s, rows, LANES : 2 * LANES] = jnp.where(
                    lane < 64, tiles[j + 2], tiles[j]
                ).astype(BF16)
    row = iota((8, LANES), 0)
    outs = []
    for s in range(len(dates)):
        taken = lhs[s]
        outs.append(
            jnp.dot(
                jnp.concatenate([taken, taken], axis=1), weights[s], preferred_element_type=F32
            )
        )
    for s, out in enumerate(outs):
        for part in range(2):
            for j in range(count):
                tile = out[ROWS * (count * part + j) : ROWS * (count * part + j + 1)]
                first, second = tile[:, :LANES], tile[:, LANES:]
                zs[s, part, j, 0:16, :] = first[:16]
                zs[s, part, j, 16:24, :] = jnp.where(row < 4, first[16:24], second[16:24])
                zs[s, part, j, 24:40, :] = second[24:]


def slabs(zs, s):
    for part in range(2):
        for k in range(LOOK_AZ):
            for j in range(zs.shape[2]):
                tile = zs[s, part, j, pl.ds(k, LROWS, stride=LOOK_AZ), :].astype(BF16)
                yield part, k, slice(LANES * j, LANES * (j + 1)), tile


def column(row, rows, offset):
    wide = row.shape[1]
    at = iota((rows, wide), 1) == iota((rows, wide), 0) + offset
    return jnp.sum(jnp.where(at, row, 0.0), axis=1, keepdims=True)


def pack_kernel(odd, own, out0, out1, ends, sems):
    far = own.shape[3] - LANES
    even = odd[0] == 0
    copies = [
        pltpu.make_async_copy(own.at[:, :, :, at : at + LANES], ends.at[n], sems.at[n])
        for n, at in enumerate((0, far))
    ]
    for copy in copies:
        copy.start()
    lane = iota((ROWS, LANES), 1) // HALO
    for copy in copies:
        copy.wait()

    def one(d, totals):
        here = lane == d
        rolled = [
            pltpu.roll(ends[n, part, d].astype(F32), HALO * d + HALO * n, 1)
            for part in range(2)
            for n in range(2)
        ]
        return tuple(jnp.where(here, r, t) for r, t in zip(rolled, totals))

    zero = jnp.zeros((ROWS, LANES), F32)
    totals = lax.fori_loop(0, own.shape[1], one, (zero,) * 4, unroll=4)
    for part in range(2):
        head, tail = totals[2 * part], totals[2 * part + 1]
        out0[part] = jnp.where(even, tail, head).astype(BF16)
        out1[part, 0:ROWS] = jnp.where(even, head, tail).astype(BF16)
        out1[part, ROWS:] = jnp.zeros((8, LANES), BF16)


def edge_kernel(table, own, near, far, lines, head, tail, lhs, weights, zs):
    local = column(partner_row(table, lines), 16, 36 - EXTRA)
    for out in (head, tail):
        out[240:256, :] = jnp.broadcast_to(local, (16, out.shape[1])).astype(BF16)

    def one(i, _):
        dates = (i, i + 9)
        resample(own, near, far, table, dates, lhs, weights, zs)
        for s, out in enumerate((head, tail)):
            for part, k, cols, tile in slabs(zs, s):
                out[pl.ds(pl.multiple_of(i * 80 + part * 40 + k * 8, 8), 8), cols] = tile
        return 0

    lax.fori_loop(0, HALF, one, 0)


def window_sum(values, matrix):
    high = values.astype(BF16)
    low = (values - high.astype(F32)).astype(BF16)
    both = jnp.dot(
        jnp.concatenate([high, low], axis=0), matrix[...], preferred_element_type=F32
    )
    return both[: values.shape[0]] + both[values.shape[0] :]


def cross_sum(first, second):
    total = None
    for k in range(LOOK_AZ):
        re1, im1 = first(0, k), first(1, k)
        re2, im2 = second(0, k), second(1, k)
        term = im1 * re2 - re1 * im2
        total = term if total is None else total + term
    return total


def power_sum(date):
    total = None
    for k in range(LOOK_AZ):
        re, im = date(0, k), date(1, k)
        term = re * re + im * im
        total = term if total is None else total + term
    return total


def phase_of(cross, power_a, power_b, mask):
    scale = 1.0 / (LOOK_AZ * LOOK_RG)
    product = (power_a * scale) * (power_b * scale) + 1e-06
    return jnp.where(mask, (cross * scale) * lax.rsqrt(product), 0.0)


def choose(names, have_a, have_b, reverse):
    a, b = names[0:1, :], names[1:2, :]
    take = ((have_a == a) & (have_b == b)).astype(F32)
    if reverse:
        take = take - ((have_a == b) & (have_b == a)).astype(F32)
    return take.astype(BF16)


def phases_of(pairs, count, pm, powers):
    mask = iota((8, 256), 1) // 32 == iota((8, 256), 0)

    def one(n, _):
        done = []
        for u in range(8):
            c = 8 * n + u
            rows = pl.ds(pl.multiple_of(c * 8, 8), 8)
            row_a = pl.ds(pl.multiple_of(pairs[0, c] * 8, 8), 8)
            row_b = pl.ds(pl.multiple_of(pairs[1, c] * 8, 8), 8)
            done.append(phase_of(pm[rows, :], powers[row_a, :], powers[row_b, :], mask))
        pm[pl.ds(pl.multiple_of(n * 64, 64), 64), :] = jnp.concatenate(done, axis=0)
        return 0

    lax.fori_loop(0, count // 8, one, 0)


def unpack_dates(packed, dates, start):
    def one(n, _):
        both = packed[pl.ds(pl.multiple_of(n * 80, 16), 80), :].astype(F32)
        dates[n + start, 0], dates[n + start, 1] = both[:40], both[40:]
        return 0

    lax.fori_loop(0, HALF, one, 0)


def inner_kernel(
    table, pairs, own, near, far, edge0, edge1, lines, matrix, names, owners, cells,
    phase_out, power_out, ys,
    lhs, weights, zs, ps, ss, pm,
):
    width = own.shape[-1]

    def one_date(n, _):
        dates = (n + 3, n + 6)
        resample(own, near, far, table, dates, lhs, weights, zs)
        for s, d in enumerate(dates):
            for part, k, cols, tile in slabs(zs, s):
                ys[d, part, 8 * k : 8 * k + 8, cols] = tile.astype(F32)
        return 0

    lax.fori_loop(0, HALF, one_date, 0)
    unpack_dates(edge0, ys, 0)
    unpack_dates(edge1, ys, 9)

    def one_power(d, _):
        ps[pl.ds(pl.multiple_of(d * 8, 8), 8), :] = power_sum(reader(d))
        return 0

    def reader(d):
        return lambda part, k: ys[d, part, 8 * k : 8 * k + 8, :]

    lax.fori_loop(0, 12, one_power, 0)

    def one_pair(c, _):
        at = pl.multiple_of(c * 8, 8)
        ss[pl.ds(at, 8), :] = cross_sum(reader(pairs[0, c]), reader(pairs[1, c]))
        return 0

    total = ss.shape[0] // 8
    lax.fori_loop(0, total, one_pair, 0)
    power_out[...] = window_sum(ps[...], matrix)
    block = ss.shape[0] // 2

    def one_block(n, _):
        rows = pl.ds(pl.multiple_of(n * block, 8), block)
        pm[rows, :] = window_sum(ss[rows, :], matrix)
        return 0

    lax.fori_loop(0, 2, one_block, 0)
    phases_of(pairs, total, pm, power_out)
    local = column(partner_row(table, lines), PAIR_ROWS, 0)
    row = iota((PAIR_ROWS, 1), 0)
    have_a = jnp.where(row < 36, row // PER_DATE, -9).astype(F32)
    take = choose(names, have_a, local, True)

    n = owners.shape[1]
    spread = (iota((n, 256), 1) == iota((n, 256), 0) + n * fact(table, 3)).astype(BF16)
    codes = jnp.concatenate([owners[...], cells[...]], axis=0).astype(F32).astype(BF16)
    placed = jnp.dot(codes, spread, preferred_element_type=F32)
    lines = iota((PAIR_ROWS, 256), 0)
    phases = jnp.dot(take, pm[...].astype(BF16), preferred_element_type=F32)
    phases = jnp.where(lines == 46, placed[0:1, :], phases)
    phase_out[...] = jnp.where(lines == 47, placed[1:2, :], phases)


def weights_kernel(inverse, weight_out, gather):
    spots = iota((1, weight_out.shape[1]), 1)
    group, k = spots // PAIR_ROWS, spots % PAIR_ROWS
    target = jnp.where(k < 36, 36 * group + k, jnp.where(k < 45, 36 * group + k - 45, -1))

    def one_rows(n, _):
        at = pl.multiple_of(n * 16, 16)
        gather[pl.ds(at, 16), :] = (iota((16, gather.shape[1]), 0) + at == target).astype(BF16)
        return 0

    lax.fori_loop(0, gather.shape[0] // 16, one_rows, 0)
    weight_out[0:191, :] = jnp.dot(
        inverse[...], gather[...], preferred_element_type=F32
    ).astype(BF16)
    weight_out[191:192, :] = jnp.zeros((1, weight_out.shape[1]), BF16)


def boundary_phases(pairs, count, later, got, ys, power, matrix, rs, ss, pm, pw):
    unpack_dates(got, rs, 0)

    def here(d):
        return lambda part, k: ys[d, part, 8 * k : 8 * k + 8, :]

    def there(d):
        return lambda part, k: rs[d - 12, part, 8 * k : 8 * k + 8, :]

    first, second = (here, there) if later else (there, here)

    def one_pair(c, _):
        at = pl.multiple_of(c * 8, 8)
        ss[pl.ds(at, 8), :] = cross_sum(first(pairs[0, c]), second(pairs[1, c]))
        return 0

    lax.fori_loop(0, count, one_pair, 0)
    rows = pm.shape[0]

    def one_power(n, _):
        ss[pl.ds(pl.multiple_of(rows + n * 8, 8), 8), :] = power_sum(there(n + 12))
        return 0

    lax.fori_loop(0, HALF, one_power, 0)
    ss[count * 8 : rows, :] = jnp.zeros_like(ss[count * 8 : rows, :])
    pw[0:96, :] = power[...]
    sums = window_sum(ss[...], matrix)
    pm[...] = sums[:rows]
    pw[96:120, :] = sums[rows:]
    phases_of(pairs, rows // 8, pm, pw)


def after_kernel(
    facts, pairs, got, ys, power, phase, lines, matrix, names, out, rs, ss, pm, pw
):
    boundary_phases(pairs, len(CROSS), True, got, ys, power, matrix, rs, ss, pm, pw)
    local = column(partner_row(facts, lines), PAIR_ROWS, 0)
    row = iota((PAIR_ROWS, 1), 0)
    have_a = jnp.where(row < 36, row // PER_DATE, -9).astype(F32)
    take = choose(names, have_a, local, False)
    out[...] = phase[...] + jnp.dot(take, pm[...].astype(BF16), preferred_element_type=F32)


def before_kernel(pairs, got, ys, power, phase, matrix, names, out, rs, ss, pm, pw):
    boundary_phases(pairs, len(BEFORE), False, got, ys, power, matrix, rs, ss, pm, pw)
    told = jnp.max(got[240:256, 0:LANES].astype(F32), axis=1, keepdims=True)
    spread = (iota((PAIR_ROWS, 16), 0) - 36 == iota((PAIR_ROWS, 16), 1)).astype(BF16)
    moved = jnp.dot(
        spread, jnp.broadcast_to(told, (16, LANES)).astype(BF16), preferred_element_type=F32
    )[:, 0:1]
    row = iota((PAIR_ROWS, 1), 0)
    theirs = (row >= 36) & (row < 36 + EXTRA)
    have_a = jnp.where(theirs, 9 + (row - 36) // PER_DATE, -9).astype(F32)
    take = choose(names, have_a, jnp.where(theirs, moved, -5.0), False)
    total = phase[...] + jnp.dot(take, pm[...].astype(BF16), preferred_element_type=F32)
    for g in range(out.shape[0]):
        out[g] = total.astype(BF16)


def series_kernel(table, got, weight, out, sums):
    stack = jnp.concatenate([got[g] for g in range(got.shape[0])], axis=0)
    series = jnp.dot(weight[...], stack, preferred_element_type=F32)
    wide = series.shape[1]
    rows = jnp.where(iota(series.shape, 0) == DATES - 1, 1.0, series).astype(BF16)
    none = jnp.zeros_like(rows)
    codes = got[0, 40:48, :].astype(F32)
    for g in range(1, got.shape[0]):
        codes = codes + got[g, 40:48, :].astype(F32)
    owner, cell = codes[6:7, :], codes[7:8, :]
    cell = cell - fact(table, 3).astype(F32) * 8.0
    select = []
    for base in (0.0, 4.0):
        mine = (cell >= base) & (cell < base + 4.0)
        target = jnp.where(mine, owner * 4.0 + cell - base, -1.0).astype(jnp.int32)
        select.append((iota((sums.shape[0], wide), 0) == target).astype(BF16))
    sums[...] = lax.dot_general(
        jnp.concatenate(select, axis=1),
        jnp.concatenate(
            [jnp.concatenate([rows, none], axis=0), jnp.concatenate([none, rows], axis=0)], axis=1
        ),
        (((1,), (1,)), ((), ())),
        preferred_element_type=F32,
    )

    def one(n, _):
        both = sums[pl.ds(pl.multiple_of(8 * n, 8), 8), :].astype(BF16)
        out[2 * n], out[2 * n + 1] = both[:4], both[4:]
        return 0

    lax.fori_loop(0, out.shape[0] // 2, one, 0, unroll=4)


def final_kernel(got, lines, out):
    total = got[0].astype(F32)
    for g in range(1, got.shape[0]):
        total = total + got[g].astype(F32)
    turned = pltpu.roll(total, DATES, 1)
    total = jnp.concatenate([total[:, 0:DATES], turned[:, 0:DATES]], axis=0)
    lane = iota(total.shape, 1)
    counts = jnp.sum(jnp.where(lane == DATES - 1, total, 0.0), axis=1, keepdims=True)
    velocity = jnp.sum(total * lines[19:20, :], axis=1, keepdims=True)
    total = jnp.where(lane == DATES - 1, velocity, total)
    out[...] = total / jnp.maximum(counts, 1.0)


SMEM = pl.BlockSpec(memory_space=pltpu.SMEM)
VMEM = pl.BlockSpec(memory_space=pltpu.VMEM)


def call(kernel, smem, vmem, outs, scratch=()):
    return pl.pallas_call(
        kernel,
        in_specs=[SMEM] * len(smem) + [VMEM] * len(vmem),
        out_specs=[VMEM] * len(outs),
        out_shape=[jax.ShapeDtypeStruct(s, t) for s, t in outs],
        scratch_shapes=list(scratch),
        compiler_params=pltpu.CompilerParams(vmem_limit_bytes=VMEM_BYTES),
    )(*smem, *vmem)


def swaps(count, start):
    return [p for i in range(start, count - 1, 2) for p in ((i, i + 1), (i + 1, i))]


def pair_names(pairs, rows):
    names = np.full((2, rows), -20.0, np.float32)
    for c, (a, b) in enumerate(pairs):
        names[0, 8 * c : 8 * c + 8] = a
        names[1, 8 * c : 8 * c + 8] = b
    return jnp.asarray(names)


def pair_table(pairs, rows):
    table = np.zeros((2, rows // 8), np.int32)
    table[:, : len(pairs)] = np.array(pairs, np.int32).T
    return jnp.asarray(table)


def local(slc_stack, offsets, kernels, partner, inverse, rate_weights, owners, map_cell):
    date_count, width = slc_stack.shape[1], slc_stack.shape[3]
    groups, strips = lax.axis_size("date"), lax.axis_size("col")
    group, strip = lax.axis_index("date"), lax.axis_index("col")
    rows = [
        jnp.transpose(kernels, (1, 2, 0)).reshape(2 * TAPS, DATES),
        offsets.T.astype(F32),
        jnp.pad(partner.reshape(1, -1).astype(F32), ((0, 0), (0, DATES - partner.shape[0]))),
    ]
    rows.append(jnp.pad(rate_weights.reshape(1, -1), ((0, 0), (0, DATES - rate_weights.shape[0]))))
    facts = jnp.stack([group * date_count, group % 2, strip % 2, group]).astype(F32)
    rows.append(jnp.broadcast_to(facts[:, None], (4, DATES)))
    facts = facts.reshape(1, -1)
    table, at = jnp.zeros((24, DATES), F32), 0
    for part in rows:
        table = table + jnp.pad(part, ((at, 24 - at - part.shape[0]), (0, 0)))
        at += part.shape[0]
    mine = lax.dynamic_slice(table, (0, group * date_count), (table.shape[0], date_count))

    tile = jax.ShapeDtypeStruct((2, ROWS, LANES), BF16)
    tile0, tile1 = pl.pallas_call(
        pack_kernel,
        in_specs=[SMEM, pl.BlockSpec(memory_space=pl.ANY)],
        out_specs=[VMEM] * 2,
        out_shape=[tile, jax.ShapeDtypeStruct((2, ROWS + 8, LANES), BF16)],
        scratch_shapes=[
            pltpu.VMEM((2,) + slc_stack.shape[:3] + (LANES,), BF16),
            pltpu.SemaphoreType.DMA((2,)),
        ],
        compiler_params=pltpu.CompilerParams(vmem_limit_bytes=53 * 1024 * 1024),
    )((strip % 2).astype(jnp.int32).reshape(1), slc_stack)
    own = lax.reduce_precision(slc_stack, 8, 7)
    near = lax.ppermute(tile0, "col", swaps(strips, 0))
    far = lax.ppermute(tile1, "col", swaps(strips, 1))
    (weight,) = call(
        weights_kernel,
        (),
        (inverse,),
        [((DATES, groups * PAIR_ROWS), BF16)],
        [pltpu.VMEM((inverse.shape[1], groups * PAIR_ROWS), BF16)],
    )
    scratch = [
        pltpu.VMEM((2, 2 * ROWS * width // LANES, 2 * LANES), BF16),
        pltpu.VMEM((2, 4 * LANES, 2 * LANES), BF16),
        pltpu.VMEM((2, 2, width // LANES, ROWS, LANES), F32),
    ]
    edge0, edge1 = call(
        edge_kernel,
        (mine,),
        (own, near, far, table),
        [((256, width), BF16)] * 2,
        scratch,
    )
    later = lax.ppermute(edge0, "date", [(i + 1, i) for i in range(groups - 1)])
    earlier = lax.ppermute(edge1, "date", [(i, i + 1) for i in range(groups - 1)])
    window = np.arange(width)[:, None] // LOOK_RG == np.arange(256)[None, :] % (width // LOOK_RG)
    matrix = jnp.asarray(window.astype(np.float32)).astype(BF16)
    inner_rows = 8 * (len(INNER) + 5)
    phase, power, ys = call(
        inner_kernel,
        (mine, pair_table(INNER, inner_rows)),
        (
            own, near, far, edge0, edge1, table, matrix, pair_names(INNER, inner_rows),
            owners.reshape(1, -1), map_cell,
        ),
        [
            ((PAIR_ROWS, 256), F32),
            ((96, 256), F32),
            ((12, 2, ROWS, width), F32),
        ],
        scratch
        + [
            pltpu.VMEM((96, width), F32),
            pltpu.VMEM((inner_rows, width), F32),
            pltpu.VMEM((inner_rows, 256), F32),
        ],
    )
    def boundary(kernel, smem, vmem, pairs, table_pairs, out):
        rows = 8 * (-(-len(pairs) // 8) * 8)
        (result,) = call(
            kernel,
            smem + (pair_table(table_pairs, rows),),
            vmem + (pair_names(pairs, rows),),
            [out],
            [
                pltpu.VMEM((HALF, 2, ROWS, width), F32),
                pltpu.VMEM((rows + 8 * HALF, width), F32),
                pltpu.VMEM((rows, 256), F32),
                pltpu.VMEM((96 + 8 * HALF, 256), F32),
            ],
        )
        return result

    later, weight = lax.optimization_barrier((later, weight))
    phase = boundary(
        after_kernel,
        (facts,),
        (later, ys, power, phase, table, matrix),
        CROSS,
        CROSS,
        ((PAIR_ROWS, 256), F32),
    )
    sent = boundary(
        before_kernel,
        (),
        (earlier, ys, power, phase, matrix),
        BEFORE,
        [(a + 3, b - 12) for a, b in BEFORE],
        ((groups, PAIR_ROWS, 256), BF16),
    )
    phases = lax.all_to_all(sent, "date", 0, 0, tiled=True)
    (routed,) = call(
        series_kernel,
        (facts,),
        (phases, weight),
        [((strips, 4, 2 * DATES), BF16)],
        [pltpu.VMEM((4 * strips, 2 * DATES), F32)],
    )
    parts = lax.all_to_all(routed, "col", 0, 0, tiled=True)
    (mean,) = call(final_kernel, (), (parts, table), [((8, DATES), F32)])
    return mean.reshape(1, 8, DATES)


def solution(mesh):
    in_specs = (
        P(None, "date", None, "col"),
        P(),
        P(),
        P("date"),
        P(),
        P(),
        P("col", "date", None),
        P("col", "date"),
    )
    out_specs = P("col", "date", None)
    return jax.shard_map(local, mesh=mesh, in_specs=in_specs, out_specs=out_specs, check_vma=False)
```

```python
import functools

import jax
import jax.numpy as jnp
import numpy as np
from jax import lax
from jax.experimental import pallas as pl
from jax.experimental.pallas import tpu as pltpu
from jax.sharding import PartitionSpec as P

PER_DATE = 3
SPAN = 6
HALF = 3
ROW_BLOCK = 20
TAPS = 8
HALO = 8
LOOK_AZ = 5
LOOK_RG = 20
LROWS = 8
LANES = 128
ROWS = 40
DATES = 192
EXTRA = 9
FACTS = 20
PAIR_ROWS = 48
F32 = jnp.float32
BF16 = jnp.bfloat16
VMEM_BYTES = 24 * 1024 * 1024

INNER = [(a, a + s) for a in range(6) for s in range(1, 7)]
INNER += [(a, b) for a in range(6, 11) for b in range(a + 1, 12)]
CROSS = [(a, b) for b in range(12, 15) for a in range(b - 6, 12)]
BEFORE = [(a, b) for b in range(15, 18) for a in range(b - 6, 12)]


def iota(shape, dim):
    return lax.broadcasted_iota(jnp.int32, shape, dim)


def fact(table, n):
    return (table[0, n] if table.shape[0] == 1 else table[FACTS + n, 0]).astype(jnp.int32)


def partner_row(table, lines):
    return lines[18:19, 0:36] - fact(table, 0).astype(F32)


def tap_weights(table, at, weights):
    lane, row = iota((16, LANES), 1), iota((16, LANES), 0)
    for b in range(2):
        start = LANES + 4 - table[2 * TAPS + b, at].astype(jnp.int32)
        line = jnp.zeros((8, LANES), F32)
        for t in range(TAPS):
            here = iota((8, LANES), 1) == lax.rem(start - t, LANES)
            line = jnp.where(here, table[TAPS * b + t, at], line)
        cols = slice(LANES * b, LANES * b + LANES)
        for m in range(0, LANES, 16):
            both = jnp.concatenate(
                [pltpu.roll(line, m + 8 * i, 1, stride=1, stride_axis=0) for i in range(2)], axis=0
            )
            apart = lane - row - m
            near = (apart < 64) & (apart > -64)
            for at_row, tile in ((m, jnp.where(near, both, 0.0)), (LANES + m, jnp.where(near, 0.0, both))):
                high = tile.astype(BF16)
                weights[at_row : at_row + 16, cols] = high
                weights[256 + at_row : 272 + at_row, cols] = (tile - high.astype(F32)).astype(BF16)


def resample(own, near, far, table, dates, lhs, weights, zs):
    is_odd = fact(table, 2) == 1
    count = own.shape[-1] // LANES
    lane = iota((ROWS, LANES), 1)
    for s, date in enumerate(dates):
        tap_weights(table, date, weights.at[s])
    for s, date in enumerate(dates):
        for part in range(2):
            tile_a, tile_b = near[part].astype(F32), far[part, 0:ROWS].astype(F32)
            left = pltpu.roll(jnp.where(is_odd, tile_a, tile_b), LANES - HALO - HALO * date, 1)
            right = pltpu.roll(
                jnp.where(is_odd, tile_b, tile_a), lax.rem(LANES - HALO * date, LANES), 1
            )
            line = own[part, date].astype(F32)
            tiles = [left] + [line[:, LANES * j : LANES * (j + 1)] for j in range(count)] + [right]
            for j in range(count):
                rows = slice(ROWS * (count * part + j), ROWS * (count * part + j + 1))
                lhs[s, rows, 0:LANES] = own[part, date, :, LANES * j : LANES * (j + 1)]
                lhs[s, rows, LANES : 2 * LANES] = jnp.where(
                    lane < 64, tiles[j + 2], tiles[j]
                ).astype(BF16)
    row = iota((8, LANES), 0)
    outs = []
    for s in range(len(dates)):
        taken = lhs[s]
        outs.append(
            jnp.dot(
                jnp.concatenate([taken, taken], axis=1), weights[s], preferred_element_type=F32
            )
        )
    for s, out in enumerate(outs):
        for part in range(2):
            for j in range(count):
                tile = out[ROWS * (count * part + j) : ROWS * (count * part + j + 1)]
                first, second = tile[:, :LANES], tile[:, LANES:]
                zs[s, part, j, 0:16, :] = first[:16]
                zs[s, part, j, 16:24, :] = jnp.where(row < 4, first[16:24], second[16:24])
                zs[s, part, j, 24:40, :] = second[24:]


def slabs(zs, s):
    for part in range(2):
        for k in range(LOOK_AZ):
            for j in range(zs.shape[2]):
                tile = zs[s, part, j, pl.ds(k, LROWS, stride=LOOK_AZ), :].astype(BF16)
                yield part, k, slice(LANES * j, LANES * (j + 1)), tile


def column(row, rows, offset):
    wide = row.shape[1]
    at = iota((rows, wide), 1) == iota((rows, wide), 0) + offset
    return jnp.sum(jnp.where(at, row, 0.0), axis=1, keepdims=True)


def pack_kernel(odd, own, out0, out1, ends, sems):
    far = own.shape[3] - LANES
    even = odd[0] == 0
    copies = [
        pltpu.make_async_copy(own.at[:, :, :, at : at + LANES], ends.at[n], sems.at[n])
        for n, at in enumerate((0, far))
    ]
    for copy in copies:
        copy.start()
    lane = iota((ROWS, LANES), 1) // HALO
    for copy in copies:
        copy.wait()

    def one(d, totals):
        here = lane == d
        rolled = [
            pltpu.roll(ends[n, part, d].astype(F32), HALO * d + HALO * n, 1)
            for part in range(2)
            for n in range(2)
        ]
        return tuple(jnp.where(here, r, t) for r, t in zip(rolled, totals))

    zero = jnp.zeros((ROWS, LANES), F32)
    totals = lax.fori_loop(0, own.shape[1], one, (zero,) * 4, unroll=4)
    for part in range(2):
        head, tail = totals[2 * part], totals[2 * part + 1]
        out0[part] = jnp.where(even, tail, head).astype(BF16)
        out1[part, 0:ROWS] = jnp.where(even, head, tail).astype(BF16)
        out1[part, ROWS:] = jnp.zeros((8, LANES), BF16)


def edge_kernel(table, own, near, far, lines, head, tail, lhs, weights, zs):
    local = column(partner_row(table, lines), 16, 36 - EXTRA)
    for out in (head, tail):
        out[240:248, 0:LANES] = jnp.broadcast_to(local[0:8], (8, LANES)).astype(BF16)
        rest = (8, out.shape[1] - LANES)
        out[240:248, LANES:] = jnp.broadcast_to(local[8:9], rest).astype(BF16)

    def one(i, _):
        dates = (i, i + 9)
        resample(own, near, far, table, dates, lhs, weights, zs)
        for s, out in enumerate((head, tail)):
            for part, k, cols, tile in slabs(zs, s):
                out[pl.ds(pl.multiple_of(i * 80 + part * 40 + k * 8, 8), 8), cols] = tile
        return 0

    lax.fori_loop(0, HALF, one, 0)


def window_sum(values, matrix):
    high = values.astype(BF16)
    low = (values - high.astype(F32)).astype(BF16)
    both = jnp.dot(
        jnp.concatenate([high, low], axis=0), matrix[...], preferred_element_type=F32
    )
    return both[: values.shape[0]] + both[values.shape[0] :]


def cross_sum(first, second):
    total = None
    for k in range(LOOK_AZ):
        re1, im1 = first(0, k), first(1, k)
        re2, im2 = second(0, k), second(1, k)
        term = im1 * re2 - re1 * im2
        total = term if total is None else total + term
    return total


def power_sum(date):
    total = None
    for k in range(LOOK_AZ):
        re, im = date(0, k), date(1, k)
        term = re * re + im * im
        total = term if total is None else total + term
    return total


def phase_of(cross, power_a, power_b, mask):
    scale = 1.0 / (LOOK_AZ * LOOK_RG)
    product = (power_a * scale) * (power_b * scale) + 1e-06
    return jnp.where(mask, (cross * scale) * lax.rsqrt(product), 0.0)


def choose(names, have_a, have_b, reverse):
    a, b = names[0:1, :], names[1:2, :]
    take = ((have_a == a) & (have_b == b)).astype(F32)
    if reverse:
        take = take - ((have_a == b) & (have_b == a)).astype(F32)
    return take.astype(BF16)


def phases_of(pairs, count, pm, powers):
    mask = iota((8, 256), 1) // 32 == iota((8, 256), 0)

    def one(n, _):
        done = []
        for u in range(8):
            c = 8 * n + u
            rows = pl.ds(pl.multiple_of(c * 8, 8), 8)
            row_a = pl.ds(pl.multiple_of(pairs[0, c] * 8, 8), 8)
            row_b = pl.ds(pl.multiple_of(pairs[1, c] * 8, 8), 8)
            done.append(phase_of(pm[rows, :], powers[row_a, :], powers[row_b, :], mask))
        pm[pl.ds(pl.multiple_of(n * 64, 64), 64), :] = jnp.concatenate(done, axis=0)
        return 0

    lax.fori_loop(0, count // 8, one, 0)


def unpack_dates(packed, dates, start):
    def one(n, _):
        both = packed[pl.ds(pl.multiple_of(n * 80, 16), 80), :].astype(F32)
        dates[n + start, 0], dates[n + start, 1] = both[:40], both[40:]
        return 0

    lax.fori_loop(0, HALF, one, 0)


def inner_kernel(
    table, pairs, own, near, far, edge0, edge1, lines, matrix, names, owners, cells,
    phase_out, power_out, ys,
    lhs, weights, zs, ps, ss, pm,
):
    width = own.shape[-1]

    def one_date(n, _):
        dates = (n + 3, n + 6)
        resample(own, near, far, table, dates, lhs, weights, zs)
        for s, d in enumerate(dates):
            for part, k, cols, tile in slabs(zs, s):
                ys[d, part, 8 * k : 8 * k + 8, cols] = tile.astype(F32)
        return 0

    lax.fori_loop(0, HALF, one_date, 0)
    unpack_dates(edge0, ys, 0)
    unpack_dates(edge1, ys, 9)

    def one_power(d, _):
        ps[pl.ds(pl.multiple_of(d * 8, 8), 8), :] = power_sum(reader(d))
        return 0

    def reader(d):
        return lambda part, k: ys[d, part, 8 * k : 8 * k + 8, :]

    lax.fori_loop(0, 12, one_power, 0)

    def one_pair(c, _):
        at = pl.multiple_of(c * 8, 8)
        ss[pl.ds(at, 8), :] = cross_sum(reader(pairs[0, c]), reader(pairs[1, c]))
        return 0

    total = ss.shape[0] // 8
    lax.fori_loop(0, total, one_pair, 0)
    power_out[...] = window_sum(ps[...], matrix)
    block = ss.shape[0] // 2

    def one_block(n, _):
        rows = pl.ds(pl.multiple_of(n * block, 8), block)
        pm[rows, :] = window_sum(ss[rows, :], matrix)
        return 0

    lax.fori_loop(0, 2, one_block, 0)
    phases_of(pairs, total, pm, power_out)
    local = column(partner_row(table, lines), PAIR_ROWS, 0)
    row = iota((PAIR_ROWS, 1), 0)
    have_a = jnp.where(row < 36, row // PER_DATE, -9).astype(F32)
    take = choose(names, have_a, local, True)

    n = owners.shape[1]
    spread = (iota((n, 256), 1) == iota((n, 256), 0) + n * fact(table, 3)).astype(BF16)
    codes = jnp.concatenate([owners[...], cells[...]], axis=0).astype(F32).astype(BF16)
    placed = jnp.dot(codes, spread, preferred_element_type=F32)
    lines = iota((PAIR_ROWS, 256), 0)
    phases = jnp.dot(take, pm[...].astype(BF16), preferred_element_type=F32)
    phases = jnp.where(lines == 46, placed[0:1, :], phases)
    phase_out[...] = jnp.where(lines == 47, placed[1:2, :], phases)


def weights_kernel(inverse, weight_out, gather):
    spots = iota((1, weight_out.shape[1]), 1)
    group, k = spots // PAIR_ROWS, spots % PAIR_ROWS
    target = jnp.where(k < 36, 36 * group + k, jnp.where(k < 45, 36 * group + k - 45, -1))

    def one_rows(n, _):
        at = pl.multiple_of(n * 16, 16)
        gather[pl.ds(at, 16), :] = (iota((16, gather.shape[1]), 0) + at == target).astype(BF16)
        return 0

    lax.fori_loop(0, gather.shape[0] // 16, one_rows, 0)
    weight_out[0:191, :] = jnp.dot(
        inverse[...], gather[...], preferred_element_type=F32
    ).astype(BF16)
    weight_out[191:192, :] = jnp.zeros((1, weight_out.shape[1]), BF16)


def boundary_phases(pairs, count, later, got, ys, power, matrix, rs, ss, pm, pw):
    unpack_dates(got, rs, 0)

    def here(d):
        return lambda part, k: ys[d, part, 8 * k : 8 * k + 8, :]

    def there(d):
        return lambda part, k: rs[d - 12, part, 8 * k : 8 * k + 8, :]

    first, second = (here, there) if later else (there, here)

    def one_pair(c, _):
        at = pl.multiple_of(c * 8, 8)
        ss[pl.ds(at, 8), :] = cross_sum(first(pairs[0, c]), second(pairs[1, c]))
        return 0

    lax.fori_loop(0, count, one_pair, 0)
    rows = pm.shape[0]

    def one_power(n, _):
        ss[pl.ds(pl.multiple_of(rows + n * 8, 8), 8), :] = power_sum(there(n + 12))
        return 0

    lax.fori_loop(0, HALF, one_power, 0)
    ss[count * 8 : rows, :] = jnp.zeros_like(ss[count * 8 : rows, :])
    pw[0:96, :] = power[...]
    sums = window_sum(ss[...], matrix)
    pm[...] = sums[:rows]
    pw[96:120, :] = sums[rows:]
    phases_of(pairs, rows // 8, pm, pw)


def after_kernel(
    facts, pairs, got, ys, power, phase, lines, matrix, names, out, rs, ss, pm, pw
):
    boundary_phases(pairs, len(CROSS), True, got, ys, power, matrix, rs, ss, pm, pw)
    local = column(partner_row(facts, lines), PAIR_ROWS, 0)
    row = iota((PAIR_ROWS, 1), 0)
    have_a = jnp.where(row < 36, row // PER_DATE, -9).astype(F32)
    take = choose(names, have_a, local, False)
    out[...] = phase[...] + jnp.dot(take, pm[...].astype(BF16), preferred_element_type=F32)


def before_kernel(pairs, got, ys, power, phase, matrix, names, out, rs, ss, pm, pw):
    boundary_phases(pairs, len(BEFORE), False, got, ys, power, matrix, rs, ss, pm, pw)
    told = jnp.concatenate(
        [got[240:248, 0:LANES].astype(F32), got[240:248, LANES : 2 * LANES].astype(F32)], axis=0
    )
    told = jnp.max(told, axis=1, keepdims=True)
    spread = (iota((PAIR_ROWS, 16), 0) - 36 == iota((PAIR_ROWS, 16), 1)).astype(BF16)
    moved = jnp.dot(
        spread, jnp.broadcast_to(told, (16, LANES)).astype(BF16), preferred_element_type=F32
    )[:, 0:1]
    row = iota((PAIR_ROWS, 1), 0)
    theirs = (row >= 36) & (row < 36 + EXTRA)
    have_a = jnp.where(theirs, 9 + (row - 36) // PER_DATE, -9).astype(F32)
    take = choose(names, have_a, jnp.where(theirs, moved, -5.0), False)
    total = phase[...] + jnp.dot(take, pm[...].astype(BF16), preferred_element_type=F32)
    for g in range(out.shape[0]):
        out[g] = total.astype(BF16)


def series_kernel(table, got, weight, out, sums):
    stack = jnp.concatenate([got[g] for g in range(got.shape[0])], axis=0)
    series = jnp.dot(weight[...], stack, preferred_element_type=F32)
    wide = series.shape[1]
    rows = jnp.where(iota(series.shape, 0) == DATES - 1, 1.0, series).astype(BF16)
    none = jnp.zeros_like(rows)
    codes = got[0, 40:48, :].astype(F32)
    for g in range(1, got.shape[0]):
        codes = codes + got[g, 40:48, :].astype(F32)
    owner, cell = codes[6:7, :], codes[7:8, :]
    cell = cell - fact(table, 3).astype(F32) * 8.0
    select = []
    for base in (0.0, 4.0):
        mine = (cell >= base) & (cell < base + 4.0)
        target = jnp.where(mine, owner * 4.0 + cell - base, -1.0).astype(jnp.int32)
        select.append((iota((sums.shape[0], wide), 0) == target).astype(BF16))
    sums[...] = lax.dot_general(
        jnp.concatenate(select, axis=1),
        jnp.concatenate(
            [jnp.concatenate([rows, none], axis=0), jnp.concatenate([none, rows], axis=0)], axis=1
        ),
        (((1,), (1,)), ((), ())),
        preferred_element_type=F32,
    )

    def one(n, _):
        both = sums[pl.ds(pl.multiple_of(8 * n, 8), 8), :].astype(BF16)
        out[2 * n], out[2 * n + 1] = both[:4], both[4:]
        return 0

    lax.fori_loop(0, out.shape[0] // 2, one, 0, unroll=4)


def final_kernel(got, lines, out):
    total = got[0].astype(F32)
    for g in range(1, got.shape[0]):
        total = total + got[g].astype(F32)
    turned = pltpu.roll(total, DATES, 1)
    total = jnp.concatenate([total[:, 0:DATES], turned[:, 0:DATES]], axis=0)
    lane = iota(total.shape, 1)
    counts = jnp.sum(jnp.where(lane == DATES - 1, total, 0.0), axis=1, keepdims=True)
    velocity = jnp.sum(total * lines[19:20, :], axis=1, keepdims=True)
    total = jnp.where(lane == DATES - 1, velocity, total)
    out[...] = total / jnp.maximum(counts, 1.0)


SMEM = pl.BlockSpec(memory_space=pltpu.SMEM)
VMEM = pl.BlockSpec(memory_space=pltpu.VMEM)


def call(kernel, smem, vmem, outs, scratch=()):
    return pl.pallas_call(
        kernel,
        in_specs=[SMEM] * len(smem) + [VMEM] * len(vmem),
        out_specs=[VMEM] * len(outs),
        out_shape=[jax.ShapeDtypeStruct(s, t) for s, t in outs],
        scratch_shapes=list(scratch),
        compiler_params=pltpu.CompilerParams(vmem_limit_bytes=VMEM_BYTES),
    )(*smem, *vmem)


def swaps(count, start):
    return [p for i in range(start, count - 1, 2) for p in ((i, i + 1), (i + 1, i))]


def pair_names(pairs, rows):
    names = np.full((2, rows), -20.0, np.float32)
    for c, (a, b) in enumerate(pairs):
        names[0, 8 * c : 8 * c + 8] = a
        names[1, 8 * c : 8 * c + 8] = b
    return jnp.asarray(names)


def pair_table(pairs, rows):
    table = np.zeros((2, rows // 8), np.int32)
    table[:, : len(pairs)] = np.array(pairs, np.int32).T
    return jnp.asarray(table)


def local(slc_stack, offsets, kernels, partner, inverse, rate_weights, owners, map_cell):
    date_count, width = slc_stack.shape[1], slc_stack.shape[3]
    groups, strips = lax.axis_size("date"), lax.axis_size("col")
    group, strip = lax.axis_index("date"), lax.axis_index("col")
    rows = [
        jnp.transpose(kernels, (1, 2, 0)).reshape(2 * TAPS, DATES),
        offsets.T.astype(F32),
        jnp.pad(partner.reshape(1, -1).astype(F32), ((0, 0), (0, DATES - partner.shape[0]))),
    ]
    rows.append(jnp.pad(rate_weights.reshape(1, -1), ((0, 0), (0, DATES - rate_weights.shape[0]))))
    facts = jnp.stack([group * date_count, group % 2, strip % 2, group]).astype(F32)
    rows.append(jnp.broadcast_to(facts[:, None], (4, DATES)))
    facts = facts.reshape(1, -1)
    table, at = jnp.zeros((24, DATES), F32), 0
    for part in rows:
        table = table + jnp.pad(part, ((at, 24 - at - part.shape[0]), (0, 0)))
        at += part.shape[0]
    mine = lax.dynamic_slice(table, (0, group * date_count), (table.shape[0], date_count))

    tile = jax.ShapeDtypeStruct((2, ROWS, LANES), BF16)
    tile0, tile1 = pl.pallas_call(
        pack_kernel,
        in_specs=[SMEM, pl.BlockSpec(memory_space=pl.ANY)],
        out_specs=[VMEM] * 2,
        out_shape=[tile, jax.ShapeDtypeStruct((2, ROWS + 8, LANES), BF16)],
        scratch_shapes=[
            pltpu.VMEM((2,) + slc_stack.shape[:3] + (LANES,), BF16),
            pltpu.SemaphoreType.DMA((2,)),
        ],
        compiler_params=pltpu.CompilerParams(vmem_limit_bytes=53 * 1024 * 1024),
    )((strip % 2).astype(jnp.int32).reshape(1), slc_stack)
    own = lax.reduce_precision(slc_stack, 8, 7)
    near = lax.ppermute(tile0, "col", swaps(strips, 0))
    far = lax.ppermute(tile1, "col", swaps(strips, 1))
    (weight,) = call(
        weights_kernel,
        (),
        (inverse,),
        [((DATES, groups * PAIR_ROWS), BF16)],
        [pltpu.VMEM((inverse.shape[1], groups * PAIR_ROWS), BF16)],
    )
    scratch = [
        pltpu.VMEM((2, 2 * ROWS * width // LANES, 2 * LANES), BF16),
        pltpu.VMEM((2, 4 * LANES, 2 * LANES), BF16),
        pltpu.VMEM((2, 2, width // LANES, ROWS, LANES), F32),
    ]
    edge0, edge1 = call(
        edge_kernel,
        (mine,),
        (own, near, far, table),
        [((248, width), BF16)] * 2,
        scratch,
    )
    later = lax.ppermute(edge0, "date", [(i + 1, i) for i in range(groups - 1)])
    earlier = lax.ppermute(edge1, "date", [(i, i + 1) for i in range(groups - 1)])
    window = np.arange(width)[:, None] // LOOK_RG == np.arange(256)[None, :] % (width // LOOK_RG)
    matrix = jnp.asarray(window.astype(np.float32)).astype(BF16)
    inner_rows = 8 * (len(INNER) + 5)
    phase, power, ys = call(
        inner_kernel,
        (mine, pair_table(INNER, inner_rows)),
        (
            own, near, far, edge0, edge1, table, matrix, pair_names(INNER, inner_rows),
            owners.reshape(1, -1), map_cell,
        ),
        [
            ((PAIR_ROWS, 256), F32),
            ((96, 256), F32),
            ((12, 2, ROWS, width), F32),
        ],
        scratch
        + [
            pltpu.VMEM((96, width), F32),
            pltpu.VMEM((inner_rows, width), F32),
            pltpu.VMEM((inner_rows, 256), F32),
        ],
    )
    def boundary(kernel, smem, vmem, pairs, table_pairs, out):
        rows = 8 * (-(-len(pairs) // 8) * 8)
        (result,) = call(
            kernel,
            smem + (pair_table(table_pairs, rows),),
            vmem + (pair_names(pairs, rows),),
            [out],
            [
                pltpu.VMEM((HALF, 2, ROWS, width), F32),
                pltpu.VMEM((rows + 8 * HALF, width), F32),
                pltpu.VMEM((rows, 256), F32),
                pltpu.VMEM((96 + 8 * HALF, 256), F32),
            ],
        )
        return result

    later, weight = lax.optimization_barrier((later, weight))
    phase = boundary(
        after_kernel,
        (facts,),
        (later, ys, power, phase, table, matrix),
        CROSS,
        CROSS,
        ((PAIR_ROWS, 256), F32),
    )
    sent = boundary(
        before_kernel,
        (),
        (earlier, ys, power, phase, matrix),
        BEFORE,
        [(a + 3, b - 12) for a, b in BEFORE],
        ((groups, PAIR_ROWS, 256), BF16),
    )
    phases = lax.all_to_all(sent, "date", 0, 0, tiled=True)
    (routed,) = call(
        series_kernel,
        (facts,),
        (phases, weight),
        [((strips, 4, 2 * DATES), BF16)],
        [pltpu.VMEM((4 * strips, 2 * DATES), F32)],
    )
    parts = lax.all_to_all(routed, "col", 0, 0, tiled=True)
    (mean,) = call(final_kernel, (), (parts, table), [((8, DATES), F32)])
    return mean.reshape(1, 8, DATES)


def solution(mesh):
    in_specs = (
        P(None, "date", None, "col"),
        P(),
        P(),
        P("date"),
        P(),
        P(),
        P("col", "date", None),
        P("col", "date"),
    )
    out_specs = P("col", "date", None)
    return jax.shard_map(local, mesh=mesh, in_specs=in_specs, out_specs=out_specs, check_vma=False)
```

```python
import functools

import jax
import jax.numpy as jnp
import numpy as np
from jax import lax
from jax.experimental import pallas as pl
from jax.experimental.pallas import tpu as pltpu
from jax.sharding import PartitionSpec as P

PER_DATE = 3
SPAN = 6
HALF = 3
ROW_BLOCK = 20
TAPS = 8
HALO = 8
LOOK_AZ = 5
LOOK_RG = 20
LROWS = 8
LANES = 128
ROWS = 40
DATES = 192
EXTRA = 9
FACTS = 20
PAIR_ROWS = 48
F32 = jnp.float32
BF16 = jnp.bfloat16
VMEM_BYTES = 24 * 1024 * 1024

INNER = [(a, a + s) for a in range(6) for s in range(1, 7)]
INNER += [(a, b) for a in range(6, 11) for b in range(a + 1, 12)]
CROSS = [(a, b) for b in range(12, 15) for a in range(b - 6, 12)]
BEFORE = [(a, b) for b in range(15, 18) for a in range(b - 6, 12)]


def iota(shape, dim):
    return lax.broadcasted_iota(jnp.int32, shape, dim)


def fact(table, n):
    return (table[0, n] if table.shape[0] == 1 else table[FACTS + n, 0]).astype(jnp.int32)


def partner_row(table, lines):
    return lines[18:19, 0:36] - fact(table, 0).astype(F32)


def tap_weights(table, at, weights):
    lane, row = iota((16, LANES), 1), iota((16, LANES), 0)
    for b in range(2):
        start = LANES + 4 - table[2 * TAPS + b, at].astype(jnp.int32)
        line = jnp.zeros((8, LANES), F32)
        for t in range(TAPS):
            here = iota((8, LANES), 1) == lax.rem(start - t, LANES)
            line = jnp.where(here, table[TAPS * b + t, at], line)
        cols = slice(LANES * b, LANES * b + LANES)
        for m in range(0, LANES, 16):
            both = jnp.concatenate(
                [pltpu.roll(line, m + 8 * i, 1, stride=1, stride_axis=0) for i in range(2)], axis=0
            )
            apart = lane - row - m
            near = (apart < 64) & (apart > -64)
            for at_row, tile in ((m, jnp.where(near, both, 0.0)), (LANES + m, jnp.where(near, 0.0, both))):
                high = tile.astype(BF16)
                weights[at_row : at_row + 16, cols] = high
                weights[256 + at_row : 272 + at_row, cols] = (tile - high.astype(F32)).astype(BF16)


def resample(own, near, far, table, dates, lhs, weights, zs):
    is_odd = fact(table, 2) == 1
    count = own.shape[-1] // LANES
    lane = iota((ROWS, LANES), 1)
    for s, date in enumerate(dates):
        tap_weights(table, date, weights.at[s])
    for s, date in enumerate(dates):
        for part in range(2):
            tile_a, tile_b = near[part].astype(F32), far[part, 0:ROWS].astype(F32)
            left = pltpu.roll(jnp.where(is_odd, tile_a, tile_b), LANES - HALO - HALO * date, 1)
            right = pltpu.roll(
                jnp.where(is_odd, tile_b, tile_a), lax.rem(LANES - HALO * date, LANES), 1
            )
            line = own[part, date].astype(F32)
            tiles = [left] + [line[:, LANES * j : LANES * (j + 1)] for j in range(count)] + [right]
            for j in range(count):
                rows = slice(ROWS * (count * part + j), ROWS * (count * part + j + 1))
                lhs[s, rows, 0:LANES] = own[part, date, :, LANES * j : LANES * (j + 1)]
                lhs[s, rows, LANES : 2 * LANES] = jnp.where(
                    lane < 64, tiles[j + 2], tiles[j]
                ).astype(BF16)
    row = iota((8, LANES), 0)
    outs = []
    for s in range(len(dates)):
        taken = lhs[s]
        outs.append(
            jnp.dot(
                jnp.concatenate([taken, taken], axis=1), weights[s], preferred_element_type=F32
            )
        )
    for s, out in enumerate(outs):
        for part in range(2):
            for j in range(count):
                tile = out[ROWS * (count * part + j) : ROWS * (count * part + j + 1)]
                first, second = tile[:, :LANES], tile[:, LANES:]
                zs[s, part, j, 0:16, :] = first[:16]
                zs[s, part, j, 16:24, :] = jnp.where(row < 4, first[16:24], second[16:24])
                zs[s, part, j, 24:40, :] = second[24:]


def slabs(zs, s):
    for part in range(2):
        for k in range(LOOK_AZ):
            for j in range(zs.shape[2]):
                tile = zs[s, part, j, pl.ds(k, LROWS, stride=LOOK_AZ), :].astype(BF16)
                yield part, k, slice(LANES * j, LANES * (j + 1)), tile


def column(row, rows, offset):
    wide = row.shape[1]
    at = iota((rows, wide), 1) == iota((rows, wide), 0) + offset
    return jnp.sum(jnp.where(at, row, 0.0), axis=1, keepdims=True)


def pack_kernel(odd, own, out0, out1, ends, sems):
    far = own.shape[3] - LANES
    even = odd[0] == 0
    copies = [
        pltpu.make_async_copy(own.at[:, :, :, at : at + LANES], ends.at[n], sems.at[n])
        for n, at in enumerate((0, far))
    ]
    for copy in copies:
        copy.start()
    lane = iota((ROWS, LANES), 1) // HALO
    for copy in copies:
        copy.wait()

    def one(d, totals):
        here = lane == d
        rolled = [
            pltpu.roll(ends[n, part, d].astype(F32), HALO * d + HALO * n, 1)
            for part in range(2)
            for n in range(2)
        ]
        return tuple(jnp.where(here, r, t) for r, t in zip(rolled, totals))

    zero = jnp.zeros((ROWS, LANES), F32)
    totals = lax.fori_loop(0, own.shape[1], one, (zero,) * 4, unroll=4)
    for part in range(2):
        head, tail = totals[2 * part], totals[2 * part + 1]
        out0[part] = jnp.where(even, tail, head).astype(BF16)
        out1[part, 0:ROWS] = jnp.where(even, head, tail).astype(BF16)
        out1[part, ROWS:] = jnp.zeros((8, LANES), BF16)


def edge_kernel(table, own, near, far, lines, head, tail, lhs, weights, zs):
    local = column(partner_row(table, lines), 16, 36 - EXTRA)
    for out in (head, tail):
        out[240:256, :] = jnp.broadcast_to(local, (16, out.shape[1])).astype(BF16)

    def one(i, _):
        dates = (i, i + 9)
        resample(own, near, far, table, dates, lhs, weights, zs)
        for s, out in enumerate((head, tail)):
            for part, k, cols, tile in slabs(zs, s):
                out[pl.ds(pl.multiple_of(i * 80 + part * 40 + k * 8, 8), 8), cols] = tile
        return 0

    lax.fori_loop(0, HALF, one, 0)


def window_sum(values, matrix):
    high = values.astype(BF16)
    low = (values - high.astype(F32)).astype(BF16)
    both = jnp.dot(
        jnp.concatenate([high, low], axis=0), matrix[...], preferred_element_type=F32
    )
    return both[: values.shape[0]] + both[values.shape[0] :]


def cross_sum(first, second):
    total = None
    for k in range(LOOK_AZ):
        re1, im1 = first(0, k), first(1, k)
        re2, im2 = second(0, k), second(1, k)
        term = im1 * re2 - re1 * im2
        total = term if total is None else total + term
    return total


def power_sum(date):
    total = None
    for k in range(LOOK_AZ):
        re, im = date(0, k), date(1, k)
        term = re * re + im * im
        total = term if total is None else total + term
    return total


def phase_of(cross, power_a, power_b, mask):
    scale = 1.0 / (LOOK_AZ * LOOK_RG)
    product = (power_a * scale) * (power_b * scale) + 1e-06
    return jnp.where(mask, (cross * scale) * lax.rsqrt(product), 0.0)


def choose(names, have_a, have_b, reverse):
    a, b = names[0:1, :], names[1:2, :]
    take = ((have_a == a) & (have_b == b)).astype(F32)
    if reverse:
        take = take - ((have_a == b) & (have_b == a)).astype(F32)
    return take.astype(BF16)


def phases_of(pairs, count, pm, powers):
    mask = iota((8, 256), 1) // 32 == iota((8, 256), 0)

    def one(n, _):
        done = []
        for u in range(8):
            c = 8 * n + u
            rows = pl.ds(pl.multiple_of(c * 8, 8), 8)
            row_a = pl.ds(pl.multiple_of(pairs[0, c] * 8, 8), 8)
            row_b = pl.ds(pl.multiple_of(pairs[1, c] * 8, 8), 8)
            done.append(phase_of(pm[rows, :], powers[row_a, :], powers[row_b, :], mask))
        pm[pl.ds(pl.multiple_of(n * 64, 64), 64), :] = jnp.concatenate(done, axis=0)
        return 0

    lax.fori_loop(0, count // 8, one, 0)


def unpack_dates(packed, dates, start):
    def one(n, _):
        both = packed[pl.ds(pl.multiple_of(n * 80, 16), 80), :].astype(F32)
        dates[n + start, 0], dates[n + start, 1] = both[:40], both[40:]
        return 0

    lax.fori_loop(0, HALF, one, 0)


def inner_kernel(
    table, pairs, own, near, far, edge0, edge1, lines, matrix, names, owners, cells,
    phase_out, power_out, ys,
    lhs, weights, zs, ss, pm,
):
    width = own.shape[-1]

    def one_date(n, _):
        dates = (n + 3, n + 6)
        resample(own, near, far, table, dates, lhs, weights, zs)
        for s, d in enumerate(dates):
            for part, k, cols, tile in slabs(zs, s):
                ys[d, part, 8 * k : 8 * k + 8, cols] = tile.astype(F32)
        return 0

    lax.fori_loop(0, HALF, one_date, 0)
    unpack_dates(edge0, ys, 0)
    unpack_dates(edge1, ys, 9)

    powers = 8 * len(INNER)

    def one_power(d, _):
        ss[pl.ds(pl.multiple_of(powers + d * 8, 8), 8), :] = power_sum(reader(d))
        return 0

    def reader(d):
        return lambda part, k: ys[d, part, 8 * k : 8 * k + 8, :]

    lax.fori_loop(0, 12, one_power, 0)

    def one_pair(c, _):
        at = pl.multiple_of(c * 8, 8)
        ss[pl.ds(at, 8), :] = cross_sum(reader(pairs[0, c]), reader(pairs[1, c]))
        return 0

    lax.fori_loop(0, len(INNER), one_pair, 0)
    ss[powers + 96 :, :] = jnp.zeros_like(ss[powers + 96 :, :])
    block = ss.shape[0] // 2

    def one_block(n, _):
        rows = pl.ds(pl.multiple_of(n * block, 8), block)
        pm[rows, :] = window_sum(ss[rows, :], matrix)
        return 0

    lax.fori_loop(0, 2, one_block, 0)
    power_out[...] = pm[powers : powers + 96, :]
    total = names.shape[1]
    phases_of(pairs, total // 8, pm, power_out)
    local = column(partner_row(table, lines), PAIR_ROWS, 0)
    row = iota((PAIR_ROWS, 1), 0)
    have_a = jnp.where(row < 36, row // PER_DATE, -9).astype(F32)
    take = choose(names, have_a, local, True)

    n = owners.shape[1]
    spread = (iota((n, 256), 1) == iota((n, 256), 0) + n * fact(table, 3)).astype(BF16)
    codes = jnp.concatenate([owners[...], cells[...]], axis=0).astype(F32).astype(BF16)
    placed = jnp.dot(codes, spread, preferred_element_type=F32)
    lines = iota((PAIR_ROWS, 256), 0)
    phases = jnp.dot(take, pm[:total, :].astype(BF16), preferred_element_type=F32)
    phases = jnp.where(lines == 46, placed[0:1, :], phases)
    phase_out[...] = jnp.where(lines == 47, placed[1:2, :], phases)


def weights_kernel(inverse, weight_out, gather):
    spots = iota((1, weight_out.shape[1]), 1)
    group, k = spots // PAIR_ROWS, spots % PAIR_ROWS
    target = jnp.where(k < 36, 36 * group + k, jnp.where(k < 45, 36 * group + k - 45, -1))

    def one_rows(n, _):
        at = pl.multiple_of(n * 16, 16)
        gather[pl.ds(at, 16), :] = (iota((16, gather.shape[1]), 0) + at == target).astype(BF16)
        return 0

    lax.fori_loop(0, gather.shape[0] // 16, one_rows, 0)
    weight_out[0:191, :] = jnp.dot(
        inverse[...], gather[...], preferred_element_type=F32
    ).astype(BF16)
    weight_out[191:192, :] = jnp.zeros((1, weight_out.shape[1]), BF16)


def boundary_phases(pairs, count, later, got, ys, power, matrix, rs, ss, pm, pw):
    unpack_dates(got, rs, 0)

    def here(d):
        return lambda part, k: ys[d, part, 8 * k : 8 * k + 8, :]

    def there(d):
        return lambda part, k: rs[d - 12, part, 8 * k : 8 * k + 8, :]

    first, second = (here, there) if later else (there, here)

    def one_pair(c, _):
        at = pl.multiple_of(c * 8, 8)
        ss[pl.ds(at, 8), :] = cross_sum(first(pairs[0, c]), second(pairs[1, c]))
        return 0

    lax.fori_loop(0, count, one_pair, 0)
    rows = pm.shape[0]

    def one_power(n, _):
        ss[pl.ds(pl.multiple_of(rows + n * 8, 8), 8), :] = power_sum(there(n + 12))
        return 0

    lax.fori_loop(0, HALF, one_power, 0)
    ss[count * 8 : rows, :] = jnp.zeros_like(ss[count * 8 : rows, :])
    pw[0:96, :] = power[...]
    sums = window_sum(ss[...], matrix)
    pm[...] = sums[:rows]
    pw[96:120, :] = sums[rows:]
    phases_of(pairs, rows // 8, pm, pw)


def after_kernel(
    facts, pairs, got, ys, power, phase, lines, matrix, names, out, rs, ss, pm, pw
):
    boundary_phases(pairs, len(CROSS), True, got, ys, power, matrix, rs, ss, pm, pw)
    local = column(partner_row(facts, lines), PAIR_ROWS, 0)
    row = iota((PAIR_ROWS, 1), 0)
    have_a = jnp.where(row < 36, row // PER_DATE, -9).astype(F32)
    take = choose(names, have_a, local, False)
    out[...] = phase[...] + jnp.dot(take, pm[...].astype(BF16), preferred_element_type=F32)


def before_kernel(pairs, got, ys, power, phase, matrix, names, out, rs, ss, pm, pw):
    boundary_phases(pairs, len(BEFORE), False, got, ys, power, matrix, rs, ss, pm, pw)
    told = jnp.max(got[240:256, 0:LANES].astype(F32), axis=1, keepdims=True)
    spread = (iota((PAIR_ROWS, 16), 0) - 36 == iota((PAIR_ROWS, 16), 1)).astype(BF16)
    moved = jnp.dot(
        spread, jnp.broadcast_to(told, (16, LANES)).astype(BF16), preferred_element_type=F32
    )[:, 0:1]
    row = iota((PAIR_ROWS, 1), 0)
    theirs = (row >= 36) & (row < 36 + EXTRA)
    have_a = jnp.where(theirs, 9 + (row - 36) // PER_DATE, -9).astype(F32)
    take = choose(names, have_a, jnp.where(theirs, moved, -5.0), False)
    total = phase[...] + jnp.dot(take, pm[...].astype(BF16), preferred_element_type=F32)
    for g in range(out.shape[0]):
        out[g] = total.astype(BF16)


def series_kernel(table, got, weight, out, sums):
    stack = jnp.concatenate([got[g] for g in range(got.shape[0])], axis=0)
    series = jnp.dot(weight[...], stack, preferred_element_type=F32)
    wide = series.shape[1]
    rows = jnp.where(iota(series.shape, 0) == DATES - 1, 1.0, series).astype(BF16)
    none = jnp.zeros_like(rows)
    codes = got[0, 40:48, :].astype(F32)
    for g in range(1, got.shape[0]):
        codes = codes + got[g, 40:48, :].astype(F32)
    owner, cell = codes[6:7, :], codes[7:8, :]
    cell = cell - fact(table, 3).astype(F32) * 8.0
    select = []
    for base in (0.0, 4.0):
        mine = (cell >= base) & (cell < base + 4.0)
        target = jnp.where(mine, owner * 4.0 + cell - base, -1.0).astype(jnp.int32)
        select.append((iota((sums.shape[0], wide), 0) == target).astype(BF16))
    sums[...] = lax.dot_general(
        jnp.concatenate(select, axis=1),
        jnp.concatenate(
            [jnp.concatenate([rows, none], axis=0), jnp.concatenate([none, rows], axis=0)], axis=1
        ),
        (((1,), (1,)), ((), ())),
        preferred_element_type=F32,
    )

    def one(n, _):
        both = sums[pl.ds(pl.multiple_of(8 * n, 8), 8), :].astype(BF16)
        out[2 * n], out[2 * n + 1] = both[:4], both[4:]
        return 0

    lax.fori_loop(0, out.shape[0] // 2, one, 0, unroll=4)


def final_kernel(got, lines, out):
    total = got[0].astype(F32)
    for g in range(1, got.shape[0]):
        total = total + got[g].astype(F32)
    turned = pltpu.roll(total, DATES, 1)
    total = jnp.concatenate([total[:, 0:DATES], turned[:, 0:DATES]], axis=0)
    lane = iota(total.shape, 1)
    counts = jnp.sum(jnp.where(lane == DATES - 1, total, 0.0), axis=1, keepdims=True)
    velocity = jnp.sum(total * lines[19:20, :], axis=1, keepdims=True)
    total = jnp.where(lane == DATES - 1, velocity, total)
    out[...] = total / jnp.maximum(counts, 1.0)


SMEM = pl.BlockSpec(memory_space=pltpu.SMEM)
VMEM = pl.BlockSpec(memory_space=pltpu.VMEM)


def call(kernel, smem, vmem, outs, scratch=()):
    return pl.pallas_call(
        kernel,
        in_specs=[SMEM] * len(smem) + [VMEM] * len(vmem),
        out_specs=[VMEM] * len(outs),
        out_shape=[jax.ShapeDtypeStruct(s, t) for s, t in outs],
        scratch_shapes=list(scratch),
        compiler_params=pltpu.CompilerParams(vmem_limit_bytes=VMEM_BYTES),
    )(*smem, *vmem)


def swaps(count, start):
    return [p for i in range(start, count - 1, 2) for p in ((i, i + 1), (i + 1, i))]


def pair_names(pairs, rows):
    names = np.full((2, rows), -20.0, np.float32)
    for c, (a, b) in enumerate(pairs):
        names[0, 8 * c : 8 * c + 8] = a
        names[1, 8 * c : 8 * c + 8] = b
    return jnp.asarray(names)


def pair_table(pairs, rows):
    table = np.zeros((2, rows // 8), np.int32)
    table[:, : len(pairs)] = np.array(pairs, np.int32).T
    return jnp.asarray(table)


def local(slc_stack, offsets, kernels, partner, inverse, rate_weights, owners, map_cell):
    date_count, width = slc_stack.shape[1], slc_stack.shape[3]
    groups, strips = lax.axis_size("date"), lax.axis_size("col")
    group, strip = lax.axis_index("date"), lax.axis_index("col")
    rows = [
        jnp.transpose(kernels, (1, 2, 0)).reshape(2 * TAPS, DATES),
        offsets.T.astype(F32),
        jnp.pad(partner.reshape(1, -1).astype(F32), ((0, 0), (0, DATES - partner.shape[0]))),
    ]
    rows.append(jnp.pad(rate_weights.reshape(1, -1), ((0, 0), (0, DATES - rate_weights.shape[0]))))
    facts = jnp.stack([group * date_count, group % 2, strip % 2, group]).astype(F32)
    rows.append(jnp.broadcast_to(facts[:, None], (4, DATES)))
    facts = facts.reshape(1, -1)
    table, at = jnp.zeros((24, DATES), F32), 0
    for part in rows:
        table = table + jnp.pad(part, ((at, 24 - at - part.shape[0]), (0, 0)))
        at += part.shape[0]
    mine = lax.dynamic_slice(table, (0, group * date_count), (table.shape[0], date_count))

    tile = jax.ShapeDtypeStruct((2, ROWS, LANES), BF16)
    tile0, tile1 = pl.pallas_call(
        pack_kernel,
        in_specs=[SMEM, pl.BlockSpec(memory_space=pl.ANY)],
        out_specs=[VMEM] * 2,
        out_shape=[tile, jax.ShapeDtypeStruct((2, ROWS + 8, LANES), BF16)],
        scratch_shapes=[
            pltpu.VMEM((2,) + slc_stack.shape[:3] + (LANES,), BF16),
            pltpu.SemaphoreType.DMA((2,)),
        ],
        compiler_params=pltpu.CompilerParams(vmem_limit_bytes=53 * 1024 * 1024),
    )((strip % 2).astype(jnp.int32).reshape(1), slc_stack)
    own = lax.reduce_precision(slc_stack, 8, 7)
    near = lax.ppermute(tile0, "col", swaps(strips, 0))
    far = lax.ppermute(tile1, "col", swaps(strips, 1))
    (weight,) = call(
        weights_kernel,
        (),
        (inverse,),
        [((DATES, groups * PAIR_ROWS), BF16)],
        [pltpu.VMEM((inverse.shape[1], groups * PAIR_ROWS), BF16)],
    )
    scratch = [
        pltpu.VMEM((2, 2 * ROWS * width // LANES, 2 * LANES), BF16),
        pltpu.VMEM((2, 4 * LANES, 2 * LANES), BF16),
        pltpu.VMEM((2, 2, width // LANES, ROWS, LANES), F32),
    ]
    edge0, edge1 = call(
        edge_kernel,
        (mine,),
        (own, near, far, table),
        [((256, width), BF16)] * 2,
        scratch,
    )
    later = lax.ppermute(edge0, "date", [(i + 1, i) for i in range(groups - 1)])
    earlier = lax.ppermute(edge1, "date", [(i, i + 1) for i in range(groups - 1)])
    window = np.arange(width)[:, None] // LOOK_RG == np.arange(256)[None, :] % (width // LOOK_RG)
    matrix = jnp.asarray(window.astype(np.float32)).astype(BF16)
    inner_rows = 8 * (len(INNER) + 5)
    phase, power, ys = call(
        inner_kernel,
        (mine, pair_table(INNER, inner_rows)),
        (
            own, near, far, edge0, edge1, table, matrix, pair_names(INNER, inner_rows),
            owners.reshape(1, -1), map_cell,
        ),
        [
            ((PAIR_ROWS, 256), F32),
            ((96, 256), F32),
            ((12, 2, ROWS, width), F32),
        ],
        scratch
        + [
            pltpu.VMEM((8 * len(INNER) + 104, width), F32),
            pltpu.VMEM((8 * len(INNER) + 104, 256), F32),
        ],
    )
    def boundary(kernel, smem, vmem, pairs, table_pairs, out):
        rows = 8 * (-(-len(pairs) // 8) * 8)
        (result,) = call(
            kernel,
            smem + (pair_table(table_pairs, rows),),
            vmem + (pair_names(pairs, rows),),
            [out],
            [
                pltpu.VMEM((HALF, 2, ROWS, width), F32),
                pltpu.VMEM((rows + 8 * HALF, width), F32),
                pltpu.VMEM((rows, 256), F32),
                pltpu.VMEM((96 + 8 * HALF, 256), F32),
            ],
        )
        return result

    later, weight = lax.optimization_barrier((later, weight))
    phase = boundary(
        after_kernel,
        (facts,),
        (later, ys, power, phase, table, matrix),
        CROSS,
        CROSS,
        ((PAIR_ROWS, 256), F32),
    )
    sent = boundary(
        before_kernel,
        (),
        (earlier, ys, power, phase, matrix),
        BEFORE,
        [(a + 3, b - 12) for a, b in BEFORE],
        ((groups, PAIR_ROWS, 256), BF16),
    )
    phases = lax.all_to_all(sent, "date", 0, 0, tiled=True)
    (routed,) = call(
        series_kernel,
        (facts,),
        (phases, weight),
        [((strips, 4, 2 * DATES), BF16)],
        [pltpu.VMEM((4 * strips, 2 * DATES), F32)],
    )
    parts = lax.all_to_all(routed, "col", 0, 0, tiled=True)
    (mean,) = call(final_kernel, (), (parts, table), [((8, DATES), F32)])
    return mean.reshape(1, 8, DATES)


def solution(mesh):
    in_specs = (
        P(None, "date", None, "col"),
        P(),
        P(),
        P("date"),
        P(),
        P(),
        P("col", "date", None),
        P("col", "date"),
    )
    out_specs = P("col", "date", None)
    return jax.shard_map(local, mesh=mesh, in_specs=in_specs, out_specs=out_specs, check_vma=False)
```

```python
import functools

import jax
import jax.numpy as jnp
import numpy as np
from jax import lax
from jax.experimental import pallas as pl
from jax.experimental.pallas import tpu as pltpu
from jax.sharding import PartitionSpec as P

PER_DATE = 3
SPAN = 6
HALF = 3
ROW_BLOCK = 20
TAPS = 8
HALO = 8
LOOK_AZ = 5
LOOK_RG = 20
LROWS = 8
LANES = 128
ROWS = 40
DATES = 192
EXTRA = 9
FACTS = 20
PAIR_ROWS = 48
F32 = jnp.float32
BF16 = jnp.bfloat16
VMEM_BYTES = 24 * 1024 * 1024

INNER = [(a, a + s) for a in range(6) for s in range(1, 7)]
INNER += [(a, b) for a in range(6, 11) for b in range(a + 1, 12)]
CROSS = [(a, b) for b in range(12, 15) for a in range(b - 6, 12)]
BEFORE = [(a, b) for b in range(15, 18) for a in range(b - 6, 12)]


def iota(shape, dim):
    return lax.broadcasted_iota(jnp.int32, shape, dim)


def fact(table, n):
    return (table[0, n] if table.shape[0] == 1 else table[FACTS + n, 0]).astype(jnp.int32)


def partner_row(table, lines):
    return lines[18:19, 0:36] - fact(table, 0).astype(F32)


def tap_weights(table, at, weights):
    lane, row = iota((16, LANES), 1), iota((16, LANES), 0)
    for b in range(2):
        start = LANES + 4 - table[2 * TAPS + b, at].astype(jnp.int32)
        line = jnp.zeros((8, LANES), F32)
        for t in range(TAPS):
            here = iota((8, LANES), 1) == lax.rem(start - t, LANES)
            line = jnp.where(here, table[TAPS * b + t, at], line)
        cols = slice(LANES * b, LANES * b + LANES)
        for m in range(0, LANES, 16):
            both = jnp.concatenate(
                [pltpu.roll(line, m + 8 * i, 1, stride=1, stride_axis=0) for i in range(2)], axis=0
            )
            apart = lane - row - m
            near = (apart < 64) & (apart > -64)
            for at_row, tile in ((m, jnp.where(near, both, 0.0)), (LANES + m, jnp.where(near, 0.0, both))):
                high = tile.astype(BF16)
                weights[at_row : at_row + 16, cols] = high
                weights[256 + at_row : 272 + at_row, cols] = (tile - high.astype(F32)).astype(BF16)


def resample(own, near, far, table, dates, lhs, weights, zs):
    is_odd = fact(table, 2) == 1
    count = own.shape[-1] // LANES
    lane = iota((ROWS, LANES), 1)
    for s, date in enumerate(dates):
        tap_weights(table, date, weights.at[s])
    for s, date in enumerate(dates):
        for part in range(2):
            tile_a, tile_b = near[part].astype(F32), far[part, 0:ROWS].astype(F32)
            left = pltpu.roll(jnp.where(is_odd, tile_a, tile_b), LANES - HALO - HALO * date, 1)
            right = pltpu.roll(
                jnp.where(is_odd, tile_b, tile_a), lax.rem(LANES - HALO * date, LANES), 1
            )
            line = own[part, date].astype(F32)
            tiles = [left] + [line[:, LANES * j : LANES * (j + 1)] for j in range(count)] + [right]
            for j in range(count):
                rows = slice(ROWS * (count * part + j), ROWS * (count * part + j + 1))
                lhs[s, rows, 0:LANES] = own[part, date, :, LANES * j : LANES * (j + 1)]
                lhs[s, rows, LANES : 2 * LANES] = jnp.where(
                    lane < 64, tiles[j + 2], tiles[j]
                ).astype(BF16)
    row = iota((8, LANES), 0)
    outs = []
    for s in range(len(dates)):
        taken = lhs[s]
        outs.append(
            jnp.dot(
                jnp.concatenate([taken, taken], axis=1), weights[s], preferred_element_type=F32
            )
        )
    for s, out in enumerate(outs):
        for part in range(2):
            for j in range(count):
                tile = out[ROWS * (count * part + j) : ROWS * (count * part + j + 1)]
                first, second = tile[:, :LANES], tile[:, LANES:]
                zs[s, part, j, 0:16, :] = first[:16]
                zs[s, part, j, 16:24, :] = jnp.where(row < 4, first[16:24], second[16:24])
                zs[s, part, j, 24:40, :] = second[24:]


def slabs(zs, s):
    for part in range(2):
        for k in range(LOOK_AZ):
            for j in range(zs.shape[2]):
                tile = zs[s, part, j, pl.ds(k, LROWS, stride=LOOK_AZ), :].astype(BF16)
                yield part, k, slice(LANES * j, LANES * (j + 1)), tile


def column(row, rows, offset):
    wide = row.shape[1]
    at = iota((rows, wide), 1) == iota((rows, wide), 0) + offset
    return jnp.sum(jnp.where(at, row, 0.0), axis=1, keepdims=True)


def pack_kernel(odd, own, out0, out1, ends, sems):
    far = own.shape[3] - LANES
    even = odd[0] == 0
    copies = [
        pltpu.make_async_copy(own.at[:, :, :, at : at + LANES], ends.at[n], sems.at[n])
        for n, at in enumerate((0, far))
    ]
    for copy in copies:
        copy.start()
    lane = iota((ROWS, LANES), 1) // HALO
    for copy in copies:
        copy.wait()

    def one(d, totals):
        here = lane == d
        rolled = [
            pltpu.roll(ends[n, part, d].astype(F32), HALO * d + HALO * n, 1)
            for part in range(2)
            for n in range(2)
        ]
        return tuple(jnp.where(here, r, t) for r, t in zip(rolled, totals))

    zero = jnp.zeros((ROWS, LANES), F32)
    totals = lax.fori_loop(0, own.shape[1], one, (zero,) * 4, unroll=4)
    for part in range(2):
        head, tail = totals[2 * part], totals[2 * part + 1]
        out0[part] = jnp.where(even, tail, head).astype(BF16)
        out1[part, 0:ROWS] = jnp.where(even, head, tail).astype(BF16)
        out1[part, ROWS:] = jnp.zeros((8, LANES), BF16)


def edge_kernel(table, own, near, far, lines, head, tail, lhs, weights, zs):
    local = column(partner_row(table, lines), 16, 36 - EXTRA)
    for out in (head, tail):
        out[240:256, :] = jnp.broadcast_to(local, (16, out.shape[1])).astype(BF16)

    def one(i, _):
        dates = (i, i + 9)
        resample(own, near, far, table, dates, lhs, weights, zs)
        for s, out in enumerate((head, tail)):
            for part, k, cols, tile in slabs(zs, s):
                out[pl.ds(pl.multiple_of(i * 80 + part * 40 + k * 8, 8), 8), cols] = tile
        return 0

    lax.fori_loop(0, HALF, one, 0)


def window_sum(values, matrix):
    high = values.astype(BF16)
    low = (values - high.astype(F32)).astype(BF16)
    both = jnp.dot(
        jnp.concatenate([high, low], axis=0), matrix[...], preferred_element_type=F32
    )
    return both[: values.shape[0]] + both[values.shape[0] :]


def cross_sum(first, second):
    total = None
    for k in range(LOOK_AZ):
        re1, im1 = first(0, k), first(1, k)
        re2, im2 = second(0, k), second(1, k)
        term = im1 * re2 - re1 * im2
        total = term if total is None else total + term
    return total


def power_sum(date):
    total = None
    for k in range(LOOK_AZ):
        re, im = date(0, k), date(1, k)
        term = re * re + im * im
        total = term if total is None else total + term
    return total


def phase_of(cross, power_a, power_b, mask):
    scale = 1.0 / (LOOK_AZ * LOOK_RG)
    product = (power_a * scale) * (power_b * scale) + 1e-06
    return jnp.where(mask, (cross * scale) * lax.rsqrt(product), 0.0)


def choose(names, have_a, have_b, reverse):
    a, b = names[0:1, :], names[1:2, :]
    take = ((have_a == a) & (have_b == b)).astype(F32)
    if reverse:
        take = take - ((have_a == b) & (have_b == a)).astype(F32)
    return take.astype(BF16)


def phases_of(pairs, count, pm, powers):
    mask = iota((8, 256), 1) // 32 == iota((8, 256), 0)

    def one(n, _):
        done = []
        for u in range(8):
            c = 8 * n + u
            rows = pl.ds(pl.multiple_of(c * 8, 8), 8)
            row_a = pl.ds(pl.multiple_of(pairs[0, c] * 8, 8), 8)
            row_b = pl.ds(pl.multiple_of(pairs[1, c] * 8, 8), 8)
            done.append(phase_of(pm[rows, :], powers[row_a, :], powers[row_b, :], mask))
        pm[pl.ds(pl.multiple_of(n * 64, 64), 64), :] = jnp.concatenate(done, axis=0)
        return 0

    lax.fori_loop(0, count // 8, one, 0)


def unpack_dates(packed, dates, start):
    def one(n, _):
        both = packed[pl.ds(pl.multiple_of(n * 80, 16), 80), :].astype(F32)
        dates[n + start, 0], dates[n + start, 1] = both[:40], both[40:]
        return 0

    lax.fori_loop(0, HALF, one, 0)


def inner_kernel(
    table, pairs, own, near, far, edge0, edge1, lines, matrix, names, owners, cells,
    phase_out, power_out, ys,
    lhs, weights, zs, ss, pm,
):
    width = own.shape[-1]

    def one_date(n, _):
        dates = (n + 3, n + 6)
        resample(own, near, far, table, dates, lhs, weights, zs)
        for s, d in enumerate(dates):
            for part, k, cols, tile in slabs(zs, s):
                ys[d, part, 8 * k : 8 * k + 8, cols] = tile.astype(F32)
        return 0

    lax.fori_loop(0, HALF, one_date, 0)
    unpack_dates(edge0, ys, 0)
    unpack_dates(edge1, ys, 9)

    powers = 8 * len(INNER)

    def one_power(d, _):
        ss[pl.ds(pl.multiple_of(powers + d * 8, 8), 8), :] = power_sum(reader(d))
        return 0

    def reader(d):
        return lambda part, k: ys[d, part, 8 * k : 8 * k + 8, :]

    lax.fori_loop(0, 12, one_power, 0, unroll=2)

    def one_pair(c, _):
        at = pl.multiple_of(c * 8, 8)
        ss[pl.ds(at, 8), :] = cross_sum(reader(pairs[0, c]), reader(pairs[1, c]))
        return 0

    lax.fori_loop(0, len(INNER), one_pair, 0)
    ss[powers + 96 :, :] = jnp.zeros_like(ss[powers + 96 :, :])
    block = ss.shape[0] // 2

    def one_block(n, _):
        rows = pl.ds(pl.multiple_of(n * block, 8), block)
        pm[rows, :] = window_sum(ss[rows, :], matrix)
        return 0

    lax.fori_loop(0, 2, one_block, 0)
    power_out[...] = pm[powers : powers + 96, :]
    total = names.shape[1]
    phases_of(pairs, total // 8, pm, power_out)
    local = column(partner_row(table, lines), PAIR_ROWS, 0)
    row = iota((PAIR_ROWS, 1), 0)
    have_a = jnp.where(row < 36, row // PER_DATE, -9).astype(F32)
    take = choose(names, have_a, local, True)

    n = owners.shape[1]
    spread = (iota((n, 256), 1) == iota((n, 256), 0) + n * fact(table, 3)).astype(BF16)
    codes = jnp.concatenate([owners[...], cells[...]], axis=0).astype(F32).astype(BF16)
    placed = jnp.dot(codes, spread, preferred_element_type=F32)
    lines = iota((PAIR_ROWS, 256), 0)
    phases = jnp.dot(take, pm[:total, :].astype(BF16), preferred_element_type=F32)
    phases = jnp.where(lines == 46, placed[0:1, :], phases)
    phase_out[...] = jnp.where(lines == 47, placed[1:2, :], phases)


def weights_kernel(inverse, weight_out, gather):
    spots = iota((1, weight_out.shape[1]), 1)
    group, k = spots // PAIR_ROWS, spots % PAIR_ROWS
    target = jnp.where(k < 36, 36 * group + k, jnp.where(k < 45, 36 * group + k - 45, -1))

    def one_rows(n, _):
        at = pl.multiple_of(n * 16, 16)
        gather[pl.ds(at, 16), :] = (iota((16, gather.shape[1]), 0) + at == target).astype(BF16)
        return 0

    lax.fori_loop(0, gather.shape[0] // 16, one_rows, 0, unroll=4)
    weight_out[0:191, :] = jnp.dot(
        inverse[...], gather[...], preferred_element_type=F32
    ).astype(BF16)
    weight_out[191:192, :] = jnp.zeros((1, weight_out.shape[1]), BF16)


def boundary_phases(pairs, count, later, got, ys, power, matrix, rs, ss, pm, pw):
    unpack_dates(got, rs, 0)

    def here(d):
        return lambda part, k: ys[d, part, 8 * k : 8 * k + 8, :]

    def there(d):
        return lambda part, k: rs[d - 12, part, 8 * k : 8 * k + 8, :]

    first, second = (here, there) if later else (there, here)

    def one_pair(c, _):
        at = pl.multiple_of(c * 8, 8)
        ss[pl.ds(at, 8), :] = cross_sum(first(pairs[0, c]), second(pairs[1, c]))
        return 0

    lax.fori_loop(0, count, one_pair, 0)
    rows = pm.shape[0]

    def one_power(n, _):
        ss[pl.ds(pl.multiple_of(rows + n * 8, 8), 8), :] = power_sum(there(n + 12))
        return 0

    lax.fori_loop(0, HALF, one_power, 0)
    ss[count * 8 : rows, :] = jnp.zeros_like(ss[count * 8 : rows, :])
    pw[0:96, :] = power[...]
    sums = window_sum(ss[...], matrix)
    pm[...] = sums[:rows]
    pw[96:120, :] = sums[rows:]
    phases_of(pairs, rows // 8, pm, pw)


def after_kernel(
    facts, pairs, got, ys, power, phase, lines, matrix, names, out, rs, ss, pm, pw
):
    boundary_phases(pairs, len(CROSS), True, got, ys, power, matrix, rs, ss, pm, pw)
    local = column(partner_row(facts, lines), PAIR_ROWS, 0)
    row = iota((PAIR_ROWS, 1), 0)
    have_a = jnp.where(row < 36, row // PER_DATE, -9).astype(F32)
    take = choose(names, have_a, local, False)
    out[...] = phase[...] + jnp.dot(take, pm[...].astype(BF16), preferred_element_type=F32)


def before_kernel(pairs, got, ys, power, phase, matrix, names, out, rs, ss, pm, pw):
    boundary_phases(pairs, len(BEFORE), False, got, ys, power, matrix, rs, ss, pm, pw)
    told = jnp.max(got[240:256, 0:LANES].astype(F32), axis=1, keepdims=True)
    spread = (iota((PAIR_ROWS, 16), 0) - 36 == iota((PAIR_ROWS, 16), 1)).astype(BF16)
    moved = jnp.dot(
        spread, jnp.broadcast_to(told, (16, LANES)).astype(BF16), preferred_element_type=F32
    )[:, 0:1]
    row = iota((PAIR_ROWS, 1), 0)
    theirs = (row >= 36) & (row < 36 + EXTRA)
    have_a = jnp.where(theirs, 9 + (row - 36) // PER_DATE, -9).astype(F32)
    take = choose(names, have_a, jnp.where(theirs, moved, -5.0), False)
    total = phase[...] + jnp.dot(take, pm[...].astype(BF16), preferred_element_type=F32)
    for g in range(out.shape[0]):
        out[g] = total.astype(BF16)


def series_kernel(table, got, weight, out, sums):
    stack = jnp.concatenate([got[g] for g in range(got.shape[0])], axis=0)
    series = jnp.dot(weight[...], stack, preferred_element_type=F32)
    wide = series.shape[1]
    rows = jnp.where(iota(series.shape, 0) == DATES - 1, 1.0, series).astype(BF16)
    none = jnp.zeros_like(rows)
    codes = got[0, 40:48, :].astype(F32)
    for g in range(1, got.shape[0]):
        codes = codes + got[g, 40:48, :].astype(F32)
    owner, cell = codes[6:7, :], codes[7:8, :]
    cell = cell - fact(table, 3).astype(F32) * 8.0
    select = []
    for base in (0.0, 4.0):
        mine = (cell >= base) & (cell < base + 4.0)
        target = jnp.where(mine, owner * 4.0 + cell - base, -1.0).astype(jnp.int32)
        select.append((iota((sums.shape[0], wide), 0) == target).astype(BF16))
    sums[...] = lax.dot_general(
        jnp.concatenate(select, axis=1),
        jnp.concatenate(
            [jnp.concatenate([rows, none], axis=0), jnp.concatenate([none, rows], axis=0)], axis=1
        ),
        (((1,), (1,)), ((), ())),
        preferred_element_type=F32,
    )

    def one(n, _):
        both = sums[pl.ds(pl.multiple_of(8 * n, 8), 8), :].astype(BF16)
        out[2 * n], out[2 * n + 1] = both[:4], both[4:]
        return 0

    lax.fori_loop(0, out.shape[0] // 2, one, 0, unroll=4)


def final_kernel(got, lines, out):
    total = got[0].astype(F32)
    for g in range(1, got.shape[0]):
        total = total + got[g].astype(F32)
    turned = pltpu.roll(total, DATES, 1)
    total = jnp.concatenate([total[:, 0:DATES], turned[:, 0:DATES]], axis=0)
    lane = iota(total.shape, 1)
    counts = jnp.sum(jnp.where(lane == DATES - 1, total, 0.0), axis=1, keepdims=True)
    velocity = jnp.sum(total * lines[19:20, :], axis=1, keepdims=True)
    total = jnp.where(lane == DATES - 1, velocity, total)
    out[...] = total / jnp.maximum(counts, 1.0)


SMEM = pl.BlockSpec(memory_space=pltpu.SMEM)
VMEM = pl.BlockSpec(memory_space=pltpu.VMEM)


def call(kernel, smem, vmem, outs, scratch=()):
    return pl.pallas_call(
        kernel,
        in_specs=[SMEM] * len(smem) + [VMEM] * len(vmem),
        out_specs=[VMEM] * len(outs),
        out_shape=[jax.ShapeDtypeStruct(s, t) for s, t in outs],
        scratch_shapes=list(scratch),
        compiler_params=pltpu.CompilerParams(vmem_limit_bytes=VMEM_BYTES),
    )(*smem, *vmem)


def swaps(count, start):
    return [p for i in range(start, count - 1, 2) for p in ((i, i + 1), (i + 1, i))]


def pair_names(pairs, rows):
    names = np.full((2, rows), -20.0, np.float32)
    for c, (a, b) in enumerate(pairs):
        names[0, 8 * c : 8 * c + 8] = a
        names[1, 8 * c : 8 * c + 8] = b
    return jnp.asarray(names)


def pair_table(pairs, rows):
    table = np.zeros((2, rows // 8), np.int32)
    table[:, : len(pairs)] = np.array(pairs, np.int32).T
    return jnp.asarray(table)


def local(slc_stack, offsets, kernels, partner, inverse, rate_weights, owners, map_cell):
    date_count, width = slc_stack.shape[1], slc_stack.shape[3]
    groups, strips = lax.axis_size("date"), lax.axis_size("col")
    group, strip = lax.axis_index("date"), lax.axis_index("col")
    rows = [
        jnp.transpose(kernels, (1, 2, 0)).reshape(2 * TAPS, DATES),
        offsets.T.astype(F32),
        jnp.pad(partner.reshape(1, -1).astype(F32), ((0, 0), (0, DATES - partner.shape[0]))),
    ]
    rows.append(jnp.pad(rate_weights.reshape(1, -1), ((0, 0), (0, DATES - rate_weights.shape[0]))))
    facts = jnp.stack([group * date_count, group % 2, strip % 2, group]).astype(F32)
    rows.append(jnp.broadcast_to(facts[:, None], (4, DATES)))
    facts = facts.reshape(1, -1)
    table, at = jnp.zeros((24, DATES), F32), 0
    for part in rows:
        table = table + jnp.pad(part, ((at, 24 - at - part.shape[0]), (0, 0)))
        at += part.shape[0]
    mine = lax.dynamic_slice(table, (0, group * date_count), (table.shape[0], date_count))

    tile = jax.ShapeDtypeStruct((2, ROWS, LANES), BF16)
    tile0, tile1 = pl.pallas_call(
        pack_kernel,
        in_specs=[SMEM, pl.BlockSpec(memory_space=pl.ANY)],
        out_specs=[VMEM] * 2,
        out_shape=[tile, jax.ShapeDtypeStruct((2, ROWS + 8, LANES), BF16)],
        scratch_shapes=[
            pltpu.VMEM((2,) + slc_stack.shape[:3] + (LANES,), BF16),
            pltpu.SemaphoreType.DMA((2,)),
        ],
        compiler_params=pltpu.CompilerParams(vmem_limit_bytes=53 * 1024 * 1024),
    )((strip % 2).astype(jnp.int32).reshape(1), slc_stack)
    own = lax.reduce_precision(slc_stack, 8, 7)
    near = lax.ppermute(tile0, "col", swaps(strips, 0))
    far = lax.ppermute(tile1, "col", swaps(strips, 1))
    (weight,) = call(
        weights_kernel,
        (),
        (inverse,),
        [((DATES, groups * PAIR_ROWS), BF16)],
        [pltpu.VMEM((inverse.shape[1], groups * PAIR_ROWS), BF16)],
    )
    scratch = [
        pltpu.VMEM((2, 2 * ROWS * width // LANES, 2 * LANES), BF16),
        pltpu.VMEM((2, 4 * LANES, 2 * LANES), BF16),
        pltpu.VMEM((2, 2, width // LANES, ROWS, LANES), F32),
    ]
    edge0, edge1 = call(
        edge_kernel,
        (mine,),
        (own, near, far, table),
        [((256, width), BF16)] * 2,
        scratch,
    )
    later = lax.ppermute(edge0, "date", [(i + 1, i) for i in range(groups - 1)])
    earlier = lax.ppermute(edge1, "date", [(i, i + 1) for i in range(groups - 1)])
    window = np.arange(width)[:, None] // LOOK_RG == np.arange(256)[None, :] % (width // LOOK_RG)
    matrix = jnp.asarray(window.astype(np.float32)).astype(BF16)
    inner_rows = 8 * (len(INNER) + 5)
    phase, power, ys = call(
        inner_kernel,
        (mine, pair_table(INNER, inner_rows)),
        (
            own, near, far, edge0, edge1, table, matrix, pair_names(INNER, inner_rows),
            owners.reshape(1, -1), map_cell,
        ),
        [
            ((PAIR_ROWS, 256), F32),
            ((96, 256), F32),
            ((12, 2, ROWS, width), F32),
        ],
        scratch
        + [
            pltpu.VMEM((8 * len(INNER) + 104, width), F32),
            pltpu.VMEM((8 * len(INNER) + 104, 256), F32),
        ],
    )
    def boundary(kernel, smem, vmem, pairs, table_pairs, out):
        rows = 8 * (-(-len(pairs) // 8) * 8)
        (result,) = call(
            kernel,
            smem + (pair_table(table_pairs, rows),),
            vmem + (pair_names(pairs, rows),),
            [out],
            [
                pltpu.VMEM((HALF, 2, ROWS, width), F32),
                pltpu.VMEM((rows + 8 * HALF, width), F32),
                pltpu.VMEM((rows, 256), F32),
                pltpu.VMEM((96 + 8 * HALF, 256), F32),
            ],
        )
        return result

    later, weight = lax.optimization_barrier((later, weight))
    phase = boundary(
        after_kernel,
        (facts,),
        (later, ys, power, phase, table, matrix),
        CROSS,
        CROSS,
        ((PAIR_ROWS, 256), F32),
    )
    sent = boundary(
        before_kernel,
        (),
        (earlier, ys, power, phase, matrix),
        BEFORE,
        [(a + 3, b - 12) for a, b in BEFORE],
        ((groups, PAIR_ROWS, 256), BF16),
    )
    phases = lax.all_to_all(sent, "date", 0, 0, tiled=True)
    (routed,) = call(
        series_kernel,
        (facts,),
        (phases, weight),
        [((strips, 4, 2 * DATES), BF16)],
        [pltpu.VMEM((4 * strips, 2 * DATES), F32)],
    )
    parts = lax.all_to_all(routed, "col", 0, 0, tiled=True)
    (mean,) = call(final_kernel, (), (parts, table), [((8, DATES), F32)])
    return mean.reshape(1, 8, DATES)


def solution(mesh):
    in_specs = (
        P(None, "date", None, "col"),
        P(),
        P(),
        P("date"),
        P(),
        P(),
        P("col", "date", None),
        P("col", "date"),
    )
    out_specs = P("col", "date", None)
    return jax.shard_map(local, mesh=mesh, in_specs=in_specs, out_specs=out_specs, check_vma=False)
```

```python
import functools

import jax
import jax.numpy as jnp
import numpy as np
from jax import lax
from jax.experimental import pallas as pl
from jax.experimental.pallas import tpu as pltpu
from jax.sharding import PartitionSpec as P

PER_DATE = 3
SPAN = 6
HALF = 3
ROW_BLOCK = 20
TAPS = 8
HALO = 8
LOOK_AZ = 5
LOOK_RG = 20
LROWS = 8
LANES = 128
ROWS = 40
DATES = 192
EXTRA = 9
FACTS = 20
PAIR_ROWS = 48
F32 = jnp.float32
BF16 = jnp.bfloat16
VMEM_BYTES = 24 * 1024 * 1024

INNER = [(a, a + s) for a in range(6) for s in range(1, 7)]
INNER += [(a, b) for a in range(6, 11) for b in range(a + 1, 12)]
CROSS = [(a, b) for b in range(12, 15) for a in range(b - 6, 12)]
BEFORE = [(a, b) for b in range(15, 18) for a in range(b - 6, 12)]


def iota(shape, dim):
    return lax.broadcasted_iota(jnp.int32, shape, dim)


def fact(table, n):
    return (table[0, n] if table.shape[0] == 1 else table[FACTS + n, 0]).astype(jnp.int32)


def partner_row(table, lines):
    return lines[18:19, 0:36] - fact(table, 0).astype(F32)


def tap_weights(table, at, weights):
    lane, row = iota((16, LANES), 1), iota((16, LANES), 0)
    for b in range(2):
        start = LANES + 4 - table[2 * TAPS + b, at].astype(jnp.int32)
        line = jnp.zeros((8, LANES), F32)
        for t in range(TAPS):
            here = iota((8, LANES), 1) == lax.rem(start - t, LANES)
            line = jnp.where(here, table[TAPS * b + t, at], line)
        cols = slice(LANES * b, LANES * b + LANES)
        for m in range(0, LANES, 16):
            both = jnp.concatenate(
                [pltpu.roll(line, m + 8 * i, 1, stride=1, stride_axis=0) for i in range(2)], axis=0
            )
            apart = lane - row - m
            near = (apart < 64) & (apart > -64)
            for at_row, tile in ((m, jnp.where(near, both, 0.0)), (LANES + m, jnp.where(near, 0.0, both))):
                high = tile.astype(BF16)
                weights[at_row : at_row + 16, cols] = high
                weights[256 + at_row : 272 + at_row, cols] = (tile - high.astype(F32)).astype(BF16)


def resample(own, near, far, table, dates, lhs, weights, zs):
    is_odd = fact(table, 2) == 1
    count = own.shape[-1] // LANES
    lane = iota((ROWS, LANES), 1)
    for s, date in enumerate(dates):
        tap_weights(table, date, weights.at[s])
    for s, date in enumerate(dates):
        for part in range(2):
            tile_a, tile_b = near[part].astype(F32), far[part, 0:ROWS].astype(F32)
            left = pltpu.roll(jnp.where(is_odd, tile_a, tile_b), LANES - HALO - HALO * date, 1)
            right = pltpu.roll(
                jnp.where(is_odd, tile_b, tile_a), lax.rem(LANES - HALO * date, LANES), 1
            )
            line = own[part, date].astype(F32)
            tiles = [left] + [line[:, LANES * j : LANES * (j + 1)] for j in range(count)] + [right]
            for j in range(count):
                rows = slice(ROWS * (count * part + j), ROWS * (count * part + j + 1))
                lhs[s, rows, 0:LANES] = own[part, date, :, LANES * j : LANES * (j + 1)]
                lhs[s, rows, LANES : 2 * LANES] = jnp.where(
                    lane < 64, tiles[j + 2], tiles[j]
                ).astype(BF16)
    row = iota((8, LANES), 0)
    outs = []
    for s in range(len(dates)):
        taken = lhs[s]
        outs.append(
            jnp.dot(
                jnp.concatenate([taken, taken], axis=1), weights[s], preferred_element_type=F32
            )
        )
    for s, out in enumerate(outs):
        for part in range(2):
            for j in range(count):
                tile = out[ROWS * (count * part + j) : ROWS * (count * part + j + 1)]
                first, second = tile[:, :LANES], tile[:, LANES:]
                zs[s, part, j, 0:16, :] = first[:16]
                zs[s, part, j, 16:24, :] = jnp.where(row < 4, first[16:24], second[16:24])
                zs[s, part, j, 24:40, :] = second[24:]


def slabs(zs, s):
    for part in range(2):
        for k in range(LOOK_AZ):
            for j in range(zs.shape[2]):
                tile = zs[s, part, j, pl.ds(k, LROWS, stride=LOOK_AZ), :].astype(BF16)
                yield part, k, slice(LANES * j, LANES * (j + 1)), tile


def column(row, rows, offset):
    wide = row.shape[1]
    at = iota((rows, wide), 1) == iota((rows, wide), 0) + offset
    return jnp.sum(jnp.where(at, row, 0.0), axis=1, keepdims=True)


def pack_kernel(odd, own, out0, out1, ends, sems):
    far = own.shape[3] - LANES
    even = odd[0] == 0
    copies = [
        pltpu.make_async_copy(own.at[:, :, :, at : at + LANES], ends.at[n], sems.at[n])
        for n, at in enumerate((0, far))
    ]
    for copy in copies:
        copy.start()
    lane = iota((ROWS, LANES), 1) // HALO
    for copy in copies:
        copy.wait()

    def one(d, totals):
        here = lane == d
        rolled = [
            pltpu.roll(ends[n, part, d].astype(F32), HALO * d + HALO * n, 1)
            for part in range(2)
            for n in range(2)
        ]
        return tuple(jnp.where(here, r, t) for r, t in zip(rolled, totals))

    zero = jnp.zeros((ROWS, LANES), F32)
    totals = lax.fori_loop(0, own.shape[1], one, (zero,) * 4, unroll=4)
    for part in range(2):
        head, tail = totals[2 * part], totals[2 * part + 1]
        out0[part] = jnp.where(even, tail, head).astype(BF16)
        out1[part, 0:ROWS] = jnp.where(even, head, tail).astype(BF16)
        out1[part, ROWS:] = jnp.zeros((8, LANES), BF16)


def edge_kernel(table, own, near, far, lines, head, tail, lhs, weights, zs):
    local = column(partner_row(table, lines), 16, 36 - EXTRA)
    for out in (head, tail):
        out[240:256, :] = jnp.broadcast_to(local, (16, out.shape[1])).astype(BF16)

    def one(i, _):
        dates = (i, i + 9)
        resample(own, near, far, table, dates, lhs, weights, zs)
        for s, out in enumerate((head, tail)):
            for part, k, cols, tile in slabs(zs, s):
                out[pl.ds(pl.multiple_of(i * 80 + part * 40 + k * 8, 8), 8), cols] = tile
        return 0

    lax.fori_loop(0, HALF, one, 0)


def window_sum(values, matrix):
    high = values.astype(BF16)
    low = (values - high.astype(F32)).astype(BF16)
    both = jnp.dot(
        jnp.concatenate([high, low], axis=0), matrix[...], preferred_element_type=F32
    )
    return both[: values.shape[0]] + both[values.shape[0] :]


def cross_sum(first, second):
    total = None
    for k in range(LOOK_AZ):
        re1, im1 = first(0, k), first(1, k)
        re2, im2 = second(0, k), second(1, k)
        term = im1 * re2 - re1 * im2
        total = term if total is None else total + term
    return total


def power_sum(date):
    total = None
    for k in range(LOOK_AZ):
        re, im = date(0, k), date(1, k)
        term = re * re + im * im
        total = term if total is None else total + term
    return total


def phase_of(cross, power_a, power_b, mask):
    scale = 1.0 / (LOOK_AZ * LOOK_RG)
    product = (power_a * scale) * (power_b * scale) + 1e-06
    return jnp.where(mask, (cross * scale) * lax.rsqrt(product), 0.0)


def choose(names, have_a, have_b, reverse):
    a, b = names[0:1, :], names[1:2, :]
    take = ((have_a == a) & (have_b == b)).astype(F32)
    if reverse:
        take = take - ((have_a == b) & (have_b == a)).astype(F32)
    return take.astype(BF16)


def phases_of(pairs, count, pm, powers):
    mask = iota((8, 256), 1) // 32 == iota((8, 256), 0)

    def one(n, _):
        done = []
        for u in range(8):
            c = 8 * n + u
            rows = pl.ds(pl.multiple_of(c * 8, 8), 8)
            row_a = pl.ds(pl.multiple_of(pairs[0, c] * 8, 8), 8)
            row_b = pl.ds(pl.multiple_of(pairs[1, c] * 8, 8), 8)
            done.append(phase_of(pm[rows, :], powers[row_a, :], powers[row_b, :], mask))
        pm[pl.ds(pl.multiple_of(n * 64, 64), 64), :] = jnp.concatenate(done, axis=0)
        return 0

    lax.fori_loop(0, count // 8, one, 0)


def unpack_dates(packed, dates, start):
    def one(n, _):
        both = packed[pl.ds(pl.multiple_of(n * 80, 16), 80), :].astype(F32)
        dates[n + start, 0], dates[n + start, 1] = both[:40], both[40:]
        return 0

    lax.fori_loop(0, HALF, one, 0)


def inner_kernel(
    table, pairs, own, near, far, edge0, edge1, lines, matrix, names, owners, cells,
    phase_out, power_out, ys,
    lhs, weights, zs, ss, pm,
):
    width = own.shape[-1]

    def one_date(n, _):
        dates = (n + 3, n + 6)
        resample(own, near, far, table, dates, lhs, weights, zs)
        for s, d in enumerate(dates):
            for part, k, cols, tile in slabs(zs, s):
                ys[d, part, 8 * k : 8 * k + 8, cols] = tile.astype(F32)
        return 0

    lax.fori_loop(0, HALF, one_date, 0)
    unpack_dates(edge0, ys, 0)
    unpack_dates(edge1, ys, 9)

    powers = 8 * len(INNER)

    def one_power(d, _):
        ss[pl.ds(pl.multiple_of(powers + d * 8, 8), 8), :] = power_sum(reader(d))
        return 0

    def reader(d):
        return lambda part, k: ys[d, part, 8 * k : 8 * k + 8, :]

    lax.fori_loop(0, 12, one_power, 0, unroll=2)

    def one_pair(c, _):
        at = pl.multiple_of(c * 8, 8)
        ss[pl.ds(at, 8), :] = cross_sum(reader(pairs[0, c]), reader(pairs[1, c]))
        return 0

    lax.fori_loop(0, len(INNER), one_pair, 0)
    ss[powers + 96 :, :] = jnp.zeros_like(ss[powers + 96 :, :])
    block = ss.shape[0] // 2

    def one_block(n, _):
        rows = pl.ds(pl.multiple_of(n * block, 8), block)
        pm[rows, :] = window_sum(ss[rows, :], matrix)
        return 0

    lax.fori_loop(0, 2, one_block, 0)
    power_out[...] = pm[powers : powers + 96, :]
    total = names.shape[1]
    phases_of(pairs, total // 8, pm, power_out)
    local = column(partner_row(table, lines), PAIR_ROWS, 0)
    row = iota((PAIR_ROWS, 1), 0)
    have_a = jnp.where(row < 36, row // PER_DATE, -9).astype(F32)
    take = choose(names, have_a, local, True)

    n = owners.shape[1]
    spread = (iota((n, 256), 1) == iota((n, 256), 0) + n * fact(table, 3)).astype(BF16)
    codes = jnp.concatenate([owners[...], cells[...]], axis=0).astype(F32).astype(BF16)
    placed = jnp.dot(codes, spread, preferred_element_type=F32)
    lines = iota((PAIR_ROWS, 256), 0)
    phases = jnp.dot(take, pm[:total, :].astype(BF16), preferred_element_type=F32)
    phases = jnp.where(lines == 46, placed[0:1, :], phases)
    phase_out[...] = jnp.where(lines == 47, placed[1:2, :], phases)


def weights_kernel(inverse, gather, weight_out):
    weight_out[0:191, :] = jnp.dot(
        inverse[...], gather[...], preferred_element_type=F32
    ).astype(BF16)
    weight_out[191:192, :] = jnp.zeros((1, weight_out.shape[1]), BF16)


def boundary_phases(pairs, count, later, got, ys, power, matrix, rs, ss, pm, pw):
    unpack_dates(got, rs, 0)

    def here(d):
        return lambda part, k: ys[d, part, 8 * k : 8 * k + 8, :]

    def there(d):
        return lambda part, k: rs[d - 12, part, 8 * k : 8 * k + 8, :]

    first, second = (here, there) if later else (there, here)

    def one_pair(c, _):
        at = pl.multiple_of(c * 8, 8)
        ss[pl.ds(at, 8), :] = cross_sum(first(pairs[0, c]), second(pairs[1, c]))
        return 0

    lax.fori_loop(0, count, one_pair, 0)
    rows = pm.shape[0]

    def one_power(n, _):
        ss[pl.ds(pl.multiple_of(rows + n * 8, 8), 8), :] = power_sum(there(n + 12))
        return 0

    lax.fori_loop(0, HALF, one_power, 0)
    ss[count * 8 : rows, :] = jnp.zeros_like(ss[count * 8 : rows, :])
    pw[0:96, :] = power[...]
    sums = window_sum(ss[...], matrix)
    pm[...] = sums[:rows]
    pw[96:120, :] = sums[rows:]
    phases_of(pairs, rows // 8, pm, pw)


def after_kernel(
    facts, pairs, got, ys, power, phase, lines, matrix, names, out, rs, ss, pm, pw
):
    boundary_phases(pairs, len(CROSS), True, got, ys, power, matrix, rs, ss, pm, pw)
    local = column(partner_row(facts, lines), PAIR_ROWS, 0)
    row = iota((PAIR_ROWS, 1), 0)
    have_a = jnp.where(row < 36, row // PER_DATE, -9).astype(F32)
    take = choose(names, have_a, local, False)
    out[...] = phase[...] + jnp.dot(take, pm[...].astype(BF16), preferred_element_type=F32)


def before_kernel(pairs, got, ys, power, phase, matrix, names, out, rs, ss, pm, pw):
    boundary_phases(pairs, len(BEFORE), False, got, ys, power, matrix, rs, ss, pm, pw)
    told = jnp.max(got[240:256, 0:LANES].astype(F32), axis=1, keepdims=True)
    spread = (iota((PAIR_ROWS, 16), 0) - 36 == iota((PAIR_ROWS, 16), 1)).astype(BF16)
    moved = jnp.dot(
        spread, jnp.broadcast_to(told, (16, LANES)).astype(BF16), preferred_element_type=F32
    )[:, 0:1]
    row = iota((PAIR_ROWS, 1), 0)
    theirs = (row >= 36) & (row < 36 + EXTRA)
    have_a = jnp.where(theirs, 9 + (row - 36) // PER_DATE, -9).astype(F32)
    take = choose(names, have_a, jnp.where(theirs, moved, -5.0), False)
    total = phase[...] + jnp.dot(take, pm[...].astype(BF16), preferred_element_type=F32)
    for g in range(out.shape[0]):
        out[g] = total.astype(BF16)


def series_kernel(table, got, weight, out, sums):
    stack = jnp.concatenate([got[g] for g in range(got.shape[0])], axis=0)
    series = jnp.dot(weight[...], stack, preferred_element_type=F32)
    wide = series.shape[1]
    rows = jnp.where(iota(series.shape, 0) == DATES - 1, 1.0, series).astype(BF16)
    none = jnp.zeros_like(rows)
    codes = got[0, 40:48, :].astype(F32)
    for g in range(1, got.shape[0]):
        codes = codes + got[g, 40:48, :].astype(F32)
    owner, cell = codes[6:7, :], codes[7:8, :]
    cell = cell - fact(table, 3).astype(F32) * 8.0
    select = []
    for base in (0.0, 4.0):
        mine = (cell >= base) & (cell < base + 4.0)
        target = jnp.where(mine, owner * 4.0 + cell - base, -1.0).astype(jnp.int32)
        select.append((iota((sums.shape[0], wide), 0) == target).astype(BF16))
    sums[...] = lax.dot_general(
        jnp.concatenate(select, axis=1),
        jnp.concatenate(
            [jnp.concatenate([rows, none], axis=0), jnp.concatenate([none, rows], axis=0)], axis=1
        ),
        (((1,), (1,)), ((), ())),
        preferred_element_type=F32,
    )

    def one(n, _):
        both = sums[pl.ds(pl.multiple_of(8 * n, 8), 8), :].astype(BF16)
        out[2 * n], out[2 * n + 1] = both[:4], both[4:]
        return 0

    lax.fori_loop(0, out.shape[0] // 2, one, 0, unroll=4)


def final_kernel(got, lines, out):
    total = got[0].astype(F32)
    for g in range(1, got.shape[0]):
        total = total + got[g].astype(F32)
    turned = pltpu.roll(total, DATES, 1)
    total = jnp.concatenate([total[:, 0:DATES], turned[:, 0:DATES]], axis=0)
    lane = iota(total.shape, 1)
    counts = jnp.sum(jnp.where(lane == DATES - 1, total, 0.0), axis=1, keepdims=True)
    velocity = jnp.sum(total * lines[19:20, :], axis=1, keepdims=True)
    total = jnp.where(lane == DATES - 1, velocity, total)
    out[...] = total / jnp.maximum(counts, 1.0)


SMEM = pl.BlockSpec(memory_space=pltpu.SMEM)
VMEM = pl.BlockSpec(memory_space=pltpu.VMEM)


def call(kernel, smem, vmem, outs, scratch=()):
    return pl.pallas_call(
        kernel,
        in_specs=[SMEM] * len(smem) + [VMEM] * len(vmem),
        out_specs=[VMEM] * len(outs),
        out_shape=[jax.ShapeDtypeStruct(s, t) for s, t in outs],
        scratch_shapes=list(scratch),
        compiler_params=pltpu.CompilerParams(vmem_limit_bytes=VMEM_BYTES),
    )(*smem, *vmem)


def swaps(count, start):
    return [p for i in range(start, count - 1, 2) for p in ((i, i + 1), (i + 1, i))]


def pair_names(pairs, rows):
    names = np.full((2, rows), -20.0, np.float32)
    for c, (a, b) in enumerate(pairs):
        names[0, 8 * c : 8 * c + 8] = a
        names[1, 8 * c : 8 * c + 8] = b
    return jnp.asarray(names)


def pair_table(pairs, rows):
    table = np.zeros((2, rows // 8), np.int32)
    table[:, : len(pairs)] = np.array(pairs, np.int32).T
    return jnp.asarray(table)


def local(slc_stack, offsets, kernels, partner, inverse, rate_weights, owners, map_cell):
    date_count, width = slc_stack.shape[1], slc_stack.shape[3]
    groups, strips = lax.axis_size("date"), lax.axis_size("col")
    group, strip = lax.axis_index("date"), lax.axis_index("col")
    rows = [
        jnp.transpose(kernels, (1, 2, 0)).reshape(2 * TAPS, DATES),
        offsets.T.astype(F32),
        jnp.pad(partner.reshape(1, -1).astype(F32), ((0, 0), (0, DATES - partner.shape[0]))),
    ]
    rows.append(jnp.pad(rate_weights.reshape(1, -1), ((0, 0), (0, DATES - rate_weights.shape[0]))))
    facts = jnp.stack([group * date_count, group % 2, strip % 2, group]).astype(F32)
    rows.append(jnp.broadcast_to(facts[:, None], (4, DATES)))
    facts = facts.reshape(1, -1)
    table, at = jnp.zeros((24, DATES), F32), 0
    for part in rows:
        table = table + jnp.pad(part, ((at, 24 - at - part.shape[0]), (0, 0)))
        at += part.shape[0]
    mine = lax.dynamic_slice(table, (0, group * date_count), (table.shape[0], date_count))

    tile = jax.ShapeDtypeStruct((2, ROWS, LANES), BF16)
    tile0, tile1 = pl.pallas_call(
        pack_kernel,
        in_specs=[SMEM, pl.BlockSpec(memory_space=pl.ANY)],
        out_specs=[VMEM] * 2,
        out_shape=[tile, jax.ShapeDtypeStruct((2, ROWS + 8, LANES), BF16)],
        scratch_shapes=[
            pltpu.VMEM((2,) + slc_stack.shape[:3] + (LANES,), BF16),
            pltpu.SemaphoreType.DMA((2,)),
        ],
        compiler_params=pltpu.CompilerParams(vmem_limit_bytes=53 * 1024 * 1024),
    )((strip % 2).astype(jnp.int32).reshape(1), slc_stack)
    own = lax.reduce_precision(slc_stack, 8, 7)
    near = lax.ppermute(tile0, "col", swaps(strips, 0))
    far = lax.ppermute(tile1, "col", swaps(strips, 1))
    spots = np.arange(groups * PAIR_ROWS)
    of, k = spots // PAIR_ROWS, spots % PAIR_ROWS
    target = np.where(k < 36, 36 * of + k, np.where(k < 36 + EXTRA, 36 * of + k - 45, -1))
    gather = np.arange(inverse.shape[1])[:, None] == target[None, :]
    (weight,) = call(
        weights_kernel,
        (),
        (inverse, jnp.asarray(gather.astype(np.float32)).astype(BF16)),
        [((DATES, groups * PAIR_ROWS), BF16)],
    )
    scratch = [
        pltpu.VMEM((2, 2 * ROWS * width // LANES, 2 * LANES), BF16),
        pltpu.VMEM((2, 4 * LANES, 2 * LANES), BF16),
        pltpu.VMEM((2, 2, width // LANES, ROWS, LANES), F32),
    ]
    edge0, edge1 = call(
        edge_kernel,
        (mine,),
        (own, near, far, table),
        [((256, width), BF16)] * 2,
        scratch,
    )
    later = lax.ppermute(edge0, "date", [(i + 1, i) for i in range(groups - 1)])
    earlier = lax.ppermute(edge1, "date", [(i, i + 1) for i in range(groups - 1)])
    window = np.arange(width)[:, None] // LOOK_RG == np.arange(256)[None, :] % (width // LOOK_RG)
    matrix = jnp.asarray(window.astype(np.float32)).astype(BF16)
    inner_rows = 8 * (len(INNER) + 5)
    phase, power, ys = call(
        inner_kernel,
        (mine, pair_table(INNER, inner_rows)),
        (
            own, near, far, edge0, edge1, table, matrix, pair_names(INNER, inner_rows),
            owners.reshape(1, -1), map_cell,
        ),
        [
            ((PAIR_ROWS, 256), F32),
            ((96, 256), F32),
            ((12, 2, ROWS, width), F32),
        ],
        scratch
        + [
            pltpu.VMEM((8 * len(INNER) + 104, width), F32),
            pltpu.VMEM((8 * len(INNER) + 104, 256), F32),
        ],
    )
    def boundary(kernel, smem, vmem, pairs, table_pairs, out):
        rows = 8 * (-(-len(pairs) // 8) * 8)
        (result,) = call(
            kernel,
            smem + (pair_table(table_pairs, rows),),
            vmem + (pair_names(pairs, rows),),
            [out],
            [
                pltpu.VMEM((HALF, 2, ROWS, width), F32),
                pltpu.VMEM((rows + 8 * HALF, width), F32),
                pltpu.VMEM((rows, 256), F32),
                pltpu.VMEM((96 + 8 * HALF, 256), F32),
            ],
        )
        return result

    later, weight = lax.optimization_barrier((later, weight))
    phase = boundary(
        after_kernel,
        (facts,),
        (later, ys, power, phase, table, matrix),
        CROSS,
        CROSS,
        ((PAIR_ROWS, 256), F32),
    )
    sent = boundary(
        before_kernel,
        (),
        (earlier, ys, power, phase, matrix),
        BEFORE,
        [(a + 3, b - 12) for a, b in BEFORE],
        ((groups, PAIR_ROWS, 256), BF16),
    )
    phases = lax.all_to_all(sent, "date", 0, 0, tiled=True)
    (routed,) = call(
        series_kernel,
        (facts,),
        (phases, weight),
        [((strips, 4, 2 * DATES), BF16)],
        [pltpu.VMEM((4 * strips, 2 * DATES), F32)],
    )
    parts = lax.all_to_all(routed, "col", 0, 0, tiled=True)
    (mean,) = call(final_kernel, (), (parts, table), [((8, DATES), F32)])
    return mean.reshape(1, 8, DATES)


def solution(mesh):
    in_specs = (
        P(None, "date", None, "col"),
        P(),
        P(),
        P("date"),
        P(),
        P(),
        P("col", "date", None),
        P("col", "date"),
    )
    out_specs = P("col", "date", None)
    return jax.shard_map(local, mesh=mesh, in_specs=in_specs, out_specs=out_specs, check_vma=False)
```
